32 devices in a mesh: dp: 16 (over z, x, core), tp: 2 (over y).
Axes of the slice: x: 2, y: 2, z: 4, core: 2. Of those that a mesh axis runs over, the one named last changes fastest.
Arguments:
- inputs: bfloat16 [32768, 640], P('dp'), may hold values from -6 to 6
- out_grad: bfloat16 [32768, 640], P('dp'), may hold values from -6 to 6
- segment_ids: int32 [32, 1024], P('dp'), may hold values from 0 to 5, never falling along the last dimension, each value on 1 to 400 neighbouring positions
- attn_weights: float32 [4, 640, 640], P(None, 'dp', 'tp'), may hold values from -6 to 6
- ffn_weights: float32 [2, 640, 2560], P(None, 'dp', 'tp'), may hold values from -4 to 4
- head_bias: float32 [3, 640], P(None, 'tp'), may hold values from -1 to 1
- hidden_bias: float32 [2560], P('tp'), may hold values from -1 to 1
- norm_vectors: float32 [6, 640], replicated, may hold values from -1 to 2
- attn_first: float32 [4, 640, 640], P(None, 'dp', 'tp')
- ffn_first: float32 [2, 640, 2560], P(None, 'dp', 'tp')
- head_first: float32 [3, 640], P(None, 'tp')
- hidden_first: float32 [2560], P('tp')
- vector_first: float32 [6, 640], replicated
- attn_second: float32 [4, 640, 640], P(None, 'dp', 'tp')
- ffn_second: float32 [2, 640, 2560], P(None, 'dp', 'tp')
- head_second: float32 [3, 640], P(None, 'tp')
- hidden_second: float32 [2560], P('tp')
- vector_second: float32 [6, 640], replicated
Outputs:
- layer_output: bfloat16 [32768, 640], P('dp')
- input_grad: bfloat16 [32768, 640], P('dp')
- new_attn_weights: float32 [4, 640, 640], P(None, 'dp', 'tp')
- new_ffn_weights: float32 [2, 640, 2560], P(None, 'dp', 'tp')
- new_head_bias: float32 [3, 640], P(None, 'tp')
- new_hidden_bias: float32 [2560], P('tp')
- new_norm_vectors: float32 [6, 640], replicated
- attn_first_new: float32 [4, 640, 640], P(None, 'dp', 'tp')
- ffn_first_new: float32 [2, 640, 2560], P(None, 'dp', 'tp')
- head_first_new: float32 [3, 640], P(None, 'tp')
- hidden_first_new: float32 [2560], P('tp')
- vector_first_new: float32 [6, 640], replicated
- attn_second_new: float32 [3, 640, 640], P(None, 'dp', 'tp')
- out_second_new: float32 [640, 640], P('dp', 'tp')
- ffn_second_new: float32 [2, 640, 2560], P(None, 'dp', 'tp')
- head_second_new: float32 [3, 640], P(None, 'tp')
- hidden_second_new: float32 [2560], P('tp')
- vector_second_new: float32 [4, 640], replicated
- norm_second_new: float32 [2, 640], replicated
- trust_norms: float32 [2, 16], replicated
The draws below stay inside these ranges and needn't reach their ends.
Inputs may be any that keep to these rules, and one draw needn't show every extreme that they name: `segment_ids`: within each row of 1024 slots the ids never fall; each of the 6 ids forms one run of 1 to 400 slots, and one run has exactly 400 slots.
All inputs are finite; a program needn't handle non-finite values.
Results may differ from the reference program's by a relative error of at most 0.019.
Values may be sent and summed in bfloat16 or wider, within the bound.
No kernel may reach another device: no remote copies, remote signals or barrier semaphores. Data moves between devices by JAX's collectives and lax.ppermute only.
A program may use at most 192 MiB of HBM per device.

```python
import math
from functools import partial
from functools import reduce
import jax
import jax.numpy as jnp
import numpy as np
from jax import lax

D = 640
HEADS = 20
HD = 32
FF = 2560
SLOTS = 1024
SEGS = 6
MOST = 400
STEP = 10
ROWS = 32
TOKENS = 32768
N_TP = 2


def scaled_normal(key, extent, scales, clip_at):
    values = jnp.clip(jax.random.normal(key, extent, jnp.float32), -clip_at, clip_at)
    return values * scales


def row_factor(lowest, highest):
    ramp = jnp.arange(D, dtype=jnp.float32) / (D - 1)
    return jnp.exp(math.log(lowest) + ramp * (math.log(highest) - math.log(lowest)))[None, :, None]


def weight_factor():
    return row_factor(0.6, 1.7)


def moment_factor():
    return row_factor(0.5, 2.0)


def first_moment(key, extent, scales):
    return scaled_normal(key, extent, scales * 0.11 * jnp.sqrt(jnp.float32(TOKENS)), 4.0)


def second_moment(key, extent, scales):
    spread = jnp.exp(jax.random.uniform(key, extent, jnp.float32, math.log(0.5), math.log(8.0)))
    magnitude = scales * jnp.sqrt(jnp.float32(TOKENS))
    return spread * 0.001 * magnitude * magnitude


def attn_scales():
    return jnp.array([1.9, 1.9, 1.9, 0.15], jnp.float32)[:, None, None]


def ffn_scales():
    return jnp.array([0.35, 0.65], jnp.float32)[:, None, None]


def vector_scales():
    return jnp.array([3.3, 3.3, 1.1, 0.7, 0.7, 1.0], jnp.float32)[:, None]


def draw_attn_weights(key, part):
    scales = jnp.array([D ** (-0.5), D ** (-0.5), D ** (-0.5), (D // 64) ** (-0.5)], jnp.float32)[:, None, None]
    return jnp.clip(scaled_normal(key, (4, D, D), scales * weight_factor(), 4.0), -6.0, 6.0)


def draw_ffn_weights(key, part):
    scales = jnp.array([D ** (-0.5), FF ** (-0.5)], jnp.float32)[:, None, None]
    return scaled_normal(key, (2, D, FF), scales * weight_factor(), 4.0)


def draw_norm_vectors(key, part):
    gains = jax.random.uniform(jax.random.fold_in(key, 1), (6, D), jnp.float32, 0.7, 1.3)
    shifts = scaled_normal(jax.random.fold_in(key, 2), (6, D), 0.2, 4.0)
    is_gain = jnp.array([1, 0, 0, 1, 0, 0], jnp.int32)[:, None] == 1
    return jnp.where(is_gain, gains, shifts)


def draw_attn_first(key, part):
    return first_moment(key, (4, D, D), attn_scales() * moment_factor())


def draw_ffn_first(key, part):
    return first_moment(key, (2, D, FF), ffn_scales() * moment_factor())


def draw_head_first(key, part):
    return first_moment(key, (3, D), 1.9)


def draw_hidden_first(key, part):
    return first_moment(key, (FF,), 0.35)


def draw_vector_first(key, part):
    return first_moment(key, (6, D), vector_scales())


def draw_attn_second(key, part):
    return second_moment(key, (4, D, D), attn_scales() / moment_factor())


def draw_ffn_second(key, part):
    return second_moment(key, (2, D, FF), ffn_scales() / moment_factor())


def draw_head_second(key, part):
    return second_moment(key, (3, D), 1.9)


def draw_hidden_second(key, part):
    return second_moment(key, (FF,), 0.35)


def draw_vector_second(key, part):
    return second_moment(key, (6, D), vector_scales())


def block_scale(own_key, dims, cuts, low, high):
    level, own = 1.0, jax.random.fold_in(own_key, 6)
    for axis_at, shards_of in cuts:
        heights = jnp.exp(jax.random.uniform(jax.random.fold_in(own, axis_at), (shards_of,), jnp.float32, low / len(cuts), high / len(cuts)))
        level = level * jnp.repeat(heights, dims[axis_at] // shards_of).reshape([-1 if axis == axis_at else 1 for axis in range(len(dims))])
    return level


def split_up(count, total, limit, slope):
    weights = [(1 << 20) // math.isqrt(standing ** slope) + 1 for standing in range(2, count + 1)]
    surplus, given = total - limit - (count - 1), [1] * (count - 1)
    while surplus > 0:
        free = [i for i in range(count - 1) if given[i] < limit]
        pool, remaining = sum([weights[i] for i in free]), surplus
        for i in free:
            addition = min(limit - given[i], max(1, remaining * weights[i] // pool), surplus)
            given[i] = given[i] + addition
            surplus = surplus - addition
    return np.array([limit] + given)


def uneven_parts(own_key, number_of, total, limit, skew):
    if number_of == 2:
        one = jax.random.randint(own_key, (), max(1, total - limit), min(limit, total - 1) + 1)
        return jnp.stack([one, total - one])
    sizes = jnp.asarray(split_up(number_of, total, limit, skew), jnp.int32)
    couples = (number_of - 1) // 2
    source_of, sink = sizes[1:1 + 2 * couples:2], sizes[2:2 + 2 * couples:2]
    room = jnp.minimum(source_of - 1, limit - sink)
    passed = jax.random.randint(jax.random.fold_in(own_key, 1), (couples,), 0, 1 << 20) % (room + 1)
    sizes = sizes.at[1:1 + 2 * couples:2].set(source_of - passed).at[2:2 + 2 * couples:2].set(sink + passed)
    return sizes[jax.random.permutation(jax.random.fold_in(own_key, 2), number_of)]


def centred(rng, shape, scale, reach, cuts=(), kind=jnp.bfloat16):
    level = block_scale(rng, shape, cuts, -0.22, 0.18) if cuts else 1.0
    drawn = jax.random.normal(rng, shape, jnp.float32) * scale * level
    return jnp.minimum(jnp.maximum(drawn, -reach), reach).astype(kind)


def setup_inputs(seed: int = 0) -> dict:
    seeds = jax.random.split(jax.random.key(seed), 19)
    inputs = centred(seeds[0], (TOKENS, D), 1.0, 6.0, ((0, 16),))
    out_grad = centred(seeds[1], (TOKENS, D), 1.0, 6.0, ((0, 16),))
    segment_ids = jax.vmap(lambda own: jnp.searchsorted(jnp.cumsum(uneven_parts(own, SEGS, SLOTS, MOST, 0)), jnp.arange(SLOTS), side="right"))(jax.random.split(seeds[2], ROWS)).reshape((ROWS, SLOTS)).astype(jnp.int32)
    attn_weights = draw_attn_weights(jax.random.fold_in(seeds[18], 71), 0)
    ffn_weights = draw_ffn_weights(jax.random.fold_in(seeds[18], 71), 0)
    head_bias = centred(seeds[5], (3, D), 0.2, 1.0, ((1, 2),), jnp.float32)
    hidden_bias = centred(seeds[6], (FF,), 0.2, 1.0, ((0, 2),), jnp.float32)
    norm_vectors = draw_norm_vectors(jax.random.fold_in(seeds[18], 71), 0)
    attn_first = draw_attn_first(jax.random.fold_in(seeds[18], 71), 0)
    ffn_first = draw_ffn_first(jax.random.fold_in(seeds[18], 71), 0)
    head_first = draw_head_first(jax.random.fold_in(seeds[18], 71), 0)
    hidden_first = draw_hidden_first(jax.random.fold_in(seeds[18], 71), 0)
    vector_first = draw_vector_first(jax.random.fold_in(seeds[18], 71), 0)
    attn_second = draw_attn_second(jax.random.fold_in(seeds[18], 71), 0)
    ffn_second = draw_ffn_second(jax.random.fold_in(seeds[18], 71), 0)
    head_second = draw_head_second(jax.random.fold_in(seeds[18], 71), 0)
    hidden_second = draw_hidden_second(jax.random.fold_in(seeds[18], 71), 0)
    vector_second = draw_vector_second(jax.random.fold_in(seeds[18], 71), 0)
    return {"inputs": inputs, "out_grad": out_grad, "segment_ids": segment_ids, "attn_weights": attn_weights, "ffn_weights": ffn_weights, "head_bias": head_bias, "hidden_bias": hidden_bias, "norm_vectors": norm_vectors, "attn_first": attn_first, "ffn_first": ffn_first, "head_first": head_first, "hidden_first": hidden_first, "vector_first": vector_first, "attn_second": attn_second, "ffn_second": ffn_second, "head_second": head_second, "hidden_second": hidden_second, "vector_second": vector_second}


EPS_NORM = 1e-05
EPS_ADAM = 1e-06
BETA_ONE = 0.9
BETA_TWO = 0.999
DECAY = 0.01
RATE = 0.5
MASKED = -1e+30

@jax.custom_vjp
def low(v):
    return lax.optimization_barrier(v.astype(jnp.bfloat16)).astype(jnp.float32)

@jax.custom_vjp
def low_back(v):
    return v

def low_keep(v):
    return (low(v), None)

def low_pass(kept, grad):
    return (grad,)

def back_keep(v):
    return (v, None)

def back_low(kept, grad):
    return (low(grad),)
low.defvjp(low_keep, low_pass)
low_back.defvjp(back_keep, back_low)

def matmul(left, right):
    return jnp.dot(left, right, precision=lax.Precision.HIGHEST, preferred_element_type=jnp.float32)

def layer_norm(values, scale_gain, offset):
    average = lax.optimization_barrier(jnp.mean(values, axis=-1, keepdims=True))
    centered = values - average
    variance = lax.optimization_barrier(jnp.mean(centered * centered, axis=-1, keepdims=True))
    return centered * lax.rsqrt(variance + EPS_NORM) * scale_gain + offset

def rope_tables(segments):
    slots_index = jnp.arange(segments.shape[0], dtype=jnp.int32)
    before = lax.optimization_barrier(jnp.sum((segments[None, :] < segments[:, None]).astype(jnp.int32), axis=1))
    position = (slots_index - before).astype(jnp.float32)
    frequency = 10000.0 ** (-jnp.arange(0, HD, 2).astype(jnp.float32) / HD)
    angles = position[:, None] * frequency[None, :]
    angles = jnp.concatenate([angles, angles], axis=-1)
    return (jnp.cos(angles), jnp.sin(angles))

def rotate(values, cosine_table, sine_table):
    middle = values.shape[-1] // 2
    turned = jnp.concatenate([-values[..., middle:], values[..., :middle]], axis=-1)
    return values * cosine_table + turned * sine_table

def attend_row(queries, keys_row, values_row, segments):
    scores = jnp.einsum('qhd,khd->hqk', queries, keys_row, precision=lax.Precision.HIGHEST) * HD ** (-0.5)
    scores = low_back(scores)
    same_protein = segments[:, None] == segments[None, :]
    scores = jnp.where(same_protein[None], scores, MASKED)
    highest = lax.optimization_barrier(jnp.max(scores, axis=-1, keepdims=True))
    weights_exp = jnp.exp(scores - highest)
    attention = low(weights_exp / lax.optimization_barrier(jnp.sum(weights_exp, axis=-1, keepdims=True)))
    return jnp.einsum('hqk,khd->qhd', attention, values_row, precision=lax.Precision.HIGHEST)

def forward(segments, cosine_table, sine_table, inputs, attn_weights, ffn_weights, head_bias, hidden_bias, norm_vectors):
    attn_low = low(attn_weights)
    ffn_low = low(ffn_weights)
    head_width = D // N_TP
    hidden_width = FF // N_TP
    local_heads = HEADS // N_TP
    normed = low(layer_norm(inputs, norm_vectors[0], norm_vectors[1]))
    pieces = []
    for member in range(N_TP):
        columns = slice(member * head_width, (member + 1) * head_width)
        copied = low_back(normed)
        project_q = matmul(copied, attn_low[0][:, columns]) + head_bias[0, columns]
        project_k = matmul(copied, attn_low[1][:, columns]) + head_bias[1, columns]
        project_v = matmul(copied, attn_low[2][:, columns]) + head_bias[2, columns]
        queries = low_back(project_q).reshape(ROWS, SLOTS, local_heads, HD)
        keys_all = low_back(project_k).reshape(ROWS, SLOTS, local_heads, HD)
        values_all = low(low_back(project_v)).reshape(ROWS, SLOTS, local_heads, HD)
        queries = low(rotate(queries, cosine_table, sine_table))
        keys_all = low(rotate(keys_all, cosine_table, sine_table))
        attended = lax.map(lambda packed: jax.checkpoint(attend_row)(packed[0], packed[1], packed[2], packed[3]), (queries, keys_all, values_all, segments))
        heads_out = low(low_back(attended.reshape(TOKENS, head_width)))
        pieces.append(low(matmul(heads_out, attn_low[3][:, columns].T)))
    attended_sum = low_back(reduce(jnp.add, pieces))
    residual = inputs + attended_sum + norm_vectors[2]
    normed_two = low(layer_norm(residual, norm_vectors[3], norm_vectors[4]))
    outputs = []
    for member in range(N_TP):
        columns = slice(member * hidden_width, (member + 1) * hidden_width)
        copied = low_back(normed_two)
        preact = low_back(matmul(copied, ffn_low[0][:, columns]) + hidden_bias[columns])
        activated = low(jax.nn.gelu(preact, approximate=False))
        outputs.append(low(matmul(activated, ffn_low[1][:, columns].T)))
    mixed_sum = low_back(reduce(jnp.add, outputs))
    return residual + mixed_sum + norm_vectors[5]

def lamb_moments(weight, gradient, moment_one, moment_two):
    first_new = BETA_ONE * moment_one + (1.0 - BETA_ONE) * gradient
    second_new = BETA_TWO * moment_two + (1.0 - BETA_TWO) * gradient * gradient
    corrected = first_new / (1.0 - BETA_ONE ** STEP)
    variance = second_new / (1.0 - BETA_TWO ** STEP)
    update = corrected / (jnp.sqrt(variance) + EPS_ADAM) + DECAY * weight
    return (first_new, second_new, update)

def group_norms(array):
    return jnp.sqrt(lax.optimization_barrier(jnp.sum(array * array, axis=tuple(range(1, array.ndim)))))

def reference(inputs, out_grad, segment_ids, attn_weights, ffn_weights, head_bias, hidden_bias, norm_vectors, attn_first, ffn_first, head_first, hidden_first, vector_first, attn_second, ffn_second, head_second, hidden_second, vector_second):
    tables = jax.vmap(rope_tables)(segment_ids)
    cosine_table = tables[0][:, :, None, :]
    sine_table = tables[1][:, :, None, :]
    result, pullback = jax.vjp(partial(forward, segment_ids, cosine_table, sine_table), inputs.astype(jnp.float32), attn_weights, ffn_weights, head_bias, hidden_bias, norm_vectors)
    gradients = pullback(out_grad.astype(jnp.float32))
    masters = [attn_weights, ffn_weights, head_bias, hidden_bias.reshape(1, -1), norm_vectors]
    grads_list = [gradients[1], gradients[2], gradients[3], gradients[4].reshape(1, -1), gradients[5]]
    firsts = [attn_first, ffn_first, head_first, hidden_first.reshape(1, -1), vector_first]
    seconds = [attn_second, ffn_second, head_second, hidden_second.reshape(1, -1), vector_second]
    results = [lamb_moments(masters[member], grads_list[member], firsts[member], seconds[member]) for member in range(5)]
    weight_norms = jnp.concatenate([group_norms(masters[member]) for member in range(5)])
    update_norms = jnp.concatenate([group_norms(results[member][2]) for member in range(5)])
    trust_ratio = weight_norms / update_norms
    counts = [4, 2, 3, 1, 6]
    new_weights = []
    begin_at = 0
    for member in range(5):
        piece_ratio = trust_ratio[begin_at:begin_at + counts[member]]
        shaped_ratio = piece_ratio.reshape((-1,) + (1,) * (masters[member].ndim - 1))
        new_weights.append(masters[member] - RATE * shaped_ratio * results[member][2])
        begin_at += counts[member]
    return (result.astype(jnp.bfloat16), gradients[0].astype(jnp.bfloat16), new_weights[0], new_weights[1], new_weights[2], new_weights[3].reshape(-1), new_weights[4], results[0][0], results[1][0], results[2][0], results[3][0].reshape(-1), results[4][0], results[0][1][:3], results[0][1][3], results[1][1], results[2][1], results[3][1].reshape(-1), results[4][1][2:], results[4][1][:2], jnp.stack([weight_norms, update_norms]))
```

```python
import math

import jax
import jax.numpy as jnp
from jax import lax
from jax.experimental import pallas as pl
from jax.experimental.pallas import tpu as pltpu
from jax.sharding import PartitionSpec as P

STEP = 10
EPS_NORM = 1e-05
EPS_ADAM = 1e-06
BETA_ONE = 0.9
BETA_TWO = 0.999
DECAY = 0.01
RATE = 0.5
HD=32
BIG=1e30
QT=128
KC=256
QSCALE=math.log2(math.e)/math.sqrt(HD)
LN2=math.log(2.0)
VM=56*1024*1024
bf=jnp.bfloat16
f32=jnp.float32

def dg(a,b,ca,cb):
    return lax.dot_general(a,b,(((ca,),(cb,)),((),())),preferred_element_type=f32)

def rope_rows(y,cos,sin,heads,sign):
    out=[]
    for h in range(heads):
        top=y[HD*h:HD*h+HD//2]; bot=y[HD*h+HD//2:HD*h+HD]
        out.append(top*cos-sign*bot*sin); out.append(bot*cos+sign*top*sin)
    return jnp.concatenate(out,axis=0)

def fwd_body(rng_ref,n1_ref,w_ref,b_ref,cos_ref,sin_ref,fq_ref,fk_ref,
             qt_ref,kt_ref,kp_ref,vn_ref,ot_ref,lse_ref,vt_ref,qbd_ref):
    width=w_ref.shape[2]; heads=width//HD; groups=heads//2; T=n1_ref.shape[0]; pad=kt_ref.shape[1]-T
    cos=cos_ref[...]; sin=sin_ref[...]
    n1=n1_ref[...]
    for c in range(3):
        y=dg(w_ref[c],n1,0,1)+b_ref[:,c:c+1]
        if c<2: y=rope_rows(y,cos,sin,heads,1.0)
        if c==0: qt_ref[...]=(y*QSCALE).astype(bf)
        elif c==1:
            yb=y.astype(bf)
            kt_ref[:,:T]=yb
            kt_ref[:,T:]=jnp.zeros((width,pad),bf)
            fk=fk_ref[...].astype(f32)
            for g in range(groups):
                piece=jnp.concatenate([y[64*g:64*g+64],fk[:,:T]],axis=0)
                kp_ref[g,:T,:]=jnp.transpose(piece).astype(bf)
                kp_ref[g,T:,:]=jnp.transpose(jnp.concatenate([jnp.zeros((64,pad),f32),fk[:,T:]],axis=0)).astype(bf)
        else:
            yb=y.astype(bf)
            ones=jnp.ones((16,T+pad),bf)
            for h in range(heads):
                vt_ref[h,:HD,:T]=yb[HD*h:HD*h+HD]
                vt_ref[h,:HD,T:]=jnp.zeros((HD,pad),bf)
                vt_ref[h,HD:,:]=ones
            for g in range(groups):
                piece=jnp.concatenate([y[64*g:64*g+64],jnp.zeros((64,T),f32)],axis=0)
                vn_ref[g,:T,:]=jnp.transpose(piece).astype(bf)
                vn_ref[g,T:,:]=jnp.zeros((pad,128),bf)
    z32=jnp.zeros((HD,QT),bf)
    def qtile(i,_):
        q0=pl.multiple_of(i*QT,QT)
        lo=rng_ref[0,i]; n=rng_ref[1,i]
        fq=fq_ref[:,pl.ds(q0,QT)]
        for g in range(groups):
            q=qt_ref[64*g:64*g+64,pl.ds(q0,QT)]
            left=jnp.concatenate([q[:HD],z32,fq],axis=0)
            right=jnp.concatenate([z32,q[HD:],fq],axis=0)
            qbd_ref[g]=jnp.concatenate([left,right],axis=1)
        def chunk(j,carry):
            k0=pl.multiple_of(lo*128+j*KC,128)
            new=[]
            for g in range(groups):
                m,acc=carry[g]
                s=jnp.dot(kp_ref[g,pl.ds(k0,KC),:],qbd_ref[g],preferred_element_type=f32)
                mn=jnp.maximum(m,jnp.max(s,axis=0,keepdims=True))
                al=jnp.exp2(m-mn)
                p=jnp.exp2(s-mn).astype(bf)
                outs=[]
                for a in range(2):
                    pv=jnp.dot(vt_ref[2*g+a,:,pl.ds(k0,KC)],p[:,QT*a:QT*a+QT],preferred_element_type=f32)
                    outs.append(acc[a]*al[:,QT*a:QT*a+QT]+pv)
                new.append((mn,tuple(outs)))
            return tuple(new)
        init=tuple((jnp.full((1,2*QT),-3e38,f32),(jnp.zeros((48,QT),f32),jnp.zeros((48,QT),f32))) for g in range(groups))
        res=lax.fori_loop(0,n,chunk,init)
        for g in range(groups):
            m,acc=res[g]
            for a in range(2):
                h=2*g+a
                l=acc[a][HD:HD+1]
                ot_ref[HD*h:HD*h+HD,pl.ds(q0,QT)]=(acc[a][:HD]/l).astype(bf)
                lse_ref[h:h+1,pl.ds(q0,QT)]=m[:,QT*a:QT*a+QT]+jnp.log2(l)
        return 0
    lax.fori_loop(0,T//QT,qtile,0)

def attn_fwd(rng,n1,w,b,cos,sin,fq,fk):
    T=n1.shape[0]; width=w.shape[2]; heads=width//HD; groups=heads//2; TP=T+128
    V=pl.BlockSpec(memory_space=pltpu.VMEM); S=pl.BlockSpec(memory_space=pltpu.SMEM)
    return pl.pallas_call(fwd_body,
        out_shape=(jax.ShapeDtypeStruct((width,T),bf),jax.ShapeDtypeStruct((width,TP),bf),jax.ShapeDtypeStruct((groups,TP,128),bf),
                   jax.ShapeDtypeStruct((groups,TP,128),bf),jax.ShapeDtypeStruct((width,T),bf),jax.ShapeDtypeStruct((16,T),f32)),
        in_specs=[S]+[V]*7, out_specs=tuple([V]*6),
        scratch_shapes=[pltpu.VMEM((heads,48,TP),bf),pltpu.VMEM((groups,128,2*QT),bf)],
        compiler_params=pltpu.CompilerParams(vmem_limit_bytes=VM),
        cost_estimate=pl.CostEstimate(flops=12*10**9,bytes_accessed=10**7,transcendentals=5*10**6),
        name="attention_forward")(rng,n1,w,b,cos,sin,fq,fk)

def bwd_body(rng_ref,g_ref,n1_ref,wo_ref,w_ref,qt_ref,kt_ref,kp_ref,vn_ref,ot_ref,lse_ref,cos_ref,sin_ref,fq_ref,gin_ref,
             dw_ref,db_ref,gn_ref,dot_ref,delta_ref,dqt_ref,dkt_ref,dvt_ref,qbd_ref,dobd_ref):
    width=w_ref.shape[2]; heads=width//HD; groups=heads//2; T=n1_ref.shape[0]
    doT=dg(wo_ref[...],g_ref[...],0,1).astype(bf)
    dot_ref[...]=doT
    prod=doT.astype(f32)*ot_ref[...].astype(f32)
    for h in range(heads):
        delta_ref[h:h+1,:]=jnp.sum(prod[HD*h:HD*h+HD],axis=0,keepdims=True)
    dkt_ref[...]=jnp.zeros_like(dkt_ref); dvt_ref[...]=jnp.zeros_like(dvt_ref)
    z32=jnp.zeros((HD,QT),bf); z64=jnp.zeros((64,2*QT),bf)
    def qtile(i,_):
        q0=pl.multiple_of(i*QT,QT)
        lo=rng_ref[0,i]; n=rng_ref[1,i]
        fq=fq_ref[:,pl.ds(q0,QT)]
        for g in range(groups):
            q=qt_ref[64*g:64*g+64,pl.ds(q0,QT)]
            qbd_ref[g]=jnp.concatenate([jnp.concatenate([q[:HD],z32,fq],axis=0),jnp.concatenate([z32,q[HD:],fq],axis=0)],axis=1)
            d=dot_ref[64*g:64*g+64,pl.ds(q0,QT)]
            dobd_ref[g]=jnp.concatenate([jnp.concatenate([jnp.concatenate([d[:HD],z32],axis=0),jnp.concatenate([z32,d[HD:]],axis=0)],axis=1),z64],axis=0)
        def chunk(j,carry):
            k0=pl.multiple_of(lo*128+j*KC,128)
            new=[]
            for g in range(groups):
                s=jnp.dot(kp_ref[g,pl.ds(k0,KC),:],qbd_ref[g],preferred_element_type=f32)
                dp=jnp.dot(vn_ref[g,pl.ds(k0,KC),:],dobd_ref[g],preferred_element_type=f32)
                lse=jnp.concatenate([lse_ref[2*g:2*g+1,pl.ds(q0,QT)],lse_ref[2*g+1:2*g+2,pl.ds(q0,QT)]],axis=1)
                dl=jnp.concatenate([delta_ref[2*g:2*g+1,pl.ds(q0,QT)],delta_ref[2*g+1:2*g+2,pl.ds(q0,QT)]],axis=1)
                p=jnp.exp2(s-lse)
                ds=(p*(dp-dl)).astype(bf)
                p=p.astype(bf)
                dqs=[]
                for a in range(2):
                    h=2*g+a
                    rows=slice(HD*h,HD*h+HD); cols=slice(QT*a,QT*a+QT)
                    dvt_ref[rows,pl.ds(k0,KC)]+=dg(dot_ref[rows,pl.ds(q0,QT)],p[:,cols],1,1)
                    dkt_ref[rows,pl.ds(k0,KC)]+=dg(qt_ref[rows,pl.ds(q0,QT)],ds[:,cols],1,1)
                    dqs.append(carry[g][a]+jnp.dot(kt_ref[rows,pl.ds(k0,KC)],ds[:,cols],preferred_element_type=f32))
                new.append(tuple(dqs))
            return tuple(new)
        init=tuple((jnp.zeros((HD,QT),f32),)*2 for g in range(groups))
        res=lax.fori_loop(0,n,chunk,init)
        for g in range(groups):
            for a in range(2):
                h=2*g+a
                dqt_ref[HD*h:HD*h+HD,pl.ds(q0,QT)]=res[g][a]
        return 0
    lax.fori_loop(0,T//QT,qtile,0)
    cos=cos_ref[...]; sin=sin_ref[...]
    n1t=jnp.transpose(n1_ref[...])
    gt=jnp.transpose(g_ref[...])
    dw_ref[3]=dg(gt,ot_ref[...],1,1).astype(bf)
    gn=gin_ref[...]
    for c in range(3):
        if c==0: y=rope_rows(dqt_ref[...]*(HD**-0.5),cos,sin,heads,-1.0)
        elif c==1: y=rope_rows(dkt_ref[:,:T]*LN2,cos,sin,heads,-1.0)
        else: y=dvt_ref[:,:T]
        yb=y.astype(bf)
        db_ref[:,c:c+1]=jnp.sum(yb.astype(f32),axis=1,keepdims=True)
        dw_ref[c]=dg(n1t,yb,1,1).astype(bf)
        gn=gn+dg(yb,w_ref[c],0,1)
    gn_ref[...]=gn

def attn_bwd(rng,g,n1,wo,w,qt,kt,kp,vn,ot,lse,cos,sin,fq,gin):
    T=n1.shape[0]; width=w.shape[2]; D=n1.shape[1]; heads=width//HD; groups=heads//2; TP=T+128
    V=pl.BlockSpec(memory_space=pltpu.VMEM); S=pl.BlockSpec(memory_space=pltpu.SMEM)
    return pl.pallas_call(bwd_body,
        out_shape=(jax.ShapeDtypeStruct((4,D,width),bf),jax.ShapeDtypeStruct((width,8),f32),jax.ShapeDtypeStruct((T,D),f32)),
        in_specs=[S]+[V]*14, out_specs=tuple([V]*3),
        scratch_shapes=[pltpu.VMEM((width,T),bf),pltpu.VMEM((16,T),f32),pltpu.VMEM((width,T),f32),pltpu.VMEM((width,TP),f32),pltpu.VMEM((width,TP),f32),
                        pltpu.VMEM((groups,128,2*QT),bf),pltpu.VMEM((groups,128,2*QT),bf)],
        compiler_params=pltpu.CompilerParams(vmem_limit_bytes=VM),
        cost_estimate=pl.CostEstimate(flops=25*10**9,bytes_accessed=2*10**7,transcendentals=5*10**6),
        name="attention_backward")(rng,g,n1,wo,w,qt,kt,kp,vn,ot,lse,cos,sin,fq,gin)

def tables(seg):
    T=seg.shape[0]; TP=T+128
    ids=jnp.arange(8,dtype=jnp.int32)
    starts=jnp.sum((seg[None,:]<ids[:,None]).astype(jnp.int32),axis=1)
    ends=jnp.sum((seg[None,:]<=ids[:,None]).astype(jnp.int32),axis=1)
    onehot=(seg[None,:]==ids[:,None])
    before=jnp.sum(jnp.where(onehot,starts[:,None],0),axis=0)
    after=jnp.sum(jnp.where(onehot,ends[:,None],0),axis=0)
    pos=(jnp.arange(T,dtype=jnp.int32)-before).astype(f32)
    freq=10000.0**(-jnp.arange(0,HD,2).astype(f32)/HD)
    ang=freq[:,None]*pos[None,:]
    fq=jnp.where(onehot,0.0,-BIG).astype(bf)
    fq=jnp.concatenate([fq,jnp.zeros((56,T),bf)],axis=0)
    padk=jnp.broadcast_to((ids[:,None]==7),(8,TP-T))
    fk=jnp.concatenate([jnp.concatenate([onehot,padk],axis=1).astype(bf),jnp.zeros((56,TP),bf)],axis=0)
    lo=before[::QT]//128
    hi=after[QT-1::QT]
    n=(hi-lo*128+KC-1)//KC
    return jnp.cos(ang),jnp.sin(ang),fq,fk,jnp.stack([lo,n])

def ffn_body(oa_ref,ob_ref,woa_ref,wob_ref,x_ref,og_ref,nv_ref,hb_ref,w1a_ref,w1b_ref,w2a_ref,w2b_ref,
             out_ref,glow_ref,gres_ref,dw1_ref,dw2_ref,dhb_ref,vec_ref,
             res_ref,n2_ref,n2t_ref,ogt_ref,mix_ref,gn_ref):
    j=pl.program_id(0); half=pl.num_programs(0)//2; last=pl.num_programs(0)-1
    D=x_ref.shape[1]
    @pl.when(j==0)
    def _():
        att=dg(oa_ref[...],woa_ref[...],0,1)+dg(ob_ref[...],wob_ref[...],0,1)
        res=x_ref[...].astype(f32)+att+nv_ref[2:3]
        res_ref[...]=res
        cen=res-jnp.mean(res,axis=1,keepdims=True)
        var=jnp.mean(cen*cen,axis=1,keepdims=True)
        n2=cen*lax.rsqrt(var+EPS_NORM)*nv_ref[3:4]+nv_ref[4:5]
        n2b=n2.astype(bf)
        n2_ref[...]=n2b
        n2t_ref[...]=jnp.transpose(n2b)
        ogt_ref[...]=jnp.transpose(og_ref[...])
        mix_ref[...]=jnp.zeros_like(mix_ref)
        gn_ref[...]=jnp.zeros_like(gn_ref)
    own=j<half
    w1=jnp.where(own,w1a_ref[...],w1b_ref[...])
    w2=jnp.where(own,w2a_ref[...],w2b_ref[...])
    pre=jnp.dot(n2_ref[...],w1,preferred_element_type=f32)+hb_ref[0]
    gact=jnp.dot(og_ref[...],w2,preferred_element_type=f32)
    cdf=0.5+0.5*lax.erf(pre*(2.0**-0.5))
    act=(pre*cdf).astype(bf)
    pdf=jnp.exp(pre*pre*-0.5)*((2.0*math.pi)**-0.5)
    gpre=(gact*(cdf+pre*pdf)).astype(bf)
    mix_ref[...]+=dg(act,w2,1,1)
    gn_ref[...]+=dg(gpre,w1,1,1)
    dw1_ref[0]=jnp.dot(n2t_ref[...],gpre,preferred_element_type=f32).astype(bf)
    dw2_ref[0]=jnp.dot(ogt_ref[...],act,preferred_element_type=f32).astype(bf)
    dhb_ref[0]=jnp.sum(gpre.astype(f32),axis=0,keepdims=True)
    @pl.when(j==last)
    def _():
        res=res_ref[...]
        out_ref[...]=(res+mix_ref[...]+nv_ref[5:6]).astype(bf)
        og=og_ref[...].astype(f32)
        cen=res-jnp.mean(res,axis=1,keepdims=True)
        var=jnp.mean(cen*cen,axis=1,keepdims=True)
        r=lax.rsqrt(var+EPS_NORM)
        xh=cen*r
        gn=gn_ref[...]
        e=gn*nv_ref[3:4]
        gres=og+r*(e-jnp.mean(e,axis=1,keepdims=True)-xh*jnp.mean(e*xh,axis=1,keepdims=True))
        gres_ref[...]=gres
        glow_ref[...]=gres.astype(bf)
        vec_ref[...]=jnp.concatenate([jnp.sum(gres,axis=0,keepdims=True),jnp.sum(gn*xh,axis=0,keepdims=True),
            jnp.sum(gn,axis=0,keepdims=True),jnp.sum(og,axis=0,keepdims=True),jnp.zeros((4,D),f32)],axis=0)

def ffn(oa,ob,woa,wob,x,og,nv,hb,w1a,w1b,w2a,w2b):
    T,D=x.shape; F=w1a.shape[1]; FB=256; half=F//FB; nb=2*half
    V=pl.BlockSpec(memory_space=pltpu.VMEM)
    wa=pl.BlockSpec((D,FB),lambda j:(0,jnp.minimum(j,half-1)))
    wb=pl.BlockSpec((D,FB),lambda j:(0,jnp.maximum(j-half,0)))
    dw=pl.BlockSpec((1,D,FB),lambda j:(j//half,0,lax.rem(j,half)))
    bb=pl.BlockSpec((1,1,FB),lambda j:(j,0,0))
    return pl.pallas_call(ffn_body,grid=(nb,),
        out_shape=(jax.ShapeDtypeStruct((T,D),bf),jax.ShapeDtypeStruct((T,D),bf),jax.ShapeDtypeStruct((T,D),f32),
            jax.ShapeDtypeStruct((2,D,F),bf),jax.ShapeDtypeStruct((2,D,F),bf),jax.ShapeDtypeStruct((nb,1,FB),f32),jax.ShapeDtypeStruct((8,D),f32)),
        in_specs=[V]*7+[bb,wa,wb,wa,wb],out_specs=(V,V,V,dw,dw,bb,V),
        scratch_shapes=[pltpu.VMEM((T,D),f32),pltpu.VMEM((T,D),bf),pltpu.VMEM((D,T),bf),pltpu.VMEM((D,T),bf),pltpu.VMEM((T,D),f32),pltpu.VMEM((T,D),f32)],
        compiler_params=pltpu.CompilerParams(vmem_limit_bytes=VM),
        cost_estimate=pl.CostEstimate(flops=22*10**9,bytes_accessed=3*10**7,transcendentals=5*10**6),
        name="ffn")(oa,ob,woa,wob,x,og,nv,hb,w1a,w1b,w2a,w2b)

def tail_body(gn_ref,gres_ref,x_ref,nv_ref,out_ref,vec_ref):
    j=pl.program_id(0); D=x_ref.shape[1]
    x=x_ref[...].astype(f32)
    cen=x-jnp.mean(x,axis=1,keepdims=True)
    var=jnp.mean(cen*cen,axis=1,keepdims=True)
    r=lax.rsqrt(var+EPS_NORM)
    xh=cen*r
    gn=gn_ref[...]
    e=gn*nv_ref[0:1]
    out_ref[...]=(gres_ref[...]+r*(e-jnp.mean(e,axis=1,keepdims=True)-xh*jnp.mean(e*xh,axis=1,keepdims=True))).astype(bf)
    v=jnp.concatenate([jnp.sum(gn*xh,axis=0,keepdims=True),jnp.sum(gn,axis=0,keepdims=True),jnp.zeros((6,D),f32)],axis=0)
    @pl.when(j==0)
    def _(): vec_ref[...]=v
    @pl.when(j>0)
    def _(): vec_ref[...]+=v

def tail(gn,gres,x,nv):
    T,D=x.shape; B=256
    row=pl.BlockSpec((B,D),lambda j:(j,0)); one=pl.BlockSpec((8,D),lambda j:(0,0))
    return pl.pallas_call(tail_body,grid=(T//B,),out_shape=(jax.ShapeDtypeStruct((T,D),bf),jax.ShapeDtypeStruct((8,D),f32)),
        in_specs=[row,row,row,one],out_specs=(row,one),
        compiler_params=pltpu.CompilerParams(vmem_limit_bytes=VM),
        cost_estimate=pl.CostEstimate(flops=2*10**7,bytes_accessed=10**7,transcendentals=0),
        name="norm_backward")(gn,gres,x,nv)

def bit_groups(count):
    bits=count.bit_length()-1
    groups=[]
    top=bits
    while top>2:
        take=2 if top>3 else 1
        groups.append((top-take,take)); top-=take
    while top>0:
        groups.append((top-1,1)); top-=1
    return groups

def swap(value,axis_name,offset):
    n=lax.axis_size(axis_name)
    return lax.ppermute(value,axis_name,[(i,i^offset) for i in range(n)])

def order_blocks(blocks,place,axis):
    count=len(blocks)
    if count==1: return blocks[0]
    half=count//2
    low=place%half if half>1 else 0
    first=order_blocks(blocks[:half],low,axis); second=order_blocks(blocks[half:],low,axis)
    high=(place//half)%2
    return jnp.where(high==0,jnp.concatenate([first,second],axis),jnp.concatenate([second,first],axis))

def gather_step(value,group,axis):
    low,take=group
    place=(lax.axis_index("dp")>>low)%(1<<take)
    return order_blocks([value]+[swap(value,"dp",k<<low) for k in range(1,1<<take)],place,axis)

def scatter_step(value,group,axis,last_type):
    low,take=group
    place=(lax.axis_index("dp")>>low)%(1<<take)
    total=lax.dynamic_slice_in_dim(value,place,1,axis).astype(f32)
    for k in range(1,1<<take):
        total=total+swap(lax.dynamic_slice_in_dim(value,place^k,1,axis),"dp",k<<low).astype(f32)
    return total.astype(last_type)

def start_blocks(value,groups):
    return value.reshape((value.shape[0],)+(1,)*len(groups)+value.shape[1:])

def merge_blocks(value):
    return value.reshape((value.shape[0],-1,value.shape[-1]))

def gather_late(value,groups):
    value=start_blocks(value,groups)
    for at,group in enumerate(groups[:-1]): value=gather_step(value,group,1+at)
    peer=swap(value,"tp",1)
    at=len(groups)
    return merge_blocks(gather_step(value,groups[-1],at)),merge_blocks(gather_step(peer,groups[-1],at))

def gather_early(value,groups):
    value=start_blocks(jnp.stack([value,swap(value,"tp",1)]).reshape((-1,)+value.shape[1:]),groups)
    for at,group in enumerate(groups): value=gather_step(value,group,1+at)
    value=merge_blocks(value)
    half=value.shape[0]//2
    return value[:half],value[half:]

def scatter(value,groups,shard_rows):
    shape=(value.shape[0],)+tuple(1<<take for _,take in groups)+(shard_rows,value.shape[-1])
    value=value.reshape(shape)
    for at in range(len(groups)-1,-1,-1):
        value=scatter_step(value,groups[at],1+at,bf)
    return value.reshape((shape[0],shard_rows,shape[-1]))

def sum_all(value):
    value=value+swap(value,"tp",1)
    step=1
    while step<lax.axis_size("dp"):
        value=value+swap(value,"dp",step); step*=2
    return value

def by_peer(own,peer,axis):
    mine=lax.axis_index("tp")
    return jnp.where(mine==0,jnp.concatenate([own,peer],axis),jnp.concatenate([peer,own],axis))

def lamb_moments(weight, gradient, moment_one, moment_two):
    first_new = BETA_ONE * moment_one + (1.0 - BETA_ONE) * gradient
    second_new = BETA_TWO * moment_two + (1.0 - BETA_TWO) * gradient * gradient
    corrected = first_new / (1.0 - BETA_ONE**STEP)
    variance = second_new / (1.0 - BETA_TWO**STEP)
    update = corrected / (jnp.sqrt(variance) + EPS_ADAM) + DECAY * weight
    return (first_new, second_new, update)

def sum_squares(array):
    return jnp.sum(array * array, axis=tuple(range(1, array.ndim)))

def on_device(inputs,out_grad,segment_ids,attn_weights,ffn_weights,head_bias,hidden_bias,norm_vectors,
    attn_first,ffn_first,head_first,hidden_first,vector_first,attn_second,ffn_second,head_second,hidden_second,vector_second):
    dpn=lax.axis_size("dp"); tpn=lax.axis_size("tp"); mine=lax.axis_index("tp")
    rows,slots=segment_ids.shape
    assert rows==tpn==2
    groups=bit_groups(dpn)
    shard=attn_weights.shape[1]; hw=attn_weights.shape[2]; fw=ffn_weights.shape[2]; D=inputs.shape[1]
    qkv_own,qkv_peer=gather_late(attn_weights[:3].astype(bf),groups)
    wo_own,wo_peer=gather_late(attn_weights[3:].astype(bf),groups)
    w1_own,w1_peer=gather_late(ffn_weights[:1].astype(bf),groups)
    w2_own,w2_peer=gather_early(ffn_weights[1:].astype(bf),groups)
    bias_own=jnp.concatenate([head_bias.reshape(-1),hidden_bias])
    bias_peer=swap(bias_own.reshape(-1,hw),"tp",1).reshape(-1)
    def split_bias(b):
        hb=jnp.concatenate([b[:3*hw].reshape(3,hw),jnp.zeros((5,hw),f32)],0).T
        return hb,b[3*hw:]
    hb_own,hid_own=split_bias(bias_own); hb_peer,hid_peer=split_bias(bias_peer)
    x=lax.dynamic_slice_in_dim(inputs,mine*slots,slots,0)
    og=lax.dynamic_slice_in_dim(out_grad,mine*slots,slots,0)
    seg=lax.dynamic_index_in_dim(segment_ids,mine,0,keepdims=False)
    cos,sin,fq,fk,rng=tables(seg)
    nv=jnp.concatenate([norm_vectors,jnp.zeros((2,D),f32)],0)
    xf=x.astype(f32)
    cen=xf-jnp.mean(xf,axis=1,keepdims=True)
    var=jnp.mean(cen*cen,axis=1,keepdims=True)
    n1=(cen*lax.rsqrt(var+EPS_NORM)*norm_vectors[0]+norm_vectors[1]).astype(bf)
    fwd_own=attn_fwd(rng,n1,qkv_own,hb_own,cos,sin,fq,fk)
    fwd_peer=attn_fwd(rng,n1,qkv_peer,hb_peer,cos,sin,fq,fk)
    hid=jnp.concatenate([hid_own,hid_peer]).reshape(-1,1,256)
    out_low,glow,gres,dw1,dw2,dhb,vec2=ffn(fwd_own[4],fwd_peer[4],wo_own[0],wo_peer[0],x,og,nv,hid,w1_own[0],w1_peer[0],w2_own[0],w2_peer[0])
    layer_output=by_peer(out_low,swap(out_low,"tp",1),0)
    gffn=scatter(jnp.concatenate([dw1,dw2],0) if False else jnp.stack([dw1[0],dw2[0],dw1[1],dw2[1]]),groups,shard)
    gffn=gffn[:2].astype(f32)+swap(gffn[2:],"tp",1).astype(f32)
    def back(fwd,wo,w,gin):
        return attn_bwd(rng,glow,n1,wo[0],w,fwd[0],fwd[1],fwd[2],fwd[3],fwd[4],fwd[5],cos,sin,fq,gin)
    dwp,dbp,gn=back(fwd_peer,wo_peer,qkv_peer,jnp.zeros((slots,D),f32))
    gpeer=scatter(dwp,groups,shard)
    gpeer_in=swap(gpeer,"tp",1)
    dwo,dbo,gn=back(fwd_own,wo_own,qkv_own,gn)
    gattn=scatter(dwo,groups,shard).astype(f32)+gpeer_in.astype(f32)
    in_low,vec1=tail(gn,gres,x,nv)
    input_grad=by_peer(in_low,swap(in_low,"tp",1),0)
    head_full=by_peer(dbo[:,:3].T,dbp[:,:3].T,1)
    half_hidden=dhb.reshape(2,-1)
    hidden_full=by_peer(half_hidden[0],half_hidden[1],0)
    small=jnp.concatenate([head_full,vec1[:2],vec2[0:4],hidden_full.reshape(-1,D)],0)
    small=sum_all(small)
    sum_head=lax.dynamic_slice_in_dim(small[:3],mine*hw,hw,1)
    sum_vectors=small[3:9]
    sum_hidden=lax.dynamic_slice_in_dim(small[9:].reshape(-1),mine*fw,fw,0)
    masters=[attn_weights,ffn_weights,head_bias,hidden_bias.reshape(1,-1),norm_vectors]
    replicas=[1.0,1.0,1.0/dpn,1.0/dpn,1.0/(dpn*tpn)]
    grads=[gattn,gffn,sum_head,sum_hidden.reshape(1,-1),sum_vectors]
    firsts=[attn_first,ffn_first,head_first,hidden_first.reshape(1,-1),vector_first]
    seconds=[attn_second,ffn_second,head_second,hidden_second.reshape(1,-1),vector_second]
    results=[lamb_moments(masters[i],grads[i],firsts[i],seconds[i]) for i in range(5)]
    wterms=jnp.concatenate([sum_squares(masters[i])*replicas[i] for i in range(5)])
    uterms=jnp.concatenate([sum_squares(results[i][2])*replicas[i] for i in range(5)])
    terms=jnp.stack([wterms,uterms])
    norms=jnp.sqrt(sum_all(jnp.pad(terms,((0,6),(0,112)))))[:2,:16]
    ratio=norms[0]/norms[1]
    counts=[4,2,3,1,6]
    new=[]
    at=0
    for i in range(5):
        piece=ratio[at:at+counts[i]].reshape((-1,)+(1,)*(masters[i].ndim-1))
        new.append(masters[i]-RATE*piece*results[i][2]); at+=counts[i]
    return (layer_output,input_grad,new[0],new[1],new[2],new[3].reshape(-1),new[4],
        results[0][0],results[1][0],results[2][0],results[3][0].reshape(-1),results[4][0],
        results[0][1][:3],results[0][1][3],results[1][1],results[2][1],results[3][1].reshape(-1),results[4][1][2:],results[4][1][:2],norms)


def solution(mesh):
    in_specs = (
        P("dp", None),
        P("dp", None),
        P("dp", None),
        P(None, "dp", "tp"),
        P(None, "dp", "tp"),
        P(None, "tp"),
        P("tp"),
        P(),
        P(None, "dp", "tp"),
        P(None, "dp", "tp"),
        P(None, "tp"),
        P("tp"),
        P(),
        P(None, "dp", "tp"),
        P(None, "dp", "tp"),
        P(None, "tp"),
        P("tp"),
        P(),
    )
    out_specs = (
        P("dp", None),
        P("dp", None),
        P(None, "dp", "tp"),
        P(None, "dp", "tp"),
        P(None, "tp"),
        P("tp"),
        P(),
        P(None, "dp", "tp"),
        P(None, "dp", "tp"),
        P(None, "tp"),
        P("tp"),
        P(),
        P(None, "dp", "tp"),
        P("dp", "tp"),
        P(None, "dp", "tp"),
        P(None, "tp"),
        P("tp"),
        P(),
        P(),
        P(),
    )
    return jax.shard_map(
        on_device, mesh=mesh, in_specs=in_specs, out_specs=out_specs, check_vma=False
    )
```

```python
import math
from functools import partial

import jax
import jax.numpy as jnp
import numpy as np
from jax import lax
from jax.experimental import pallas as pl
from jax.experimental.pallas import tpu as pltpu
from jax.sharding import PartitionSpec as P

STEP = 10
EPS_NORM = 1e-05
EPS_ADAM = 1e-06
BETA_ONE = 0.9
BETA_TWO = 0.999
DECAY = 0.01
RATE = 0.5

HD = 32
QT = 128
KC = 256
BIG = 1e30
LN2 = math.log(2.0)
QSCALE = math.log2(math.e) / math.sqrt(HD)
bf = jnp.bfloat16
f32 = jnp.float32
VM = pl.BlockSpec(memory_space=pltpu.VMEM)
SM = pl.BlockSpec(memory_space=pltpu.SMEM)


def dg(a, b, ca, cb):
    return lax.dot_general(a, b, (((ca,), (cb,)), ((), ())), preferred_element_type=f32)


def shape(dims, kind):
    return jax.ShapeDtypeStruct(dims, kind)


def cost(gflop, mbytes):
    return pl.CostEstimate(
        flops=int(gflop * 1e9), bytes_accessed=int(mbytes * 1e6), transcendentals=0
    )


def params(mbytes=56):
    return pltpu.CompilerParams(vmem_limit_bytes=mbytes * 1024 * 1024)


def rope_rows(y, cos, sin, sign):
    out = []
    for h in range(y.shape[0] // HD):
        top = y[HD * h : HD * h + HD // 2]
        bot = y[HD * h + HD // 2 : HD * h + HD]
        out.append(top * cos - sign * bot * sin)
        out.append(bot * cos + sign * top * sin)
    return jnp.concatenate(out, axis=0)


def two_heads(block, extra):
    zero = jnp.zeros((HD, QT), bf)
    left = jnp.concatenate([block[:HD], zero] + extra, axis=0)
    right = jnp.concatenate([zero, block[HD:]] + extra, axis=0)
    return jnp.concatenate([left, right], axis=1)


def attention_forward(rng_ref, n1t_ref, an_ref, af_ref, b_ref, cos_ref, sin_ref, fq_ref, fk_ref, *refs):
    count = len(PARTS)
    qts, kts, kps, vns = (refs[count * i : count * i + count] for i in range(4))
    ot_ref, lse_ref, vt_ref, qbd_ref, s_ref = refs[4 * count :]
    width = ot_ref.shape[0]
    heads = width // HD
    groups = heads // 2
    slots = n1t_ref.shape[1]
    pad = kts[0].shape[1] - slots
    cos, sin = cos_ref[...], sin_ref[...]
    a = jnp.concatenate([an_ref[:, : 3 * width], af_ref[:, : 3 * width]], axis=0)
    y = dg(a, n1t_ref[...], 0, 0)
    qb = (rope_rows(y[:width] + b_ref[:, 0:1], cos, sin, 1.0) * QSCALE).astype(bf)
    kb = rope_rows(y[width : 2 * width] + b_ref[:, 1:2], cos, sin, 1.0).astype(bf)
    vb = (y[2 * width :] + b_ref[:, 2:3]).astype(bf)
    ones = jnp.ones((16, slots + pad), bf)
    for h in range(heads):
        vt_ref[h, :HD, :slots] = vb[HD * h : HD * h + HD]
        vt_ref[h, :HD, slots:] = jnp.zeros((HD, pad), bf)
        vt_ref[h, HD:, :] = ones
    past = jnp.transpose(jnp.concatenate([jnp.zeros((64, pad), bf), fk_ref[:, slots:]], axis=0))
    for (first, last), qt_ref, kt_ref, kp_ref, vn_ref in zip(PARTS, qts, kts, kps, vns):
        qt_ref[...] = qb[64 * first : 64 * last]
        kt_ref[:, :slots] = kb[64 * first : 64 * last]
        kt_ref[:, slots:] = jnp.zeros((64 * (last - first), pad), bf)
        for g in range(first, last):
            rows = slice(64 * g, 64 * g + 64)
            both = jnp.concatenate([kb[rows], fk_ref[:, :slots]], axis=0)
            kp_ref[g - first, :slots, :] = jnp.transpose(both)
            kp_ref[g - first, slots:, :] = past
            both = jnp.concatenate([vb[rows], jnp.zeros((64, slots), bf)], axis=0)
            vn_ref[g - first, :slots, :] = jnp.transpose(both)
            vn_ref[g - first, slots:, :] = jnp.zeros((pad, 128), bf)
    where = [(p, g - first) for p, (first, last) in enumerate(PARTS) for g in range(first, last)]

    def tile(i, _):
        q0 = pl.multiple_of(i * QT, QT)
        lo, count = rng_ref[0, i], rng_ref[1, i]
        fq = fq_ref[:, pl.ds(q0, QT)]
        for g in range(groups):
            p, r = where[g]
            qbd_ref[g] = two_heads(qts[p][64 * r : 64 * r + 64, pl.ds(q0, QT)], [fq])

        def scores(j, tops):
            k0 = pl.multiple_of(lo * 128 + j * KC, 128)
            at = pl.multiple_of(j * KC, KC)
            out = []
            for g in range(groups):
                p, r = where[g]
                keys = kps[p][r, pl.ds(k0, KC), :]
                s = jnp.dot(keys, qbd_ref[g], preferred_element_type=f32)
                s_ref[g, pl.ds(at, KC), :] = s
                top = tops[g]
                for r in range(KC // 8):
                    top = jnp.maximum(top, s[8 * r : 8 * r + 8])
                out.append(top)
            return tuple(out)

        start = tuple(jnp.full((8, 2 * QT), -3e38, f32) for _ in range(groups))
        tops = lax.fori_loop(0, count, scores, start)
        tops = [jnp.max(top, axis=0, keepdims=True) for top in tops]

        def mix(j, sums):
            k0 = pl.multiple_of(lo * 128 + j * KC, 128)
            at = pl.multiple_of(j * KC, KC)
            out = []
            for g in range(groups):
                p = jnp.exp2(s_ref[g, pl.ds(at, KC), :] - tops[g]).astype(bf)
                for a in range(2):
                    part = jnp.dot(
                        vt_ref[2 * g + a, :, pl.ds(k0, KC)],
                        p[:, QT * a : QT * a + QT],
                        preferred_element_type=f32,
                    )
                    out.append(sums[2 * g + a] + part)
            return tuple(out)

        start = tuple(jnp.zeros((48, QT), f32) for _ in range(heads))
        sums = lax.fori_loop(0, count, mix, start)
        for h in range(heads):
            total = sums[h][HD : HD + 1]
            ot_ref[HD * h : HD * h + HD, pl.ds(q0, QT)] = (sums[h][:HD] / total).astype(bf)
            col = QT * (h % 2)
            lse_ref[h : h + 1, pl.ds(q0, QT)] = tops[h // 2][:, col : col + QT] + jnp.log2(total)
        return 0

    lax.fori_loop(0, slots // QT, tile, 0)


PARTS = ((0, 5),)


def attn_fwd(rng, n1t, a, b, cos, sin, fq, fk):
    slots, width = n1t.shape[1], b.shape[0]
    heads, groups, longer = width // HD, width // 64, slots + 128
    assert groups == PARTS[-1][1]
    sizes = [last - first for first, last in PARTS]
    out = pl.pallas_call(
        attention_forward,
        out_shape=tuple(
            [shape((64 * n, slots), bf) for n in sizes]
            + [shape((64 * n, longer), bf) for n in sizes]
            + [shape((n, longer, 128), bf) for n in sizes] * 2
            + [shape((width, slots), bf), shape((16, slots), f32)]
        ),
        in_specs=[SM] + [VM] * 8,
        out_specs=(VM,) * (4 * len(sizes) + 2),
        scratch_shapes=[
            pltpu.VMEM((heads, 48, longer), bf),
            pltpu.VMEM((groups, 128, 2 * QT), bf),
            pltpu.VMEM((groups, longer, 2 * QT), f32),
        ],
        compiler_params=params(),
        cost_estimate=cost(12, 10),
        name="attention_forward",
    )(rng, n1t, *a, b, cos, sin, fq, fk)
    count = len(sizes)
    saved = [tuple(out[count * i + p] for i in range(4)) for p in range(count)]
    return saved, out[4 * count], out[4 * count + 1]


def attention_backward(
    first, rng_ref, dot_ref, qt_ref, kt_ref, kp_ref, vn_ref, lse_ref, delta_ref, cos_ref, sin_ref, fq_ref,
    dt_ref, dqt_ref, dkt_ref, dvt_ref, qbd_ref, dobd_ref,
):
    width, slots = qt_ref.shape
    heads = width // HD
    groups = heads // 2
    base = 64 * first
    dkt_ref[...] = jnp.zeros_like(dkt_ref)
    dvt_ref[...] = jnp.zeros_like(dvt_ref)
    blank = jnp.zeros((64, QT), bf)

    def tile(i, _):
        q0 = pl.multiple_of(i * QT, QT)
        lo, count = rng_ref[0, i], rng_ref[1, i]
        fq = fq_ref[:, pl.ds(q0, QT)]
        for g in range(groups):
            rows = slice(64 * g, 64 * g + 64)
            qbd_ref[g] = two_heads(qt_ref[rows, pl.ds(q0, QT)], [fq])
            dobd_ref[g] = two_heads(
                dot_ref[base + 64 * g : base + 64 * g + 64, pl.ds(q0, QT)], [blank]
            )

        def pair(ref, g):
            return jnp.concatenate(
                [
                    ref[2 * (first + g) + a : 2 * (first + g) + a + 1, pl.ds(q0, QT)]
                    for a in range(2)
                ],
                axis=1,
            )

        def chunk(j, sums):
            k0 = pl.multiple_of(lo * 128 + j * KC, 128)
            out = []
            for g in range(groups):
                s = jnp.dot(kp_ref[g, pl.ds(k0, KC), :], qbd_ref[g], preferred_element_type=f32)
                dp = jnp.dot(vn_ref[g, pl.ds(k0, KC), :], dobd_ref[g], preferred_element_type=f32)
                p = jnp.exp2(s - pair(lse_ref, g))
                ds = (p * (dp - pair(delta_ref, g))).astype(bf)
                p = p.astype(bf)
                for a in range(2):
                    h = 2 * g + a
                    rows, cols = slice(HD * h, HD * h + HD), slice(QT * a, QT * a + QT)
                    dvt_ref[rows, pl.ds(k0, KC)] += dg(
                        dot_ref[base + HD * h : base + HD * h + HD, pl.ds(q0, QT)], p[:, cols], 1, 1
                    )
                    dkt_ref[rows, pl.ds(k0, KC)] += dg(
                        qt_ref[rows, pl.ds(q0, QT)], ds[:, cols], 1, 1
                    )
                    out.append(
                        sums[h]
                        + jnp.dot(
                            kt_ref[rows, pl.ds(k0, KC)], ds[:, cols], preferred_element_type=f32
                        )
                    )
            return tuple(out)

        start = tuple(jnp.zeros((HD, QT), f32) for _ in range(heads))
        sums = lax.fori_loop(0, count, chunk, start)
        for h in range(heads):
            dqt_ref[HD * h : HD * h + HD, pl.ds(q0, QT)] = sums[h]
        return 0

    lax.fori_loop(0, slots // QT, tile, 0)
    cos, sin = cos_ref[...], sin_ref[...]
    dt_ref[0] = rope_rows(dqt_ref[...] * HD**-0.5, cos, sin, -1.0).astype(bf)
    dt_ref[1] = rope_rows(dkt_ref[:, :slots] * LN2, cos, sin, -1.0).astype(bf)
    dt_ref[2] = dvt_ref[:, :slots].astype(bf)


def attn_bwd(part, rng, dot, saved, lse, delta, cos, sin, fq):
    first, last = PARTS[part]
    width, slots = saved[0].shape
    groups, longer = last - first, slots + 128
    return pl.pallas_call(
        partial(attention_backward, first),
        out_shape=shape((3, width, slots), bf),
        in_specs=[SM] + [VM] * 10,
        out_specs=VM,
        scratch_shapes=[
            pltpu.VMEM((width, slots), f32),
            pltpu.VMEM((width, longer), f32),
            pltpu.VMEM((width, longer), f32),
            pltpu.VMEM((groups, 128, 2 * QT), bf),
            pltpu.VMEM((groups, 128, 2 * QT), bf),
        ],
        compiler_params=params(),
        cost_estimate=cost(4 * groups, 10),
        name="attention_backward",
    )(rng, dot, *saved, lse, delta, cos, sin, fq)


def weight_gradients(n1t_ref, gt_ref, ot_ref, *refs):
    *parts, keep_ref, send_ref, db_ref, rows_ref = refs
    at = pl.program_id(0)
    wide = rows_ref.shape[0]
    width = wide // 3

    @pl.when(at == 0)
    def _():
        begin = 0
        for c in range(3):
            for part in parts:
                count = part.shape[1]
                rows_ref[begin : begin + count] = part[c]
                begin += count
            db_ref[:, c : c + 1] = jnp.sum(
                rows_ref[c * width : c * width + width].astype(f32), axis=1, keepdims=True
            )

    left = dg(n1t_ref[...], rows_ref[...], 1, 1).astype(bf)
    right = dg(gt_ref[...], ot_ref[...], 1, 1).astype(bf)
    for step, out_ref in ((0, keep_ref), (1, send_ref)):

        @pl.when(at == step)
        def _():
            out_ref[:, :wide] = left
            out_ref[:, wide:] = right


def attn_grads(n1t, gt, ot, parts):
    model, slots = n1t.shape
    width = ot.shape[0]
    rows = pl.BlockSpec((model // 2, slots), lambda j: (j, 0))
    return pl.pallas_call(
        weight_gradients,
        grid=(2,),
        out_shape=(shape((model // 2, 4 * width), bf),) * 2 + (shape((width, 8), f32),),
        in_specs=[rows] * 2 + [VM] * (1 + len(parts)),
        out_specs=(VM, VM, VM),
        scratch_shapes=[pltpu.VMEM((3 * width, slots), bf)],
        compiler_params=params(),
        cost_estimate=cost(2, 10),
        name="attention_weight_gradients",
    )(n1t, gt, ot, *parts)


def normalize(values):
    centered = values - jnp.mean(values, axis=1, keepdims=True)
    scale = lax.rsqrt(jnp.mean(centered * centered, axis=1, keepdims=True) + EPS_NORM)
    return centered * scale, scale


def norm_backward(grad, gain, xhat, scale):
    e = grad * gain
    return scale * (
        e - jnp.mean(e, axis=1, keepdims=True) - xhat * jnp.mean(e * xhat, axis=1, keepdims=True)
    )


def column_sums(ref, parts, width):
    rows = [jnp.sum(part, axis=0, keepdims=True) for part in parts]
    rows.append(jnp.zeros((8 - len(parts), width), f32))
    total = jnp.concatenate(rows, axis=0)

    @pl.when(pl.program_id(0) == 0)
    def _():
        ref[...] = total

    @pl.when(pl.program_id(0) > 0)
    def _():
        ref[...] += total


TB = 256


def token_block(width):
    return pl.BlockSpec((TB, width), lambda j: (j, 0))


def lane_block(height):
    return pl.BlockSpec((height, TB), lambda j: (0, j))


def late_columns(a):
    return pl.BlockSpec((a[0].shape[0], a[0].shape[1] // 2), lambda j: (0, 1))


def attended_norm(oa_ref, ob_ref, aan_ref, aaf_ref, abn_ref, abf_ref, x_ref, nv_ref, res_ref, n2_ref, n2t_ref):
    width = oa_ref.shape[0]
    planes = [
        jnp.dot(a_ref[:, width:], oa_ref[...], preferred_element_type=f32)
        + jnp.dot(b_ref[:, width:], ob_ref[...], preferred_element_type=f32)
        for a_ref, b_ref in ((aan_ref, abn_ref), (aaf_ref, abf_ref))
    ]
    attended = jnp.transpose(jnp.concatenate(planes, axis=0))
    res = x_ref[...].astype(f32) + attended + nv_ref[2:3]
    res_ref[...] = res
    n2 = (normalize(res)[0] * nv_ref[3:4] + nv_ref[4:5]).astype(bf)
    n2_ref[...] = n2
    n2t_ref[...] = jnp.transpose(n2)


def middle(oa, ob, aa, ab, x, nv):
    slots, model = x.shape
    width = oa.shape[0]
    return pl.pallas_call(
        attended_norm,
        grid=(slots // TB,),
        out_shape=(
            shape((slots, model), f32),
            shape((slots, model), bf),
            shape((model, slots), bf),
        ),
        in_specs=[lane_block(width)] * 2 + [late_columns(aa)] * 4 + [token_block(model), VM],
        out_specs=(token_block(model),) * 2 + (lane_block(model),),
        compiler_params=params(),
        cost_estimate=cost(2, 10),
        name="attended_norm",
    )(oa, ob, *aa, *ab, x, nv)


def gelu_parts(pre):
    z = jnp.abs(pre) * (2.0**-0.5)
    bell = jnp.exp(-z * z)
    t = 1.0 / (1.0 + 0.3275911 * z)
    tail = t * (0.254829592 + t * (-0.284496736 + t * (1.421413741 + t * (-1.453152027 + t * 1.061405429))))
    half = 0.5 * tail * bell
    return jnp.where(pre >= 0.0, 1.0 - half, half), bell * ((2.0 * math.pi) ** -0.5)


def feed_forward(
    n2_ref, n2t_ref, og_ref, ogt_ref, hb_ref, w1n_ref, w1f_ref, w2n_ref, w2f_ref,
    mix_ref, gn_ref, keep_ref, send_ref, dhb_ref, up_ref, down_ref, act_ref, gpre_ref,
):
    j = pl.program_id(0)
    w1 = jnp.concatenate([w1n_ref[...], w1f_ref[...]], axis=0)
    w2 = jnp.concatenate([w2n_ref[...], w2f_ref[...]], axis=0)
    here = pl.ds(pl.multiple_of(j * FB, FB), FB)
    up_ref[:, here] = w1
    down_ref[:, here] = w2
    pre = jnp.dot(n2_ref[...], w1, preferred_element_type=f32) + hb_ref[0]
    gact = jnp.dot(og_ref[...], w2, preferred_element_type=f32)
    cdf = 0.5 + 0.5 * lax.erf(pre * (2.0**-0.5))
    pdf = jnp.exp(pre * pre * -0.5) * ((2.0 * math.pi) ** -0.5)
    act = (pre * cdf).astype(bf)
    gpre = (gact * (cdf + pre * pdf)).astype(bf)
    act_ref[:, here] = act
    gpre_ref[:, here] = gpre
    half = keep_ref.shape[0]
    for at, left, right in ((0, n2t_ref, gpre), (FB, ogt_ref, act)):
        dw = jnp.dot(left[...], right, preferred_element_type=f32).astype(bf)
        keep_ref[:, at : at + FB] = dw[:half]
        send_ref[:, at : at + FB] = dw[half:]
    dhb_ref[0] = jnp.sum(gpre.astype(f32), axis=0, keepdims=True)

    @pl.when(j == pl.num_programs(0) - 1)
    def _():
        mix_ref[...] = dg(act_ref[...], down_ref[...], 1, 1).astype(bf)
        gn_ref[...] = dg(gpre_ref[...], up_ref[...], 1, 1).astype(bf)


FB = 256


def ffn(n2, n2t, og, ogt, hb, w):
    slots, model = n2.shape
    hidden = w[0].shape[1] // 2
    blocks = hidden // FB
    up = pl.BlockSpec((model // 2, FB), lambda j: (0, j))
    down = pl.BlockSpec((model // 2, FB), lambda j: (0, blocks + j))
    bias = pl.BlockSpec((1, 1, FB), lambda j: (j, 0, 0))
    pair = pl.BlockSpec((model // 2, 2 * FB), lambda j: (0, j))
    return pl.pallas_call(
        feed_forward,
        grid=(hidden // FB,),
        out_shape=(
            shape((slots, model), bf),
            shape((slots, model), bf),
            shape((model // 2, 2 * hidden), bf),
            shape((model // 2, 2 * hidden), bf),
            shape((hidden // FB, 1, FB), f32),
        ),
        in_specs=[VM] * 4 + [bias, up, up, down, down],
        out_specs=(VM, VM, pair, pair, bias),
        scratch_shapes=[pltpu.VMEM((model, hidden), bf)] * 2 + [pltpu.VMEM((slots, hidden), bf)] * 2,
        compiler_params=params(),
        cost_estimate=cost(10, 10),
        name="feed_forward",
    )(n2, n2t, og, ogt, hb, *w, *w)


def second_norm_backward(
    ma_ref, mb_ref, ga_ref, gb_ref, res_ref, og_ref, nv_ref, perm_ref, aan_ref, aaf_ref, abn_ref, abf_ref, oa_ref, ob_ref,
    out_ref, gres_ref, gt_ref, dota_ref, dotb_ref, dela_ref, delb_ref, vec_ref, wot_ref,
):
    res, og = res_ref[...], og_ref[...].astype(f32)
    out = (res + (ma_ref[...].astype(f32) + mb_ref[...].astype(f32)) + nv_ref[5:6]).astype(bf)
    out_ref[...] = dg(out, perm_ref[...], 1, 1).astype(bf)
    xhat, scale = normalize(res)
    gn = ga_ref[...].astype(f32) + gb_ref[...].astype(f32)
    gres = og + norm_backward(gn, nv_ref[3:4], xhat, scale)
    gres_ref[...] = gres.astype(bf)
    width = oa_ref.shape[0]

    @pl.when(pl.program_id(0) == 0)
    def _():
        for at, near, far in ((0, aan_ref, aaf_ref), (1, abn_ref, abf_ref)):
            both = jnp.concatenate([near[:, width:], far[:, width:]], axis=0)
            wot_ref[at] = jnp.transpose(both)

    low = jnp.transpose(gres.astype(bf))
    gt_ref[...] = low
    for at, o_ref, dot_ref, del_ref in (
        (0, oa_ref, dota_ref, dela_ref),
        (1, ob_ref, dotb_ref, delb_ref),
    ):
        dot = jnp.dot(wot_ref[at], low, preferred_element_type=f32).astype(bf)
        dot_ref[...] = dot
        prod = dot.astype(f32) * o_ref[...].astype(f32)
        for h in range(prod.shape[0] // HD):
            del_ref[h : h + 1, :] = jnp.sum(prod[HD * h : HD * h + HD], axis=0, keepdims=True)
    column_sums(vec_ref, [gres, gn * xhat, gn, og], res.shape[1])


def middle_back(ma, mb, ga, gb, res, og, nv, perm, aa, ab, oa, ob):
    slots, model = res.shape
    width = oa.shape[0]
    tok, lane = token_block(model), lane_block(width)
    return pl.pallas_call(
        second_norm_backward,
        grid=(slots // TB,),
        out_shape=(
            shape((slots, model), bf),
            shape((slots, model), bf),
            shape((model, slots), bf),
            shape((width, slots), bf),
            shape((width, slots), bf),
            shape((16, slots), f32),
            shape((16, slots), f32),
            shape((8, model), f32),
        ),
        in_specs=[tok] * 6 + [VM] * 2 + [late_columns(aa)] * 4 + [lane] * 2,
        out_specs=(tok, tok, lane_block(model), lane, lane, lane_block(16), lane_block(16), VM),
        scratch_shapes=[pltpu.VMEM((2, width, model), bf)],
        compiler_params=params(),
        cost_estimate=cost(2, 10),
        name="second_norm_backward",
    )(ma, mb, ga, gb, res, og, nv, perm, *aa, *ab, oa, ob)


def first_norm_backward(aan_ref, aaf_ref, abn_ref, abf_ref, gres_ref, x_ref, nv_ref, perm_ref, *refs):
    *parts, out_ref, vec_ref = refs
    half = len(parts) // 2
    rows = [
        jnp.concatenate([part[c] for c in range(3) for part in mine], axis=0)
        for mine in (parts[:half], parts[half:])
    ]
    wide = rows[0].shape[0]
    planes = [
        jnp.dot(a_ref[:, :wide], rows[0], preferred_element_type=f32)
        + jnp.dot(b_ref[:, :wide], rows[1], preferred_element_type=f32)
        for a_ref, b_ref in ((aan_ref, abn_ref), (aaf_ref, abf_ref))
    ]
    gn = jnp.transpose(jnp.concatenate(planes, axis=0))
    xhat, scale = normalize(x_ref[...].astype(f32))
    gres = gres_ref[...].astype(f32)
    out = (gres + norm_backward(gn, nv_ref[0:1], xhat, scale)).astype(bf)
    out_ref[...] = dg(out, perm_ref[...], 1, 1).astype(bf)
    column_sums(vec_ref, [gn * xhat, gn], gn.shape[1])


def tail(aa, ab, gres, x, nv, perm, parts):
    slots, model = x.shape
    tok = token_block(model)
    blocks = [pl.BlockSpec((3, part.shape[1], TB), lambda j: (0, 0, j)) for part in parts]
    return pl.pallas_call(
        first_norm_backward,
        grid=(slots // TB,),
        out_shape=(shape((slots, model), bf), shape((8, model), f32)),
        in_specs=[VM] * 4 + [tok] * 2 + [VM] * 2 + blocks,
        out_specs=(tok, VM),
        compiler_params=params(),
        cost_estimate=cost(2, 10),
        name="first_norm_backward",
    )(*aa, *ab, gres, x, nv, perm, *parts)


def tables(seg):
    slots = seg.shape[0]
    ids = jnp.arange(8, dtype=jnp.int32)
    starts = jnp.sum((seg[None, :] < ids[:, None]).astype(jnp.int32), axis=1)
    ends = jnp.sum((seg[None, :] <= ids[:, None]).astype(jnp.int32), axis=1)
    member = seg[None, :] == ids[:, None]
    before = jnp.sum(jnp.where(member, starts[:, None], 0), axis=0)
    after = jnp.sum(jnp.where(member, ends[:, None], 0), axis=0)
    position = (jnp.arange(slots, dtype=jnp.int32) - before).astype(f32)
    frequency = 10000.0 ** (-jnp.arange(0, HD, 2).astype(f32) / HD)
    angles = frequency[:, None] * position[None, :]
    fq = jnp.concatenate([jnp.where(member, 0.0, -BIG), jnp.zeros((56, slots))], axis=0).astype(bf)
    past = jnp.broadcast_to(ids[:, None] == 7, (8, 128))
    fk = jnp.concatenate([member, past], axis=1).astype(bf)
    fk = jnp.concatenate([fk, jnp.zeros((56, slots + 128), bf)], axis=0)
    lo = before[::QT] // 128
    count = (after[QT - 1 :: QT] - lo * 128 + KC - 1) // KC
    return jnp.cos(angles), jnp.sin(angles), fq, fk, jnp.stack([lo, count])


def moments(weight, grad, first, second):
    first = BETA_ONE * first + (1.0 - BETA_ONE) * grad
    second = BETA_TWO * second + (1.0 - BETA_TWO) * grad * grad
    corrected = first / (1.0 - BETA_ONE**STEP)
    variance = second / (1.0 - BETA_TWO**STEP)
    return first, second, corrected / (jnp.sqrt(variance) + EPS_ADAM) + DECAY * weight


class Squares:
    def __init__(self):
        self.lane = lax.broadcasted_iota(jnp.int32, (8, 128), 1)
        self.row = lax.broadcasted_iota(jnp.int32, (8, 128), 0)
        self.total = jnp.zeros((8, 128), f32)

    def add(self, group, weight, update, share=1.0):
        for row, value in ((0, weight), (1, update)):
            square = jnp.sum(value * value, axis=(0, 1), keepdims=True) * share
            self.total = self.total + jnp.where(
                (self.lane == group) & (self.row == row), square, 0.0
            )


def all_parts(parts_ref, peer_ref):
    total = peer_ref[...].astype(f32)
    for i in range(parts_ref.shape[0]):
        total = total + parts_ref[i].astype(f32)
    return total


def lamb_ffn(parts_ref, peer_ref, w_ref, m_ref, v_ref, m_out, v_out, u_out, sq_out):
    grad = all_parts(parts_ref, peer_ref)
    blocks = w_ref.shape[2] // FB
    squares = Squares()
    for c in range(2):
        pieces = [grad[:, (2 * j + c) * FB : (2 * j + c + 1) * FB] for j in range(blocks)]
        first, second, update = moments(
            w_ref[c], jnp.concatenate(pieces, axis=1), m_ref[c], v_ref[c]
        )
        m_out[c], v_out[c], u_out[c] = first, second, update
        squares.add(4 + c, w_ref[c], update)
    sq_out[...] = squares.total


def step_ffn(parts, peer, w, m, v):
    return pl.pallas_call(
        lamb_ffn,
        out_shape=(shape(w.shape, f32),) * 3 + (shape((8, 128), f32),),
        in_specs=[VM] * 5,
        out_specs=(VM,) * 4,
        compiler_params=params(),
        cost_estimate=cost(1, 5),
        name="lamb_ffn",
    )(parts, peer, w, m, v)


def lamb_rest(
    shares, mine_ref, parts_ref, peer_ref, small_ref, sq_ref,
    w_ref, m_ref, v_ref, hw_ref, hm_ref, hv_ref, bw_ref, bm_ref, bv_ref, nw_ref, nm_ref, nv_ref,
    m_out, v_out, vo_out, u_out, hm_out, hv_out, hu_out, bm_out, bv_out, bu_out,
    nm_out, nv_out, nvo_out, nu_out, sq_out,
):
    grad = all_parts(parts_ref, peer_ref)
    width = w_ref.shape[2]
    squares = Squares()
    for c in range(4):
        first, second, update = moments(
            w_ref[c], grad[:, c * width : c * width + width], m_ref[c], v_ref[c]
        )
        m_out[c], u_out[c] = first, update
        if c < 3:
            v_out[c] = second
        else:
            vo_out[...] = second
        squares.add(c, w_ref[c], update)
    lower = mine_ref[0] == 0
    small = small_ref[...]
    grad = jnp.where(lower, small[0:3, :width], small[0:3, width:])
    hm_out[...], hv_out[...], hu_out[...] = moments(hw_ref[...], grad, hm_ref[...], hv_ref[...])
    grad = jnp.where(lower, small[9:11], small[11:13])
    bm_out[...], bv_out[...], bu_out[...] = moments(bw_ref[...], grad, bm_ref[...], bv_ref[...])
    first, second, update = moments(nw_ref[...], small[3:9], nm_ref[...], nv_ref[...])
    nm_out[...], nu_out[...] = first, update
    nvo_out[...], nv_out[...] = second[:2], second[2:]
    for c in range(3):
        squares.add(6 + c, hw_ref[c : c + 1], hu_out[c : c + 1], shares[0])
    squares.add(9, bw_ref[...], bu_out[...], shares[0])
    for c in range(6):
        squares.add(10 + c, nw_ref[c : c + 1], update[c : c + 1], shares[1])
    sq_out[...] = squares.total + sq_ref[...]


def step_rest(shares, mine, parts, peer, small, sq, attn, head, hidden, vector):
    w, h, b, n = attn[0], head[0], hidden[0], vector[0]
    return pl.pallas_call(
        partial(lamb_rest, shares),
        out_shape=tuple(
            shape(dims, f32)
            for dims in (
                w.shape, (3,) + w.shape[1:], w.shape[1:], w.shape,
                h.shape, h.shape, h.shape, b.shape, b.shape, b.shape,
                n.shape, (4, n.shape[1]), (2, n.shape[1]), n.shape, (8, 128),
            )
        ),
        in_specs=[SM] + [VM] * 16,
        out_specs=(VM,) * 15,
        compiler_params=params(),
        cost_estimate=cost(1, 5),
        name="lamb_rest",
    )(mine, parts, peer, small, sq, *attn, *head, *hidden, *vector)


def apply_updates(sums_ref, *refs):
    weights, updates, outs, norms_out = refs[:5], refs[5:10], refs[10:15], refs[15]
    total = sums_ref[0]
    for i in range(1, sums_ref.shape[0]):
        total = total + sums_ref[i]
    norms = jnp.sqrt(total)
    norms_out[...] = norms
    ratio = norms[0:1] / norms[1:2]
    lane = lax.broadcasted_iota(jnp.int32, (1, 128), 1)

    def rate(group):
        picked = jnp.where(lane == group, ratio, 0.0)
        return RATE * jnp.sum(picked, axis=1, keepdims=True)

    at = 0
    for count, w, u, out in zip((4, 2, 3, 1, 6), weights, updates, outs):
        for c in range(count):
            where = c if len(w.shape) == 3 else slice(None) if count == 1 else slice(c, c + 1)
            out[where] = w[where] - rate(at + c) * u[where]
        at += count


def new_weights(sums, weights, updates):
    return pl.pallas_call(
        apply_updates,
        out_shape=tuple(shape(w.shape, f32) for w in weights) + (shape((8, 128), f32),),
        in_specs=[VM] * 11,
        out_specs=(VM,) * 6,
        compiler_params=params(),
        cost_estimate=cost(1, 5),
        name="new_weights",
    )(sums, *weights, *updates)


def swap(value, axis_name, offset):
    count = lax.axis_size(axis_name)
    return lax.ppermute(value, axis_name, [(i, i ^ offset) for i in range(count)])


def planes():
    count = lax.axis_size("dp")
    return [[2 * u + core for u in range(count // 2)] for core in range(2)]


def exchange(blocks):
    return lax.all_to_all(blocks, "dp", 0, 0, axis_index_groups=planes())


def row_order(model, count):
    block = model // count
    place = np.arange(model) // block
    other = jnp.asarray(place // (count // 2), jnp.int32)
    owner = jnp.asarray(2 * (place % (count // 2)), jnp.int32) + (lax.axis_index("dp") % 2 ^ other)
    feature = owner * block + jnp.asarray(np.arange(model) % block, jnp.int32)
    return jnp.arange(model, dtype=jnp.int32)[:, None] == feature[None, :]


class Gather:
    def __init__(self, value, steps=("plane", "core")):
        self.value, self.steps, self.flying = value, list(steps), []

    def peer(self):
        return Gather(self.value, ("tp", "core"))

    def launch(self):
        step = self.steps[0]
        if step == "plane":
            count = lax.axis_size("dp") // 2
            spread = jnp.broadcast_to(self.value[None], (count,) + self.value.shape)
            self.flying = [exchange(spread)]
        else:
            self.flying = [swap(self.value, "dp" if step == "core" else "tp", 1)]

    def finish(self):
        step = self.steps.pop(0)
        if step == "core":
            self.value = (self.value, self.flying[0])
        else:
            self.value = self.flying[0].reshape(-1, self.flying[0].shape[-1])
        self.flying = []


class Scatter:
    def __init__(self, keep, send):
        self.value, self.send = keep, send
        self.steps, self.flying = ["core", "plane", "tp"], []

    def launch(self):
        step = self.steps[0]
        if step == "core":
            self.flying = [swap(self.send, "dp", 1)]
        elif step == "plane":
            count = lax.axis_size("dp") // 2
            self.flying = [exchange(self.value.reshape(count, -1, self.value.shape[-1]))]
        else:
            self.flying = [swap(jnp.sum(self.value.astype(f32), axis=0).astype(bf), "tp", 1)]

    def finish(self):
        step = self.steps.pop(0)
        if step == "core":
            self.value = (self.value.astype(f32) + self.flying[0].astype(f32)).astype(bf)
        else:
            self.value = self.flying[0]
        self.flying = []


def tie(value, *others):
    return lax.optimization_barrier((value, *others))[0]


def meet(value, *movers):
    out = lax.optimization_barrier((value, *[a for mover in movers for a in mover.flying]))
    at = 1
    for mover in movers:
        count = len(mover.flying)
        mover.flying = list(out[at : at + count])
        at += count
        mover.finish()
    return out[0]


def sum_over_dp(value):
    step = 1
    while step < lax.axis_size("dp"):
        value = value + swap(value, "dp", step)
        step *= 2
    return value


def by_peer(own, peer, axis):
    first = lax.axis_index("tp") == 0
    return jnp.where(
        first, jnp.concatenate([own, peer], axis), jnp.concatenate([peer, own], axis)
    )


def on_device(
    inputs, out_grad, segment_ids, attn_weights, ffn_weights, head_bias, hidden_bias, norm_vectors,
    attn_first, ffn_first, head_first, hidden_first, vector_first,
    attn_second, ffn_second, head_second, hidden_second, vector_second,
):
    dp_count, tp_count = lax.axis_size("dp"), lax.axis_size("tp")
    mine = lax.axis_index("tp")
    rows, slots = segment_ids.shape
    assert rows == tp_count == 2
    shard, head_width = attn_weights.shape[1:]
    hidden = ffn_weights.shape[2]
    model = inputs.shape[1]

    a_own = Gather(jnp.concatenate(list(attn_weights.astype(bf)), axis=1))
    a_own.launch()
    x = lax.dynamic_slice_in_dim(inputs, mine * slots, slots, 0)
    order = row_order(model, dp_count)
    perm = order.astype(bf)
    exact = partial(jnp.dot, precision=lax.Precision.HIGHEST, preferred_element_type=f32)
    nv = exact(jnp.concatenate([norm_vectors, jnp.zeros((2, model), f32)], 0), order.astype(f32))
    xt = dg(perm, x, 0, 1)
    centered = xt - jnp.mean(xt, axis=0, keepdims=True)
    scale = lax.rsqrt(jnp.mean(centered * centered, axis=0, keepdims=True) + EPS_NORM)
    n1t = (centered * scale * nv[0][:, None] + nv[1][:, None]).astype(bf)
    bias_own = jnp.concatenate([head_bias.reshape(-1), hidden_bias])
    bias_peer = swap(bias_own.reshape(-1, head_width), "tp", 1).reshape(-1)

    def head_columns(bias):
        biases = bias[: 3 * head_width].reshape(3, head_width)
        return jnp.concatenate([biases, jnp.zeros((5, head_width), f32)], 0).T

    def hidden_blocks(bias):
        return bias[3 * head_width :].reshape(-1, 1, FB)

    both = jnp.concatenate(list(ffn_weights.astype(bf)), axis=1)
    og = lax.dynamic_slice_in_dim(out_grad, mine * slots, slots, 0)
    seg = lax.dynamic_index_in_dim(segment_ids, mine, 0, keepdims=False)
    cos, sin, fq, fk, rng = tables(seg)
    x = dg(x, perm, 1, 0).astype(bf)
    ogt = dg(perm, og, 0, 1).astype(bf)
    og = dg(og, perm, 1, 0).astype(bf)
    n1t, cos, sin, fq, fk, rng, x, ogt, og, both = lax.optimization_barrier(
        (n1t, cos, sin, fq, fk, rng, x, ogt, og, both)
    )
    n1t = meet(tie(n1t, bias_peer), a_own)
    a_peer = a_own.peer()
    w_own = Gather(tie(both, a_own.value))
    a_own.launch()
    a_peer.launch()
    w_own.launch()

    n1t = meet(n1t, a_own)
    a_one = a_own.value
    saved_own, o_own, lse_own = attn_fwd(rng, n1t, a_one, head_columns(bias_own), cos, sin, fq, fk)
    o_own = meet(o_own, a_peer)
    a_peer.launch()
    again = meet(tie(n1t, o_own), a_peer)
    a_two = a_peer.value
    saved_peer, o_peer, lse_peer = attn_fwd(
        rng, again, a_two, head_columns(bias_peer), cos, sin, fq, fk
    )
    o_peer = meet(o_peer, w_own)
    w_peer = w_own.peer()
    w_own.launch()
    w_peer.launch()
    res, n2, n2t = middle(o_own, o_peer, a_one, a_two, x, nv)

    n2 = meet(n2, w_own)
    mix_own, gn_own, keep, send, dhb_own = ffn(n2, n2t, og, ogt, hidden_blocks(bias_own), w_own.value)
    f_own = Scatter(keep, send)
    f_own.launch()
    again = meet(tie(n2, mix_own), w_peer)
    w_peer.launch()
    again = meet(again, w_peer)
    mix_peer, gn_peer, keep, send, dhb_peer = ffn(
        again, n2t, og, ogt, hidden_blocks(bias_peer), w_peer.value
    )
    f_peer = Scatter(keep, send)
    mix_peer = meet(mix_peer, f_own)
    f_own.launch()
    f_peer.launch()
    out_low, gres, gt, dot_own, dot_peer, delta_own, delta_peer, sums_two = middle_back(
        mix_own, mix_peer, gn_own, gn_peer, res, og, nv, perm, a_one, a_two, o_own, o_peer
    )

    out_far = swap(out_low, "tp", 1)

    def back(part, dot, saved, lse, delta):
        return attn_bwd(part, rng, dot, saved[part], lse, delta, cos, sin, fq)

    dot_peer = meet(dot_peer, f_peer)
    dt_peer = back(0, dot_peer, saved_peer, lse_peer, delta_peer)
    o_last = meet(tie(o_peer, dt_peer), f_own)
    f_peer.value = tie(f_peer.value, dt_peer)
    f_peer.launch()
    keep, send, dbias_peer = attn_grads(n1t, gt, o_last, [dt_peer])
    g_peer = Scatter(keep, send)
    g_peer.launch()
    dot_own, out_far = lax.optimization_barrier((tie(dot_own, send), out_far))
    dt_own = back(0, dot_own, saved_own, lse_own, delta_own)
    o_last = meet(tie(o_own, dt_own), g_peer)
    keep, send, dbias_own = attn_grads(n1t, gt, o_last, [dt_own])
    g_own = Scatter(keep, send)
    g_own.launch()
    gres = meet(tie(gres, send), f_peer)
    g_peer.launch()
    f_peer.launch()
    gres = meet(gres, g_own, f_peer)
    in_low, sums_one = tail(a_one, a_two, gres, x, nv, perm, [dt_own, dt_peer])
    sums = exact(jnp.concatenate([sums_one[:2], sums_two[:4]], 0), order.astype(f32).T)
    small = jnp.concatenate(
        [
            by_peer(dbias_own[:, :3].T, dbias_peer[:, :3].T, 1),
            sums,
            by_peer(dhb_own.reshape(-1), dhb_peer.reshape(-1), 0).reshape(-1, model),
        ],
        0,
    )
    small = small + swap(small, "tp", 1)
    in_low = tie(in_low, small)
    in_far = swap(in_low, "tp", 1)
    g_peer.finish()
    g_own.value = tie(g_own.value, g_peer.value)
    g_own.launch()
    g_peer.launch()
    g_peer.finish()
    g_own.finish()

    def place(low, far):
        whole = jnp.zeros((2 * slots, model), bf)
        whole = lax.dynamic_update_slice_in_dim(whole, low, mine * slots, 0)
        return lax.dynamic_update_slice_in_dim(whole, far, (1 - mine) * slots, 0)

    layer_output = place(out_low, tie(out_far, in_low))
    input_grad = place(in_low, in_far)
    small = sum_over_dp(small)
    ffn_first_new, ffn_second_new, ffn_update, squares = step_ffn(
        f_own.value, f_peer.value, ffn_weights, ffn_first, ffn_second
    )
    wide = lambda v: v.reshape(2, -1)
    shares = (1.0 / dp_count, 1.0 / (dp_count * tp_count))
    (
        attn_first_new, attn_second_new, out_second_new, attn_update,
        head_first_new, head_second_new, head_update,
        hidden_first_new, hidden_second_new, hidden_update,
        vector_first_new, vector_second_new, norm_second_new, vector_update, squares,
    ) = step_rest(
        shares, mine.reshape(1), g_own.value, g_peer.value, small, squares,
        (attn_weights, attn_first, attn_second),
        (head_bias, head_first, head_second),
        (wide(hidden_bias), wide(hidden_first), wide(hidden_second)),
        (norm_vectors, vector_first, vector_second),
    )
    copies = dp_count * tp_count
    sums = lax.all_to_all(
        jnp.broadcast_to(squares[None], (copies, 8, 128)), ("dp", "tp"), 0, 0
    )
    new_attn, new_ffn, new_head, new_hidden, new_vectors, norms = new_weights(
        sums,
        (attn_weights, ffn_weights, head_bias, wide(hidden_bias), norm_vectors),
        (attn_update, ffn_update, head_update, hidden_update, vector_update),
    )
    return (
        layer_output,
        input_grad,
        new_attn,
        new_ffn,
        new_head,
        new_hidden.reshape(-1),
        new_vectors,
        attn_first_new,
        ffn_first_new,
        head_first_new,
        hidden_first_new.reshape(-1),
        vector_first_new,
        attn_second_new,
        out_second_new,
        ffn_second_new,
        head_second_new,
        hidden_second_new.reshape(-1),
        vector_second_new,
        norm_second_new,
        norms[:2, :16],
    )


def solution(mesh):
    in_specs = (
        P("dp", None),
        P("dp", None),
        P("dp", None),
        P(None, "dp", "tp"),
        P(None, "dp", "tp"),
        P(None, "tp"),
        P("tp"),
        P(),
        P(None, "dp", "tp"),
        P(None, "dp", "tp"),
        P(None, "tp"),
        P("tp"),
        P(),
        P(None, "dp", "tp"),
        P(None, "dp", "tp"),
        P(None, "tp"),
        P("tp"),
        P(),
    )
    out_specs = (
        P("dp", None),
        P("dp", None),
        P(None, "dp", "tp"),
        P(None, "dp", "tp"),
        P(None, "tp"),
        P("tp"),
        P(),
        P(None, "dp", "tp"),
        P(None, "dp", "tp"),
        P(None, "tp"),
        P("tp"),
        P(),
        P(None, "dp", "tp"),
        P("dp", "tp"),
        P(None, "dp", "tp"),
        P(None, "tp"),
        P("tp"),
        P(),
        P(),
        P(),
    )
    return jax.shard_map(
        on_device, mesh=mesh, in_specs=in_specs, out_specs=out_specs, check_vma=False
    )
```

```python
import math
from functools import partial

import jax
import jax.numpy as jnp
import numpy as np
from jax import lax
from jax.experimental import pallas as pl
from jax.experimental.pallas import tpu as pltpu
from jax.sharding import PartitionSpec as P

STEP = 10
EPS_NORM = 1e-05
EPS_ADAM = 1e-06
BETA_ONE = 0.9
BETA_TWO = 0.999
DECAY = 0.01
RATE = 0.5

HD = 32
QT = 128
KC = 256
BIG = 1e30
STRIDE = 64
SPARE = 256
LN2 = math.log(2.0)
QSCALE = math.log2(math.e) / math.sqrt(HD)
bf = jnp.bfloat16
f32 = jnp.float32
VM = pl.BlockSpec(memory_space=pltpu.VMEM)
SM = pl.BlockSpec(memory_space=pltpu.SMEM)


def dg(a, b, ca, cb):
    return lax.dot_general(a, b, (((ca,), (cb,)), ((), ())), preferred_element_type=f32)


def shape(dims, kind):
    return jax.ShapeDtypeStruct(dims, kind)


def cost(gflop, mbytes):
    return pl.CostEstimate(
        flops=int(gflop * 1e9), bytes_accessed=int(mbytes * 1e6), transcendentals=0
    )


def params(mbytes=56):
    return pltpu.CompilerParams(vmem_limit_bytes=mbytes * 1024 * 1024)


def rope_rows(y, cos, sin, sign):
    out = []
    for h in range(y.shape[0] // HD):
        top = y[HD * h : HD * h + HD // 2]
        bot = y[HD * h + HD // 2 : HD * h + HD]
        out.append(top * cos - sign * bot * sin)
        out.append(bot * cos + sign * top * sin)
    return jnp.concatenate(out, axis=0)


def two_heads(block, extra):
    zero = jnp.zeros((HD, QT), bf)
    left = jnp.concatenate([block[:HD], zero] + extra, axis=0)
    right = jnp.concatenate([zero, block[HD:]] + extra, axis=0)
    return jnp.concatenate([left, right], axis=1)


def attention_forward(col, rng_ref, n1t_ref, an_ref, af_ref, b_ref, cos_ref, sin_ref, fq_ref, fk_ref, *refs):
    count = len(PARTS)
    outs = refs[: 4 * count]
    ot_ref, lse_ref, vt_ref, qbd_ref, s_ref, *held, sem = refs[4 * count :]
    qts, kts, kps, vns = (held[count * i : count * i + count] for i in range(4))
    width = ot_ref.shape[0]
    heads = width // HD
    groups = heads // 2
    slots = n1t_ref.shape[1]
    pad = kts[0].shape[1] - slots
    cos, sin = cos_ref[...], sin_ref[...]
    a = jnp.concatenate([an_ref[:, : 3 * width], af_ref[:, : 3 * width]], axis=0)
    y = dg(a, n1t_ref[...], 0, 0)
    qb = (rope_rows(y[:width] + b_ref[:, col : col + 1], cos, sin, 1.0) * QSCALE).astype(bf)
    kb = rope_rows(y[width : 2 * width] + b_ref[:, col + 1 : col + 2], cos, sin, 1.0).astype(bf)
    vb = (y[2 * width :] + b_ref[:, col + 2 : col + 3]).astype(bf)
    ones = jnp.ones((16, slots + pad), bf)
    for odd, moved in enumerate((vb, vb[:, STRIDE:])):
        moved = jnp.concatenate(
            [moved, jnp.zeros((width, slots + pad - moved.shape[1]), bf)], axis=1
        )
        for h in range(heads):
            vt_ref[odd, h, :HD, :] = moved[HD * h : HD * h + HD]
            vt_ref[odd, h, HD:, :] = ones
    past = jnp.transpose(jnp.concatenate([jnp.zeros((64, pad), bf), fk_ref[:, slots:]], axis=0))
    for (first, last), qt_ref, kt_ref, kp_ref, vn_ref in zip(PARTS, qts, kts, kps, vns):
        qt_ref[...] = qb[64 * first : 64 * last]
        kt_ref[:, :slots] = kb[64 * first : 64 * last]
        kt_ref[:, slots:] = jnp.zeros((64 * (last - first), pad), bf)
        for g in range(first, last):
            rows = slice(64 * g, 64 * g + 64)
            both = jnp.concatenate([kb[rows], fk_ref[:, :slots]], axis=0)
            kp_ref[g - first, :slots, :] = jnp.transpose(both)
            kp_ref[g - first, slots:, :] = past
            both = jnp.concatenate([vb[rows], jnp.zeros((64, slots), bf)], axis=0)
            vn_ref[g - first, :slots, :] = jnp.transpose(both)
            vn_ref[g - first, slots:, :] = jnp.zeros((pad, 128), bf)
    saving = [
        pltpu.make_async_copy(src, dst, sem.at[i]) for i, (src, dst) in enumerate(zip(held, outs))
    ]
    for copy in saving:
        copy.start()
    where = [(p, g - first) for p, (first, last) in enumerate(PARTS) for g in range(first, last)]

    def tile(i, _):
        q0 = pl.multiple_of(i * QT, QT)
        lo, count = rng_ref[0, i], rng_ref[1, i]
        fq = fq_ref[:, pl.ds(q0, QT)]
        for g in range(groups):
            p, r = where[g]
            qbd_ref[g] = two_heads(qts[p][64 * r : 64 * r + 64, pl.ds(q0, QT)], [fq])

        def scores(j, tops):
            k0 = pl.multiple_of(lo * STRIDE + j * KC, STRIDE)
            at = pl.multiple_of(j * KC, KC)
            out = []
            for g in range(groups):
                p, r = where[g]
                keys = kps[p][r, pl.ds(k0, KC), :]
                s = jnp.dot(keys, qbd_ref[g], preferred_element_type=f32)
                s_ref[g, pl.ds(at, KC), :] = s
                top = tops[g]
                for r in range(KC // 8):
                    top = jnp.maximum(top, s[8 * r : 8 * r + 8])
                out.append(top)
            return tuple(out)

        start = tuple(jnp.full((8, 2 * QT), -3e38, f32) for _ in range(groups))
        tops = lax.fori_loop(0, count, scores, start)
        tops = [jnp.max(top, axis=0, keepdims=True) for top in tops]

        def mix(j, sums):
            k0 = pl.multiple_of((lo >> 1) * 128 + j * KC, 128)
            at = pl.multiple_of(j * KC, KC)
            out = []
            for g in range(groups):
                p = jnp.exp2(s_ref[g, pl.ds(at, KC), :] - tops[g]).astype(bf)
                for a in range(2):
                    part = jnp.dot(
                        vt_ref[lo & 1, 2 * g + a, :, pl.ds(k0, KC)],
                        p[:, QT * a : QT * a + QT],
                        preferred_element_type=f32,
                    )
                    out.append(sums[2 * g + a] + part)
            return tuple(out)

        start = tuple(jnp.zeros((48, QT), f32) for _ in range(heads))
        sums = lax.fori_loop(0, count, mix, start)
        for h in range(heads):
            total = sums[h][HD : HD + 1]
            ot_ref[HD * h : HD * h + HD, pl.ds(q0, QT)] = (sums[h][:HD] / total).astype(bf)
            col = QT * (h % 2)
            lse_ref[h : h + 1, pl.ds(q0, QT)] = tops[h // 2][:, col : col + QT] + jnp.log2(total)
        return 0

    lax.fori_loop(0, slots // QT, tile, 0)
    for copy in saving:
        copy.wait()


PARTS = ((0, 5),)


def attn_fwd(col, rng, n1t, a, b, cos, sin, fq, fk):
    slots, width = n1t.shape[1], b.shape[0]
    heads, groups, longer = width // HD, width // 64, slots + SPARE
    assert groups == PARTS[-1][1]
    sizes = [last - first for first, last in PARTS]
    held = (
        [(64 * n, slots) for n in sizes]
        + [(64 * n, longer) for n in sizes]
        + [(n, longer, 128) for n in sizes] * 2
    )
    out = pl.pallas_call(
        partial(attention_forward, col),
        out_shape=tuple(
            [shape(dims, bf) for dims in held] + [shape((width, slots), bf), shape((16, slots), f32)]
        ),
        in_specs=[SM] + [VM] * 8,
        out_specs=(pl.BlockSpec(memory_space=pl.ANY),) * len(held) + (VM, VM),
        scratch_shapes=[
            pltpu.VMEM((2, heads, 48, longer), bf),
            pltpu.VMEM((groups, 128, 2 * QT), bf),
            pltpu.VMEM((groups, longer, 2 * QT), f32),
        ]
        + [pltpu.VMEM(dims, bf) for dims in held]
        + [pltpu.SemaphoreType.DMA((len(held),))],
        compiler_params=params(),
        cost_estimate=cost(12, 10),
        name="attention_forward",
    )(rng, n1t, *a, b, cos, sin, fq, fk)
    count = len(sizes)
    saved = [tuple(out[count * i + p] for i in range(4)) for p in range(count)]
    return saved, out[4 * count], out[4 * count + 1]


def attention_backward(
    first, rng_ref, dot_ref, qt_ref, kt_ref, kp_ref, vn_ref, lse_ref, delta_ref, cos_ref, sin_ref, fq_ref,
    n1t_far, gt_far, ot_far, keep_ref, send_ref, db_ref, dt_far,
    dqt_ref, dkt_ref, dvt_ref, qbd_ref, dobd_ref, both_ref, n1t_ref, gt_ref, ot_ref, dt_ref, sem,
):
    loads = [
        pltpu.make_async_copy(src, dst, sem.at[i])
        for i, (src, dst) in enumerate(((n1t_far, n1t_ref), (gt_far, gt_ref), (ot_far, ot_ref)))
    ]
    for copy in loads:
        copy.start()
    width, slots = qt_ref.shape
    heads = width // HD
    groups = heads // 2
    base = 64 * first
    dkt_ref[...] = jnp.zeros_like(dkt_ref)
    dvt_ref[...] = jnp.zeros_like(dvt_ref)
    both_ref[0] = kt_ref[...]
    both_ref[1] = jnp.concatenate(
        [kt_ref[:, STRIDE:], jnp.zeros((width, STRIDE), bf)], axis=1
    )
    blank = jnp.zeros((64, QT), bf)

    def tile(i, _):
        q0 = pl.multiple_of(i * QT, QT)
        lo, count = rng_ref[0, i], rng_ref[1, i]
        fq = fq_ref[:, pl.ds(q0, QT)]
        for g in range(groups):
            rows = slice(64 * g, 64 * g + 64)
            qbd_ref[g] = two_heads(qt_ref[rows, pl.ds(q0, QT)], [fq])
            dobd_ref[g] = two_heads(
                dot_ref[base + 64 * g : base + 64 * g + 64, pl.ds(q0, QT)], [blank]
            )

        def pair(ref, g):
            return jnp.concatenate(
                [
                    ref[2 * (first + g) + a : 2 * (first + g) + a + 1, pl.ds(q0, QT)]
                    for a in range(2)
                ],
                axis=1,
            )

        def chunk(j, sums):
            k0 = pl.multiple_of(lo * STRIDE + j * KC, STRIDE)
            kl = pl.multiple_of((lo >> 1) * 128 + j * KC, 128)
            odd = lo & 1
            out = []
            for g in range(groups):
                s = jnp.dot(kp_ref[g, pl.ds(k0, KC), :], qbd_ref[g], preferred_element_type=f32)
                dp = jnp.dot(vn_ref[g, pl.ds(k0, KC), :], dobd_ref[g], preferred_element_type=f32)
                p = jnp.exp2(s - pair(lse_ref, g))
                ds = (p * (dp - pair(delta_ref, g))).astype(bf)
                p = p.astype(bf)
                for a in range(2):
                    h = 2 * g + a
                    rows, cols = slice(HD * h, HD * h + HD), slice(QT * a, QT * a + QT)
                    dvt_ref[odd, rows, pl.ds(kl, KC)] += dg(
                        dot_ref[base + HD * h : base + HD * h + HD, pl.ds(q0, QT)], p[:, cols], 1, 1
                    )
                    dkt_ref[odd, rows, pl.ds(kl, KC)] += dg(
                        qt_ref[rows, pl.ds(q0, QT)], ds[:, cols], 1, 1
                    )
                    out.append(
                        sums[h]
                        + jnp.dot(
                            both_ref[odd, rows, pl.ds(kl, KC)],
                            ds[:, cols],
                            preferred_element_type=f32,
                        )
                    )
            return tuple(out)

        start = tuple(jnp.zeros((HD, QT), f32) for _ in range(heads))
        sums = lax.fori_loop(0, count, chunk, start)
        for h in range(heads):
            dqt_ref[HD * h : HD * h + HD, pl.ds(q0, QT)] = sums[h]
        return 0

    lax.fori_loop(0, slots // QT, tile, 0)
    cos, sin = cos_ref[...], sin_ref[...]
    dt_ref[0] = rope_rows(dqt_ref[...] * HD**-0.5, cos, sin, -1.0).astype(bf)

    def joined(ref):
        moved = jnp.concatenate(
            [jnp.zeros((width, STRIDE), f32), ref[1, :, : slots - STRIDE]], axis=1
        )
        return ref[0, :, :slots] + moved

    dt_ref[1] = rope_rows(joined(dkt_ref) * LN2, cos, sin, -1.0).astype(bf)
    dt_ref[2] = joined(dvt_ref).astype(bf)
    store = pltpu.make_async_copy(dt_ref, dt_far, sem.at[3])
    store.start()
    rows = jnp.concatenate([dt_ref[c] for c in range(3)], axis=0)
    for c in range(3):
        db_ref[:, c : c + 1] = jnp.sum(dt_ref[c].astype(f32), axis=1, keepdims=True)
    for copy in loads:
        copy.wait()
    half, wide = keep_ref.shape[0], rows.shape[0]
    for cols, left, right in (
        (slice(0, wide), n1t_ref[...], rows),
        (slice(wide, keep_ref.shape[1]), gt_ref[...], ot_ref[...]),
    ):
        dw = dg(left, right, 1, 1).astype(bf)
        keep_ref[:, cols] = dw[:half]
        send_ref[:, cols] = dw[half:]
    store.wait()


def attn_bwd(rng, dot, saved, lse, delta, cos, sin, fq, n1t, gt, ot):
    first, last = PARTS[0]
    width, slots = saved[0].shape
    model = n1t.shape[0]
    groups, longer = last - first, slots + SPARE
    far = pl.BlockSpec(memory_space=pl.ANY)
    return pl.pallas_call(
        partial(attention_backward, first),
        out_shape=(shape((model // 2, 4 * width), bf),) * 2
        + (shape((width, 8), f32), shape((3, width, slots), bf)),
        in_specs=[SM] + [VM] * 10 + [far] * 3,
        out_specs=(VM, VM, VM, far),
        scratch_shapes=[
            pltpu.VMEM((width, slots), f32),
            pltpu.VMEM((2, width, longer), f32),
            pltpu.VMEM((2, width, longer), f32),
            pltpu.VMEM((groups, 128, 2 * QT), bf),
            pltpu.VMEM((groups, 128, 2 * QT), bf),
            pltpu.VMEM((2, width, longer), bf),
            pltpu.VMEM((model, slots), bf),
            pltpu.VMEM((model, slots), bf),
            pltpu.VMEM((width, slots), bf),
            pltpu.VMEM((3, width, slots), bf),
            pltpu.SemaphoreType.DMA((4,)),
        ],
        compiler_params=params(),
        cost_estimate=cost(4 * groups, 10),
        name="attention_backward",
    )(rng, dot, *saved, lse, delta, cos, sin, fq, n1t, gt, ot)


def normalize(values):
    centered = values - jnp.mean(values, axis=1, keepdims=True)
    scale = lax.rsqrt(jnp.mean(centered * centered, axis=1, keepdims=True) + EPS_NORM)
    return centered * scale, scale


def norm_backward(grad, gain, xhat, scale):
    e = grad * gain
    return scale * (
        e - jnp.mean(e, axis=1, keepdims=True) - xhat * jnp.mean(e * xhat, axis=1, keepdims=True)
    )


def column_sums(ref, parts, width):
    rows = [jnp.sum(part, axis=0, keepdims=True) for part in parts]
    rows.append(jnp.zeros((8 - len(parts), width), f32))
    total = jnp.concatenate(rows, axis=0)

    @pl.when(pl.program_id(0) == 0)
    def _():
        ref[...] = total

    @pl.when(pl.program_id(0) > 0)
    def _():
        ref[...] += total


TB = 256


def token_block(width):
    return pl.BlockSpec((TB, width), lambda j: (j, 0))


def lane_block(height):
    return pl.BlockSpec((height, TB), lambda j: (0, j))


def late_columns(a):
    return pl.BlockSpec((a[0].shape[0], a[0].shape[1] // 2), lambda j: (0, 1))


def attended_norm(oa_ref, ob_ref, aan_ref, aaf_ref, abn_ref, abf_ref, x_ref, nv_ref, res_ref, n2_ref, n2t_ref):
    width = oa_ref.shape[0]
    planes = [
        jnp.dot(a_ref[:, width:], oa_ref[...], preferred_element_type=f32)
        + jnp.dot(b_ref[:, width:], ob_ref[...], preferred_element_type=f32)
        for a_ref, b_ref in ((aan_ref, abn_ref), (aaf_ref, abf_ref))
    ]
    attended = jnp.transpose(jnp.concatenate(planes, axis=0))
    res = x_ref[...].astype(f32) + attended + nv_ref[2:3]
    res_ref[...] = res
    n2 = (normalize(res)[0] * nv_ref[3:4] + nv_ref[4:5]).astype(bf)
    n2_ref[...] = n2
    n2t_ref[...] = jnp.transpose(n2)


def middle(oa, ob, aa, ab, x, nv):
    slots, model = x.shape
    width = oa.shape[0]
    return pl.pallas_call(
        attended_norm,
        grid=(slots // TB,),
        out_shape=(
            shape((slots, model), f32),
            shape((slots, model), bf),
            shape((model, slots), bf),
        ),
        in_specs=[lane_block(width)] * 2 + [late_columns(aa)] * 4 + [token_block(model), VM],
        out_specs=(token_block(model),) * 2 + (lane_block(model),),
        compiler_params=params(),
        cost_estimate=cost(2, 10),
        name="attended_norm",
    )(oa, ob, *aa, *ab, x, nv)


def gelu_parts(pre):
    z = jnp.abs(pre) * (2.0**-0.5)
    bell = jnp.exp(-z * z)
    t = 1.0 / (1.0 + 0.3275911 * z)
    tail = t * (0.254829592 + t * (-0.284496736 + t * (1.421413741 + t * (-1.453152027 + t * 1.061405429))))
    half = 0.5 * tail * bell
    return jnp.where(pre >= 0.0, 1.0 - half, half), bell * ((2.0 * math.pi) ** -0.5)


def feed_forward(
    n2_far, n2t_far, og_far, ogt_far, hb_ref, w1n_ref, w1f_ref, w2n_ref, w2f_ref,
    mix_far, gn_ref, keep_ref, send_ref, dhb_ref,
    up_ref, down_ref, act_ref, gpre_ref, n2_ref, og_ref, n2t_ref, ogt_ref, mix_ref, sem,
):
    j = pl.program_id(0)
    pairs = ((n2_far, n2_ref), (og_far, og_ref), (n2t_far, n2t_ref), (ogt_far, ogt_ref))
    loads = [pltpu.make_async_copy(src, dst, sem.at[i]) for i, (src, dst) in enumerate(pairs)]

    @pl.when(j == 0)
    def _():
        for copy in loads:
            copy.start()
        loads[0].wait()
        loads[1].wait()

    w1 = jnp.concatenate([w1n_ref[...], w1f_ref[...]], axis=0)
    w2 = jnp.concatenate([w2n_ref[...], w2f_ref[...]], axis=0)
    here = pl.ds(pl.multiple_of(j * FB, FB), FB)
    up_ref[:, here] = w1
    down_ref[:, here] = w2
    pre = jnp.dot(n2_ref[...], w1, preferred_element_type=f32) + hb_ref[0]
    gact = jnp.dot(og_ref[...], w2, preferred_element_type=f32)
    cdf = 0.5 + 0.5 * lax.erf(pre * (2.0**-0.5))
    pdf = jnp.exp(pre * pre * -0.5) * ((2.0 * math.pi) ** -0.5)
    act = (pre * cdf).astype(bf)
    gpre = (gact * (cdf + pre * pdf)).astype(bf)
    act_ref[:, here] = act
    gpre_ref[:, here] = gpre

    @pl.when(j == 0)
    def _():
        loads[2].wait()
        loads[3].wait()

    half = keep_ref.shape[0]
    for at, left, right in ((0, n2t_ref, gpre), (FB, ogt_ref, act)):
        dw = jnp.dot(left[...], right, preferred_element_type=f32).astype(bf)
        keep_ref[:, at : at + FB] = dw[:half]
        send_ref[:, at : at + FB] = dw[half:]
    dhb_ref[0] = jnp.sum(gpre.astype(f32), axis=0, keepdims=True)

    @pl.when(j == pl.num_programs(0) - 1)
    def _():
        mix_ref[...] = dg(act_ref[...], down_ref[...], 1, 1).astype(bf)
        store = pltpu.make_async_copy(mix_ref, mix_far, sem.at[4])
        store.start()
        gn_ref[...] = dg(gpre_ref[...], up_ref[...], 1, 1).astype(bf)
        store.wait()


FB = 256


def ffn(n2, n2t, og, ogt, hb, w):
    slots, model = n2.shape
    hidden = w[0].shape[1] // 2
    blocks = hidden // FB
    far = pl.BlockSpec(memory_space=pl.ANY)
    up = pl.BlockSpec((model // 2, FB), lambda j: (0, j))
    down = pl.BlockSpec((model // 2, FB), lambda j: (0, blocks + j))
    bias = pl.BlockSpec((1, 1, FB), lambda j: (j, 0, 0))
    pair = pl.BlockSpec((model // 2, 2 * FB), lambda j: (0, j))
    return pl.pallas_call(
        feed_forward,
        grid=(hidden // FB,),
        out_shape=(
            shape((slots, model), bf),
            shape((slots, model), bf),
            shape((model // 2, 2 * hidden), bf),
            shape((model // 2, 2 * hidden), bf),
            shape((hidden // FB, 1, FB), f32),
        ),
        in_specs=[far] * 4 + [bias, up, up, down, down],
        out_specs=(far, VM, pair, pair, bias),
        scratch_shapes=[pltpu.VMEM((model, hidden), bf)] * 2
        + [pltpu.VMEM((slots, hidden), bf)] * 2
        + [pltpu.VMEM((slots, model), bf)] * 2
        + [pltpu.VMEM((model, slots), bf)] * 2
        + [pltpu.VMEM((slots, model), bf), pltpu.SemaphoreType.DMA((5,))],
        compiler_params=params(),
        cost_estimate=cost(10, 10),
        name="feed_forward",
    )(n2, n2t, og, ogt, hb, *w, *w)


def second_norm_backward(
    ma_ref, mb_ref, ga_ref, gb_ref, res_ref, og_ref, nv_ref, perm_ref, aan_ref, aaf_ref, abn_ref, abf_ref, oa_ref, ob_ref,
    out_ref, gres_ref, gt_ref, dota_ref, dotb_ref, dela_ref, delb_ref, vec_ref, wot_ref,
):
    res, og = res_ref[...], og_ref[...].astype(f32)
    out = (res + (ma_ref[...].astype(f32) + mb_ref[...].astype(f32)) + nv_ref[5:6]).astype(bf)
    out_ref[...] = dg(out, perm_ref[...], 1, 1).astype(bf)
    xhat, scale = normalize(res)
    gn = ga_ref[...].astype(f32) + gb_ref[...].astype(f32)
    gres = og + norm_backward(gn, nv_ref[3:4], xhat, scale)
    gres_ref[...] = gres.astype(bf)
    width = oa_ref.shape[0]

    @pl.when(pl.program_id(0) == 0)
    def _():
        for at, near, far in ((0, aan_ref, aaf_ref), (1, abn_ref, abf_ref)):
            both = jnp.concatenate([near[:, width:], far[:, width:]], axis=0)
            wot_ref[at] = jnp.transpose(both)

    low = jnp.transpose(gres.astype(bf))
    gt_ref[...] = low
    for at, o_ref, dot_ref, del_ref in (
        (0, oa_ref, dota_ref, dela_ref),
        (1, ob_ref, dotb_ref, delb_ref),
    ):
        dot = jnp.dot(wot_ref[at], low, preferred_element_type=f32).astype(bf)
        dot_ref[...] = dot
        prod = dot.astype(f32) * o_ref[...].astype(f32)
        for h in range(prod.shape[0] // HD):
            del_ref[h : h + 1, :] = jnp.sum(prod[HD * h : HD * h + HD], axis=0, keepdims=True)
    column_sums(vec_ref, [gres, gn * xhat, gn, og], res.shape[1])


def middle_back(ma, mb, ga, gb, res, og, nv, perm, aa, ab, oa, ob):
    slots, model = res.shape
    width = oa.shape[0]
    tok, lane = token_block(model), lane_block(width)
    return pl.pallas_call(
        second_norm_backward,
        grid=(slots // TB,),
        out_shape=(
            shape((slots, model), bf),
            shape((slots, model), bf),
            shape((model, slots), bf),
            shape((width, slots), bf),
            shape((width, slots), bf),
            shape((16, slots), f32),
            shape((16, slots), f32),
            shape((8, model), f32),
        ),
        in_specs=[tok] * 6 + [VM] * 2 + [late_columns(aa)] * 4 + [lane] * 2,
        out_specs=(tok, tok, lane_block(model), lane, lane, lane_block(16), lane_block(16), VM),
        scratch_shapes=[pltpu.VMEM((2, width, model), bf)],
        compiler_params=params(),
        cost_estimate=cost(2, 10),
        name="second_norm_backward",
    )(ma, mb, ga, gb, res, og, nv, perm, *aa, *ab, oa, ob)


def first_norm_backward(aan_ref, aaf_ref, abn_ref, abf_ref, gres_ref, x_ref, nv_ref, perm_ref, *refs):
    *parts, out_ref, vec_ref = refs
    half = len(parts) // 2
    rows = [
        jnp.concatenate([part[c] for c in range(3) for part in mine], axis=0)
        for mine in (parts[:half], parts[half:])
    ]
    wide = rows[0].shape[0]
    planes = [
        jnp.dot(a_ref[:, :wide], rows[0], preferred_element_type=f32)
        + jnp.dot(b_ref[:, :wide], rows[1], preferred_element_type=f32)
        for a_ref, b_ref in ((aan_ref, abn_ref), (aaf_ref, abf_ref))
    ]
    gn = jnp.transpose(jnp.concatenate(planes, axis=0))
    xhat, scale = normalize(x_ref[...].astype(f32))
    gres = gres_ref[...].astype(f32)
    out = (gres + norm_backward(gn, nv_ref[0:1], xhat, scale)).astype(bf)
    out_ref[...] = dg(out, perm_ref[...], 1, 1).astype(bf)
    column_sums(vec_ref, [gn * xhat, gn], gn.shape[1])


def tail(aa, ab, gres, x, nv, perm, parts):
    slots, model = x.shape
    tok = token_block(model)
    blocks = [pl.BlockSpec((3, part.shape[1], TB), lambda j: (0, 0, j)) for part in parts]
    return pl.pallas_call(
        first_norm_backward,
        grid=(slots // TB,),
        out_shape=(shape((slots, model), bf), shape((8, model), f32)),
        in_specs=[VM] * 4 + [tok] * 2 + [VM] * 2 + blocks,
        out_specs=(tok, VM),
        compiler_params=params(),
        cost_estimate=cost(2, 10),
        name="first_norm_backward",
    )(*aa, *ab, gres, x, nv, perm, *parts)


def tables(seg):
    slots = seg.shape[0]
    ids = jnp.arange(8, dtype=jnp.int32)
    starts = jnp.sum((seg[None, :] < ids[:, None]).astype(jnp.int32), axis=1)
    ends = jnp.sum((seg[None, :] <= ids[:, None]).astype(jnp.int32), axis=1)
    member = seg[None, :] == ids[:, None]
    before = jnp.sum(jnp.where(member, starts[:, None], 0), axis=0)
    after = jnp.sum(jnp.where(member, ends[:, None], 0), axis=0)
    position = (jnp.arange(slots, dtype=jnp.int32) - before).astype(f32)
    frequency = 10000.0 ** (-jnp.arange(0, HD, 2).astype(f32) / HD)
    angles = frequency[:, None] * position[None, :]
    fq = jnp.concatenate([jnp.where(member, 0.0, -BIG), jnp.zeros((56, slots))], axis=0).astype(bf)
    past = jnp.broadcast_to(ids[:, None] == 7, (8, SPARE))
    fk = jnp.concatenate([member, past], axis=1).astype(bf)
    fk = jnp.concatenate([fk, jnp.zeros((56, slots + SPARE), bf)], axis=0)
    lo = before[::QT] // STRIDE
    count = (after[QT - 1 :: QT] - lo * STRIDE + KC - 1) // KC
    return jnp.cos(angles), jnp.sin(angles), fq, fk, jnp.stack([lo, count])


def moments(weight, grad, first, second):
    first = BETA_ONE * first + (1.0 - BETA_ONE) * grad
    second = BETA_TWO * second + (1.0 - BETA_TWO) * grad * grad
    corrected = first / (1.0 - BETA_ONE**STEP)
    variance = second / (1.0 - BETA_TWO**STEP)
    return first, second, corrected / (jnp.sqrt(variance) + EPS_ADAM) + DECAY * weight


class Squares:
    def __init__(self):
        self.lane = lax.broadcasted_iota(jnp.int32, (8, 128), 1)
        self.row = lax.broadcasted_iota(jnp.int32, (8, 128), 0)
        self.total = jnp.zeros((8, 128), f32)

    def add(self, group, weight, update, share=1.0):
        for row, value in ((0, weight), (1, update)):
            square = jnp.sum(value * value, axis=(0, 1), keepdims=True) * share
            self.total = self.total + jnp.where(
                (self.lane == group) & (self.row == row), square, 0.0
            )


def all_parts(parts_ref, width):
    total = parts_ref[0, :, :width].astype(f32)
    for i in range(1, parts_ref.shape[0]):
        total = total + parts_ref[i, :, :width].astype(f32)
    return total


def lamb_ffn(parts_ref, peer_ref, w_ref, m_ref, v_ref, m_out, v_out, u_out, sq_out):
    grad = all_parts(parts_ref, peer_ref.shape[1]) + peer_ref[...].astype(f32)
    blocks = w_ref.shape[2] // FB
    squares = Squares()
    for c in range(2):
        pieces = [grad[:, (2 * j + c) * FB : (2 * j + c + 1) * FB] for j in range(blocks)]
        first, second, update = moments(
            w_ref[c], jnp.concatenate(pieces, axis=1), m_ref[c], v_ref[c]
        )
        m_out[c], v_out[c], u_out[c] = first, second, update
        squares.add(4 + c, w_ref[c], update)
    sq_out[...] = squares.total


def step_ffn(parts, peer, w, m, v):
    return pl.pallas_call(
        lamb_ffn,
        out_shape=(shape(w.shape, f32),) * 3 + (shape((8, 128), f32),),
        in_specs=[VM] * 5,
        out_specs=(VM,) * 4,
        compiler_params=params(),
        cost_estimate=cost(1, 5),
        name="lamb_ffn",
    )(parts, peer, w, m, v)


def lamb_rest(
    shares, mine_ref, parts_ref, small_ref, sq_ref,
    w_ref, m_ref, v_ref, hw_ref, hm_ref, hv_ref, bw_ref, bm_ref, bv_ref, nw_ref, nm_ref, nv_ref,
    m_out, v_out, vo_out, u_out, hm_out, hv_out, hu_out, bm_out, bv_out, bu_out,
    nm_out, nv_out, nvo_out, nu_out, sq_out,
):
    grad = all_parts(parts_ref, parts_ref.shape[2])
    width = w_ref.shape[2]
    squares = Squares()
    for c in range(4):
        first, second, update = moments(
            w_ref[c], grad[:, c * width : c * width + width], m_ref[c], v_ref[c]
        )
        m_out[c], u_out[c] = first, update
        if c < 3:
            v_out[c] = second
        else:
            vo_out[...] = second
        squares.add(c, w_ref[c], update)
    lower = mine_ref[0] == 0
    small = small_ref[...]
    grad = jnp.where(lower, small[0:3, :width], small[0:3, width:])
    hm_out[...], hv_out[...], hu_out[...] = moments(hw_ref[...], grad, hm_ref[...], hv_ref[...])
    grad = jnp.where(lower, small[9:11], small[11:13])
    bm_out[...], bv_out[...], bu_out[...] = moments(bw_ref[...], grad, bm_ref[...], bv_ref[...])
    first, second, update = moments(nw_ref[...], small[3:9], nm_ref[...], nv_ref[...])
    nm_out[...], nu_out[...] = first, update
    nvo_out[...], nv_out[...] = second[:2], second[2:]
    for c in range(3):
        squares.add(6 + c, hw_ref[c : c + 1], hu_out[c : c + 1], shares[0])
    squares.add(9, bw_ref[...], bu_out[...], shares[0])
    for c in range(6):
        squares.add(10 + c, nw_ref[c : c + 1], update[c : c + 1], shares[1])
    sq_out[...] = squares.total + sq_ref[...]


def step_rest(shares, mine, parts, small, sq, attn, head, hidden, vector):
    w, h, b, n = attn[0], head[0], hidden[0], vector[0]
    return pl.pallas_call(
        partial(lamb_rest, shares),
        out_shape=tuple(
            shape(dims, f32)
            for dims in (
                w.shape, (3,) + w.shape[1:], w.shape[1:], w.shape,
                h.shape, h.shape, h.shape, b.shape, b.shape, b.shape,
                n.shape, (4, n.shape[1]), (2, n.shape[1]), n.shape, (8, 128),
            )
        ),
        in_specs=[SM] + [VM] * 15,
        out_specs=(VM,) * 15,
        compiler_params=params(),
        cost_estimate=cost(1, 5),
        name="lamb_rest",
    )(mine, parts, small, sq, *attn, *head, *hidden, *vector)


def apply_updates(sums_ref, *refs):
    weights, updates, outs, norms_out = refs[:5], refs[5:10], refs[10:15], refs[15]
    total = sums_ref[0]
    for i in range(1, sums_ref.shape[0]):
        total = total + sums_ref[i]
    norms = jnp.sqrt(total)
    norms_out[...] = norms[:2, :16]
    ratio = norms[0:1] / norms[1:2]
    lane = lax.broadcasted_iota(jnp.int32, (1, 128), 1)

    def rate(group):
        picked = jnp.where(lane == group, ratio, 0.0)
        return RATE * jnp.sum(picked, axis=1, keepdims=True)

    at = 0
    for count, w, u, out in zip((4, 2, 3, 1, 6), weights, updates, outs):
        for c in range(count):
            where = c if len(w.shape) == 3 else slice(None) if count == 1 else slice(c, c + 1)
            out[where] = w[where] - rate(at + c) * u[where]
        at += count


def new_weights(sums, weights, updates):
    return pl.pallas_call(
        apply_updates,
        out_shape=tuple(shape(w.shape, f32) for w in weights) + (shape((2, 16), f32),),
        in_specs=[VM] * 11,
        out_specs=(VM,) * 6,
        compiler_params=params(),
        cost_estimate=cost(1, 5),
        name="new_weights",
    )(sums, *weights, *updates)


def swap(value, axis_name, offset):
    count = lax.axis_size(axis_name)
    return lax.ppermute(value, axis_name, [(i, i ^ offset) for i in range(count)])


def planes():
    count = lax.axis_size("dp")
    return [[2 * u + core for u in range(count // 2)] for core in range(2)]


def exchange(blocks):
    return lax.all_to_all(blocks, "dp", 0, 0, axis_index_groups=planes())


def row_order(model, count):
    block = model // count
    place = np.arange(model) // block
    other = jnp.asarray(place // (count // 2), jnp.int32)
    owner = jnp.asarray(2 * (place % (count // 2)), jnp.int32) + (lax.axis_index("dp") % 2 ^ other)
    feature = owner * block + jnp.asarray(np.arange(model) % block, jnp.int32)
    return jnp.arange(model, dtype=jnp.int32)[:, None] == feature[None, :]


class Gather:
    def __init__(self, value, steps=("plane", "core")):
        self.value, self.steps, self.flying = value, list(steps), []

    def peer(self):
        return Gather(self.value, ("tp", "core"))

    def launch(self):
        step = self.steps[0]
        if step == "plane":
            count = lax.axis_size("dp") // 2
            spread = jnp.broadcast_to(self.value[None], (count,) + self.value.shape)
            self.flying = [exchange(spread)]
        else:
            self.flying = [swap(self.value, "dp" if step == "core" else "tp", 1)]

    def finish(self):
        step = self.steps.pop(0)
        if step == "core":
            self.value = (self.value, self.flying[0])
        else:
            self.value = self.flying[0].reshape(-1, self.flying[0].shape[-1])
        self.flying = []


def far_exchange(blocks):
    count = lax.axis_size("dp") // 4
    groups = [[4 * z + low for z in range(count)] for low in range(4)]
    return lax.all_to_all(blocks, "dp", 0, 0, axis_index_groups=groups)


class Scatter:
    def __init__(self, keep, send):
        self.parts, self.send = [keep], send
        self.steps, self.flying = ["core", "pair", "tp", "far"], []

    def side(self, other):
        at = (lax.axis_index("dp") >> 1) % 2 ^ other
        count = lax.axis_size("dp") // 4
        total = 0.0
        for part in self.parts:
            blocks = part.reshape(count, 2, -1, part.shape[-1])
            total = total + lax.dynamic_index_in_dim(blocks, at, 1, False).astype(f32)
        return total

    def launch(self):
        step = self.steps[0]
        if step == "pair":
            self.send = self.side(1).astype(bf)
        if step == "far":
            self.flying = [far_exchange(self.value)]
        elif step == "tp":
            self.flying = [swap(self.value, "tp", 1)]
        else:
            self.flying = [swap(self.send, "dp", 1 if step == "core" else 2)]

    def finish(self):
        step = self.steps.pop(0)
        if step == "core":
            self.parts = self.parts + self.flying
        elif step == "pair":
            self.value = (self.side(0) + self.flying[0].astype(f32)).astype(bf)
        else:
            self.value = self.flying[0]
        self.flying = []

    def merge(self, peer):
        self.value = (self.value.astype(f32) + peer.value.astype(f32)).astype(bf)
        self.steps = ["far"]


class Pool:
    def __init__(self, own, peer):
        self.width = own.value.shape[-1]
        self.value = jnp.concatenate([own.value, peer.value], axis=-1)
        self.steps, self.flying = ["far", "tp"], []

    def launch(self):
        if self.steps[0] == "far":
            self.flying = [far_exchange(self.value)]
        else:
            peer = self.value[..., self.width :].astype(f32)
            self.flying = [swap(jnp.sum(peer, axis=0).astype(bf), "tp", 1)]

    def finish(self):
        if self.steps.pop(0) == "far":
            self.value = self.flying[0]
        else:
            self.peer = self.flying[0]
        self.flying = []


def tie(value, *others):
    return lax.optimization_barrier((value, *others))[0]


def meet(value, *movers):
    out = lax.optimization_barrier((value, *[a for mover in movers for a in mover.flying]))
    at = 1
    for mover in movers:
        count = len(mover.flying)
        mover.flying = list(out[at : at + count])
        at += count
        mover.finish()
    return out[0]


def sum_over_dp(value):
    step = 1
    while step < lax.axis_size("dp"):
        value = value + swap(value, "dp", step)
        step *= 2
    return value


def by_peer(own, peer, axis):
    first = lax.axis_index("tp") == 0
    return jnp.where(
        first, jnp.concatenate([own, peer], axis), jnp.concatenate([peer, own], axis)
    )


def on_device(
    inputs, out_grad, segment_ids, attn_weights, ffn_weights, head_bias, hidden_bias, norm_vectors,
    attn_first, ffn_first, head_first, hidden_first, vector_first,
    attn_second, ffn_second, head_second, hidden_second, vector_second,
):
    dp_count, tp_count = lax.axis_size("dp"), lax.axis_size("tp")
    mine = lax.axis_index("tp")
    rows, slots = segment_ids.shape
    assert rows == tp_count == 2
    shard, head_width = attn_weights.shape[1:]
    hidden = ffn_weights.shape[2]
    model = inputs.shape[1]

    a_own = Gather(jnp.concatenate(list(attn_weights.astype(bf)), axis=1))
    a_own.launch()
    x = lax.dynamic_slice_in_dim(inputs, mine * slots, slots, 0)
    order = row_order(model, dp_count)
    perm = order.astype(bf)
    exact = partial(jnp.dot, precision=lax.Precision.HIGHEST, preferred_element_type=f32)
    nv = exact(jnp.concatenate([norm_vectors, jnp.zeros((2, model), f32)], 0), order.astype(f32))
    xt = dg(perm, x, 0, 1)
    centered = xt - jnp.mean(xt, axis=0, keepdims=True)
    scale = lax.rsqrt(jnp.mean(centered * centered, axis=0, keepdims=True) + EPS_NORM)
    n1t = (centered * scale * nv[0][:, None] + nv[1][:, None]).astype(bf)
    bias_own = jnp.concatenate([head_bias.reshape(-1), hidden_bias])
    bias_peer = swap(bias_own.reshape(-1, head_width), "tp", 1).reshape(-1)

    head_columns = jnp.concatenate(
        [bias[: 3 * head_width].reshape(3, head_width) for bias in (bias_own, bias_peer)]
        + [jnp.zeros((2, head_width), f32)],
        0,
    ).T

    def hidden_blocks(bias):
        return bias[3 * head_width :].reshape(-1, 1, FB)

    both = jnp.concatenate(list(ffn_weights.astype(bf)), axis=1)
    og = lax.dynamic_slice_in_dim(out_grad, mine * slots, slots, 0)
    seg = lax.dynamic_index_in_dim(segment_ids, mine, 0, keepdims=False)
    cos, sin, fq, fk, rng = tables(seg)
    x = dg(x, perm, 1, 0).astype(bf)
    ogt = dg(perm, og, 0, 1).astype(bf)
    og = dg(og, perm, 1, 0).astype(bf)
    n1t, cos, sin, fq, fk, rng, x, ogt, og, both, head_columns = lax.optimization_barrier(
        (n1t, cos, sin, fq, fk, rng, x, ogt, og, both, head_columns)
    )
    n1t = meet(n1t, a_own)
    a_peer = a_own.peer()
    w_own = Gather(tie(both, a_own.value))
    a_own.launch()
    a_peer.launch()
    w_own.launch()

    n1t = meet(n1t, a_own)
    a_one = a_own.value
    saved_own, o_own, lse_own = attn_fwd(0, rng, n1t, a_one, head_columns, cos, sin, fq, fk)
    o_own = meet(o_own, a_peer)
    a_peer.launch()
    again = meet(tie(n1t, o_own), a_peer)
    a_two = a_peer.value
    saved_peer, o_peer, lse_peer = attn_fwd(
        3, rng, again, a_two, head_columns, cos, sin, fq, fk
    )
    o_peer = meet(o_peer, w_own)
    w_peer = w_own.peer()
    w_own.launch()
    w_peer.launch()
    res, n2, n2t = middle(o_own, o_peer, a_one, a_two, x, nv)

    n2 = meet(n2, w_own)
    mix_own, gn_own, keep, send, dhb_own = ffn(n2, n2t, og, ogt, hidden_blocks(bias_own), w_own.value)
    f_own = Scatter(keep, send)
    f_own.launch()
    again = meet(tie(n2, mix_own), w_peer)
    w_peer.launch()
    again = meet(again, w_peer)
    mix_peer, gn_peer, keep, send, dhb_peer = ffn(
        again, n2t, og, ogt, hidden_blocks(bias_peer), w_peer.value
    )
    f_peer = Scatter(keep, send)
    mix_peer = meet(mix_peer, f_own)
    f_own.launch()
    f_peer.launch()
    out_low, gres, gt, dot_own, dot_peer, delta_own, delta_peer, sums_two = middle_back(
        mix_own, mix_peer, gn_own, gn_peer, res, og, nv, perm, a_one, a_two, o_own, o_peer
    )

    out_far = swap(out_low, "tp", 1)

    def back(dot, saved, lse, delta, heads):
        return attn_bwd(rng, dot, saved[0], lse, delta, cos, sin, fq, n1t, gt, heads)

    dot_peer = meet(dot_peer, f_peer)
    f_peer.launch()
    keep, send, dbias_peer, dt_peer = back(dot_peer, saved_peer, lse_peer, delta_peer, o_peer)
    g_peer = Scatter(keep, send)
    dot_own, out_far, dt_peer = lax.optimization_barrier((dot_own, out_far, dt_peer))
    dot_own = meet(dot_own, f_own, f_peer)
    f_pool = Pool(f_own, f_peer)
    f_pool.launch()
    g_peer.launch()
    keep, send, dbias_own, dt_own = back(dot_own, saved_own, lse_own, delta_own, o_own)
    g_own = Scatter(keep, send)
    dt_own, gres = lax.optimization_barrier((dt_own, gres))
    gres = meet(gres, g_peer, f_pool)
    g_own.launch()
    g_peer.launch()
    f_pool.launch()
    gres = meet(gres, f_pool, g_own, g_peer)
    g_own.launch()
    g_peer.launch()
    in_low, sums_one = tail(a_one, a_two, gres, x, nv, perm, [dt_own, dt_peer])
    in_low = meet(in_low, g_own, g_peer)
    g_own.merge(g_peer)
    g_own.launch()
    sums = exact(jnp.concatenate([sums_one[:2], sums_two[:4]], 0), order.astype(f32).T)
    small = jnp.concatenate(
        [
            by_peer(dbias_own[:, :3].T, dbias_peer[:, :3].T, 1),
            sums,
            by_peer(dhb_own.reshape(-1), dhb_peer.reshape(-1), 0).reshape(-1, model),
        ],
        0,
    )
    small_far = swap(small, "tp", 1)
    in_low, small_far = lax.optimization_barrier((in_low, small_far))
    small = small + small_far
    in_far = swap(in_low, "tp", 1)
    g_own.finish()

    def place(low, far):
        whole = jnp.zeros((2 * slots, model), bf)
        whole = lax.dynamic_update_slice_in_dim(whole, low, mine * slots, 0)
        return lax.dynamic_update_slice_in_dim(whole, far, (1 - mine) * slots, 0)

    layer_output = place(out_low, tie(out_far, in_low))
    input_grad = place(in_low, in_far)
    small = sum_over_dp(small)
    ffn_first_new, ffn_second_new, ffn_update, squares = step_ffn(
        f_pool.value, f_pool.peer, ffn_weights, ffn_first, ffn_second
    )
    wide = lambda v: v.reshape(2, -1)
    shares = (1.0 / dp_count, 1.0 / (dp_count * tp_count))
    (
        attn_first_new, attn_second_new, out_second_new, attn_update,
        head_first_new, head_second_new, head_update,
        hidden_first_new, hidden_second_new, hidden_update,
        vector_first_new, vector_second_new, norm_second_new, vector_update, squares,
    ) = step_rest(
        shares, mine.reshape(1), g_own.value, small, squares,
        (attn_weights, attn_first, attn_second),
        (head_bias, head_first, head_second),
        (wide(hidden_bias), wide(hidden_first), wide(hidden_second)),
        (norm_vectors, vector_first, vector_second),
    )
    copies = dp_count * tp_count
    sums = lax.all_to_all(
        jnp.broadcast_to(squares[None], (copies, 8, 128)), ("dp", "tp"), 0, 0
    )
    sums, input_grad, layer_output = lax.optimization_barrier((sums, input_grad, layer_output))
    new_attn, new_ffn, new_head, new_hidden, new_vectors, norms = new_weights(
        sums,
        (attn_weights, ffn_weights, head_bias, wide(hidden_bias), norm_vectors),
        (attn_update, ffn_update, head_update, hidden_update, vector_update),
    )
    return (
        layer_output,
        input_grad,
        new_attn,
        new_ffn,
        new_head,
        new_hidden.reshape(-1),
        new_vectors,
        attn_first_new,
        ffn_first_new,
        head_first_new,
        hidden_first_new.reshape(-1),
        vector_first_new,
        attn_second_new,
        out_second_new,
        ffn_second_new,
        head_second_new,
        hidden_second_new.reshape(-1),
        vector_second_new,
        norm_second_new,
        norms,
    )


def solution(mesh):
    in_specs = (
        P("dp", None),
        P("dp", None),
        P("dp", None),
        P(None, "dp", "tp"),
        P(None, "dp", "tp"),
        P(None, "tp"),
        P("tp"),
        P(),
        P(None, "dp", "tp"),
        P(None, "dp", "tp"),
        P(None, "tp"),
        P("tp"),
        P(),
        P(None, "dp", "tp"),
        P(None, "dp", "tp"),
        P(None, "tp"),
        P("tp"),
        P(),
    )
    out_specs = (
        P("dp", None),
        P("dp", None),
        P(None, "dp", "tp"),
        P(None, "dp", "tp"),
        P(None, "tp"),
        P("tp"),
        P(),
        P(None, "dp", "tp"),
        P(None, "dp", "tp"),
        P(None, "tp"),
        P("tp"),
        P(),
        P(None, "dp", "tp"),
        P("dp", "tp"),
        P(None, "dp", "tp"),
        P(None, "tp"),
        P("tp"),
        P(),
        P(),
        P(),
    )
    return jax.shard_map(
        on_device, mesh=mesh, in_specs=in_specs, out_specs=out_specs, check_vma=False
    )
```

```python
import math
from functools import partial

import jax
import jax.numpy as jnp
import numpy as np
from jax import lax
from jax.experimental import pallas as pl
from jax.experimental.pallas import tpu as pltpu
from jax.sharding import PartitionSpec as P

STEP = 10
EPS_NORM = 1e-05
EPS_ADAM = 1e-06
BETA_ONE = 0.9
BETA_TWO = 0.999
DECAY = 0.01
RATE = 0.5

HD = 32
QT = 128
KC = 256
BIG = 1e30
STRIDE = 64
SPARE = 256
LN2 = math.log(2.0)
QSCALE = math.log2(math.e) / math.sqrt(HD)
bf = jnp.bfloat16
f32 = jnp.float32
VM = pl.BlockSpec(memory_space=pltpu.VMEM)
SM = pl.BlockSpec(memory_space=pltpu.SMEM)


def dg(a, b, ca, cb):
    return lax.dot_general(a, b, (((ca,), (cb,)), ((), ())), preferred_element_type=f32)


def shape(dims, kind):
    return jax.ShapeDtypeStruct(dims, kind)


def cost(gflop, mbytes):
    return pl.CostEstimate(
        flops=int(gflop * 1e9), bytes_accessed=int(mbytes * 1e6), transcendentals=0
    )


def params(mbytes=56):
    return pltpu.CompilerParams(vmem_limit_bytes=mbytes * 1024 * 1024)


def rope_rows(y, cos, sin, sign):
    out = []
    for h in range(y.shape[0] // HD):
        top = y[HD * h : HD * h + HD // 2]
        bot = y[HD * h + HD // 2 : HD * h + HD]
        out.append(top * cos - sign * bot * sin)
        out.append(bot * cos + sign * top * sin)
    return jnp.concatenate(out, axis=0)


def two_heads(block, extra):
    zero = jnp.zeros((HD, QT), bf)
    left = jnp.concatenate([block[:HD], zero] + extra, axis=0)
    right = jnp.concatenate([zero, block[HD:]] + extra, axis=0)
    return jnp.concatenate([left, right], axis=1)


def attention_forward(col, rng_ref, n1t_ref, an_ref, af_ref, b_ref, cos_ref, sin_ref, fq_ref, fk_ref, *refs):
    count = len(PARTS)
    outs = refs[: 4 * count]
    ot_ref, lse_ref, vt_ref, qbd_ref, s_ref, *held, sem = refs[4 * count :]
    qts, kts, kps, vns = (held[count * i : count * i + count] for i in range(4))
    width = ot_ref.shape[0]
    heads = width // HD
    groups = heads // 2
    slots = n1t_ref.shape[1]
    pad = kts[0].shape[1] - slots
    cos, sin = cos_ref[...], sin_ref[...]
    a = jnp.concatenate([an_ref[:, : 3 * width], af_ref[:, : 3 * width]], axis=0)
    y = dg(a, n1t_ref[...], 0, 0)
    qb = (rope_rows(y[:width] + b_ref[:, col : col + 1], cos, sin, 1.0) * QSCALE).astype(bf)
    kb = rope_rows(y[width : 2 * width] + b_ref[:, col + 1 : col + 2], cos, sin, 1.0).astype(bf)
    vb = (y[2 * width :] + b_ref[:, col + 2 : col + 3]).astype(bf)
    ones = jnp.ones((16, slots + pad), bf)
    for odd, moved in enumerate((vb, vb[:, STRIDE:])):
        moved = jnp.concatenate(
            [moved, jnp.zeros((width, slots + pad - moved.shape[1]), bf)], axis=1
        )
        for h in range(heads):
            top = 48 * (h % 2)
            vt_ref[odd, h // 2, top : top + HD, :] = moved[HD * h : HD * h + HD]
            vt_ref[odd, h // 2, top + HD : top + 48, :] = ones
    past = jnp.transpose(jnp.concatenate([jnp.zeros((64, pad), bf), fk_ref[:, slots:]], axis=0))
    for (first, last), qt_ref, kt_ref, kp_ref, vn_ref in zip(PARTS, qts, kts, kps, vns):
        qt_ref[...] = qb[64 * first : 64 * last]
        kt_ref[:, :slots] = kb[64 * first : 64 * last]
        kt_ref[:, slots:] = jnp.zeros((64 * (last - first), pad), bf)
        for g in range(first, last):
            rows = slice(64 * g, 64 * g + 64)
            both = jnp.concatenate([kb[rows], fk_ref[:, :slots]], axis=0)
            kp_ref[g - first, :slots, :] = jnp.transpose(both)
            kp_ref[g - first, slots:, :] = past
            both = jnp.concatenate([vb[rows], jnp.zeros((64, slots), bf)], axis=0)
            vn_ref[g - first, :slots, :] = jnp.transpose(both)
            vn_ref[g - first, slots:, :] = jnp.zeros((pad, 128), bf)
    saving = [
        pltpu.make_async_copy(src, dst, sem.at[i]) for i, (src, dst) in enumerate(zip(held, outs))
    ]
    for copy in saving:
        copy.start()
    where = [(p, g - first) for p, (first, last) in enumerate(PARTS) for g in range(first, last)]

    def tile(i, _):
        q0 = pl.multiple_of(i * QT, QT)
        lo, count = rng_ref[0, i], rng_ref[1, i]
        fq = fq_ref[:, pl.ds(q0, QT)]
        for g in range(groups):
            p, r = where[g]
            qbd_ref[g] = two_heads(qts[p][64 * r : 64 * r + 64, pl.ds(q0, QT)], [fq])

        def scores(j, tops):
            k0 = pl.multiple_of(lo * STRIDE + j * KC, STRIDE)
            at = pl.multiple_of(j * KC, KC)
            out = []
            for g in range(groups):
                p, r = where[g]
                keys = kps[p][r, pl.ds(k0, KC), :]
                s = jnp.dot(keys, qbd_ref[g], preferred_element_type=f32)
                s_ref[g, pl.ds(at, KC), :] = s
                top = tops[g]
                for r in range(KC // 8):
                    top = jnp.maximum(top, s[8 * r : 8 * r + 8])
                out.append(top)
            return tuple(out)

        start = tuple(jnp.full((8, 2 * QT), -3e38, f32) for _ in range(groups))
        tops = lax.fori_loop(0, count, scores, start)
        tops = [jnp.max(top, axis=0, keepdims=True) for top in tops]

        def mix(j, sums):
            k0 = pl.multiple_of((lo >> 1) * 128 + j * KC, 128)
            at = pl.multiple_of(j * KC, KC)
            out = []
            for g in range(groups):
                p = jnp.exp2(s_ref[g, pl.ds(at, KC), :] - tops[g]).astype(bf)
                values = vt_ref[lo & 1, g, :, pl.ds(k0, KC)]
                part = jnp.dot(values, p, preferred_element_type=f32)
                out.append(sums[2 * g] + part[:48, :QT])
                out.append(sums[2 * g + 1] + part[48:, QT:])
            return tuple(out)

        start = tuple(jnp.zeros((48, QT), f32) for _ in range(heads))
        sums = lax.fori_loop(0, count, mix, start)
        for h in range(heads):
            total = sums[h][HD : HD + 1]
            ot_ref[HD * h : HD * h + HD, pl.ds(q0, QT)] = (sums[h][:HD] / total).astype(bf)
            col = QT * (h % 2)
            lse_ref[h : h + 1, pl.ds(q0, QT)] = tops[h // 2][:, col : col + QT] + jnp.log2(total)
        return 0

    lax.fori_loop(0, slots // QT, tile, 0)
    for copy in saving:
        copy.wait()


PARTS = ((0, 5),)


def attn_fwd(col, rng, n1t, a, b, cos, sin, fq, fk):
    slots, width = n1t.shape[1], b.shape[0]
    heads, groups, longer = width // HD, width // 64, slots + SPARE
    assert groups == PARTS[-1][1]
    sizes = [last - first for first, last in PARTS]
    held = (
        [(64 * n, slots) for n in sizes]
        + [(64 * n, longer) for n in sizes]
        + [(n, longer, 128) for n in sizes] * 2
    )
    out = pl.pallas_call(
        partial(attention_forward, col),
        out_shape=tuple(
            [shape(dims, bf) for dims in held] + [shape((width, slots), bf), shape((16, slots), f32)]
        ),
        in_specs=[SM] + [VM] * 8,
        out_specs=(pl.BlockSpec(memory_space=pl.ANY),) * len(held) + (VM, VM),
        scratch_shapes=[
            pltpu.VMEM((2, groups, 96, longer), bf),
            pltpu.VMEM((groups, 128, 2 * QT), bf),
            pltpu.VMEM((groups, longer, 2 * QT), f32),
        ]
        + [pltpu.VMEM(dims, bf) for dims in held]
        + [pltpu.SemaphoreType.DMA((len(held),))],
        compiler_params=params(),
        cost_estimate=cost(12, 10),
        name="attention_forward",
    )(rng, n1t, *a, b, cos, sin, fq, fk)
    count = len(sizes)
    saved = [tuple(out[count * i + p] for i in range(4)) for p in range(count)]
    return saved, out[4 * count], out[4 * count + 1]


def attention_backward(
    first, rng_ref, dot_ref, qt_ref, kt_ref, kp_ref, vn_ref, lse_ref, delta_ref, cos_ref, sin_ref, fq_ref,
    n1t_far, gt_far, ot_far, keep_ref, send_ref, db_ref, dt_far,
    dqt_ref, dkt_ref, dvt_ref, qbd_ref, dobd_ref, both_ref, n1t_ref, gt_ref, ot_ref, dt_ref, sem,
):
    loads = [
        pltpu.make_async_copy(src, dst, sem.at[i])
        for i, (src, dst) in enumerate(((n1t_far, n1t_ref), (gt_far, gt_ref), (ot_far, ot_ref)))
    ]
    for copy in loads:
        copy.start()
    width, slots = qt_ref.shape
    heads = width // HD
    groups = heads // 2
    base = 64 * first
    dkt_ref[...] = jnp.zeros_like(dkt_ref)
    dvt_ref[...] = jnp.zeros_like(dvt_ref)
    both_ref[0] = kt_ref[...]
    both_ref[1] = jnp.concatenate(
        [kt_ref[:, STRIDE:], jnp.zeros((width, STRIDE), bf)], axis=1
    )
    blank = jnp.zeros((64, QT), bf)

    def tile(i, _):
        q0 = pl.multiple_of(i * QT, QT)
        lo, count = rng_ref[0, i], rng_ref[1, i]
        fq = fq_ref[:, pl.ds(q0, QT)]
        for g in range(groups):
            rows = slice(64 * g, 64 * g + 64)
            qbd_ref[g] = two_heads(qt_ref[rows, pl.ds(q0, QT)], [fq])
            dobd_ref[g] = two_heads(
                dot_ref[base + 64 * g : base + 64 * g + 64, pl.ds(q0, QT)], [blank]
            )

        def pair(ref, g):
            return jnp.concatenate(
                [
                    ref[2 * (first + g) + a : 2 * (first + g) + a + 1, pl.ds(q0, QT)]
                    for a in range(2)
                ],
                axis=1,
            )

        def chunk(j, sums):
            k0 = pl.multiple_of(lo * STRIDE + j * KC, STRIDE)
            kl = pl.multiple_of((lo >> 1) * 128 + j * KC, 128)
            odd = lo & 1
            out = []
            for g in range(groups):
                s = jnp.dot(kp_ref[g, pl.ds(k0, KC), :], qbd_ref[g], preferred_element_type=f32)
                dp = jnp.dot(vn_ref[g, pl.ds(k0, KC), :], dobd_ref[g], preferred_element_type=f32)
                p = jnp.exp2(s - pair(lse_ref, g))
                ds = (p * (dp - pair(delta_ref, g))).astype(bf)
                p = p.astype(bf)
                rows = slice(64 * g, 64 * g + 64)
                dvt_ref[odd, rows, pl.ds(kl, KC)] += dg(dobd_ref[g, :64], p, 1, 1)
                dkt_ref[odd, rows, pl.ds(kl, KC)] += dg(qbd_ref[g, :64], ds, 1, 1)
                dq = jnp.dot(both_ref[odd, rows, pl.ds(kl, KC)], ds, preferred_element_type=f32)
                out.append(sums[2 * g] + dq[:HD, :QT])
                out.append(sums[2 * g + 1] + dq[HD:, QT:])
            return tuple(out)

        start = tuple(jnp.zeros((HD, QT), f32) for _ in range(heads))
        sums = lax.fori_loop(0, count, chunk, start)
        for h in range(heads):
            dqt_ref[HD * h : HD * h + HD, pl.ds(q0, QT)] = sums[h]
        return 0

    lax.fori_loop(0, slots // QT, tile, 0)
    cos, sin = cos_ref[...], sin_ref[...]
    dt_ref[0] = rope_rows(dqt_ref[...] * HD**-0.5, cos, sin, -1.0).astype(bf)

    def joined(ref):
        moved = jnp.concatenate(
            [jnp.zeros((width, STRIDE), f32), ref[1, :, : slots - STRIDE]], axis=1
        )
        return ref[0, :, :slots] + moved

    dt_ref[1] = rope_rows(joined(dkt_ref) * LN2, cos, sin, -1.0).astype(bf)
    dt_ref[2] = joined(dvt_ref).astype(bf)
    store = pltpu.make_async_copy(dt_ref, dt_far, sem.at[3])
    store.start()
    rows = jnp.concatenate([dt_ref[c] for c in range(3)], axis=0)
    for c in range(3):
        db_ref[:, c : c + 1] = jnp.sum(dt_ref[c].astype(f32), axis=1, keepdims=True)
    for copy in loads:
        copy.wait()
    half, wide = keep_ref.shape[0], rows.shape[0]
    for cols, left, right in (
        (slice(0, wide), n1t_ref[...], rows),
        (slice(wide, keep_ref.shape[1]), gt_ref[...], ot_ref[...]),
    ):
        dw = dg(left, right, 1, 1).astype(bf)
        keep_ref[:, cols] = dw[:half]
        send_ref[:, cols] = dw[half:]
    store.wait()


def attn_bwd(rng, dot, saved, lse, delta, cos, sin, fq, n1t, gt, ot):
    first, last = PARTS[0]
    width, slots = saved[0].shape
    model = n1t.shape[0]
    groups, longer = last - first, slots + SPARE
    far = pl.BlockSpec(memory_space=pl.ANY)
    return pl.pallas_call(
        partial(attention_backward, first),
        out_shape=(shape((model // 2, 4 * width), bf),) * 2
        + (shape((width, 8), f32), shape((3, width, slots), bf)),
        in_specs=[SM] + [VM] * 10 + [far] * 3,
        out_specs=(VM, VM, VM, far),
        scratch_shapes=[
            pltpu.VMEM((width, slots), f32),
            pltpu.VMEM((2, width, longer), f32),
            pltpu.VMEM((2, width, longer), f32),
            pltpu.VMEM((groups, 128, 2 * QT), bf),
            pltpu.VMEM((groups, 128, 2 * QT), bf),
            pltpu.VMEM((2, width, longer), bf),
            pltpu.VMEM((model, slots), bf),
            pltpu.VMEM((model, slots), bf),
            pltpu.VMEM((width, slots), bf),
            pltpu.VMEM((3, width, slots), bf),
            pltpu.SemaphoreType.DMA((4,)),
        ],
        compiler_params=params(),
        cost_estimate=cost(4 * groups, 10),
        name="attention_backward",
    )(rng, dot, *saved, lse, delta, cos, sin, fq, n1t, gt, ot)


def normalize(values):
    centered = values - jnp.mean(values, axis=1, keepdims=True)
    scale = lax.rsqrt(jnp.mean(centered * centered, axis=1, keepdims=True) + EPS_NORM)
    return centered * scale, scale


def norm_backward(grad, gain, xhat, scale):
    e = grad * gain
    return scale * (
        e - jnp.mean(e, axis=1, keepdims=True) - xhat * jnp.mean(e * xhat, axis=1, keepdims=True)
    )


def column_sums(ref, parts, width):
    rows = [jnp.sum(part, axis=0, keepdims=True) for part in parts]
    rows.append(jnp.zeros((8 - len(parts), width), f32))
    total = jnp.concatenate(rows, axis=0)

    @pl.when(pl.program_id(0) == 0)
    def _():
        ref[...] = total

    @pl.when(pl.program_id(0) > 0)
    def _():
        ref[...] += total


TB = 512


def own_rows(slots, width):
    return pl.BlockSpec((TB, width), lambda j, mine: (mine[0] * (slots // TB) + j, 0))


def token_block(width):
    return pl.BlockSpec((TB, width), lambda j, *_: (j, 0))


def lane_block(height):
    return pl.BlockSpec((height, TB), lambda j, *_: (0, j))


def late_columns(a):
    return pl.BlockSpec((a[0].shape[0], a[0].shape[1] // 2), lambda j, *_: (0, 1))


def attended_norm(oa_ref, ob_ref, aan_ref, aaf_ref, abn_ref, abf_ref, x_ref, nv_ref, res_ref, n2_ref, n2t_ref):
    width = oa_ref.shape[0]
    planes = [
        jnp.dot(a_ref[:, width:], oa_ref[...], preferred_element_type=f32)
        + jnp.dot(b_ref[:, width:], ob_ref[...], preferred_element_type=f32)
        for a_ref, b_ref in ((aan_ref, abn_ref), (aaf_ref, abf_ref))
    ]
    attended = jnp.transpose(jnp.concatenate(planes, axis=0))
    res = x_ref[...].astype(f32) + attended + nv_ref[2:3]
    res_ref[...] = res
    n2 = (normalize(res)[0] * nv_ref[3:4] + nv_ref[4:5]).astype(bf)
    n2_ref[...] = n2
    n2t_ref[...] = jnp.transpose(n2)


def middle(oa, ob, aa, ab, x, nv):
    slots, model = x.shape
    width = oa.shape[0]
    return pl.pallas_call(
        attended_norm,
        grid=(slots // TB,),
        out_shape=(
            shape((slots, model), f32),
            shape((slots, model), bf),
            shape((model, slots), bf),
        ),
        in_specs=[lane_block(width)] * 2 + [late_columns(aa)] * 4 + [token_block(model), VM],
        out_specs=(token_block(model),) * 2 + (lane_block(model),),
        compiler_params=params(),
        cost_estimate=cost(2, 10),
        name="attended_norm",
    )(oa, ob, *aa, *ab, x, nv)


def gelu_parts(pre):
    z = jnp.abs(pre) * (2.0**-0.5)
    bell = jnp.exp(-z * z)
    t = 1.0 / (1.0 + 0.3275911 * z)
    tail = t * (0.254829592 + t * (-0.284496736 + t * (1.421413741 + t * (-1.453152027 + t * 1.061405429))))
    half = 0.5 * tail * bell
    return jnp.where(pre >= 0.0, 1.0 - half, half), bell * ((2.0 * math.pi) ** -0.5)


def feed_forward(
    n2_far, n2t_far, og_far, ogt_far, hb_ref, w1n_ref, w1f_ref, w2n_ref, w2f_ref,
    mix_far, gn_ref, keep_ref, send_ref, dhb_ref,
    up_ref, down_ref, act_ref, gpre_ref, n2_ref, og_ref, n2t_ref, ogt_ref, mix_ref, sem,
):
    j = pl.program_id(0)
    pairs = ((n2_far, n2_ref), (og_far, og_ref), (n2t_far, n2t_ref), (ogt_far, ogt_ref))
    loads = [pltpu.make_async_copy(src, dst, sem.at[i]) for i, (src, dst) in enumerate(pairs)]

    @pl.when(j == 0)
    def _():
        for copy in loads:
            copy.start()
        loads[0].wait()
        loads[1].wait()

    w1 = jnp.concatenate([w1n_ref[...], w1f_ref[...]], axis=0)
    w2 = jnp.concatenate([w2n_ref[...], w2f_ref[...]], axis=0)
    here = pl.ds(pl.multiple_of(j * FB, FB), FB)
    up_ref[:, here] = w1
    down_ref[:, here] = w2
    pre = jnp.dot(n2_ref[...], w1, preferred_element_type=f32) + hb_ref[0]
    gact = jnp.dot(og_ref[...], w2, preferred_element_type=f32)
    cdf = 0.5 + 0.5 * lax.erf(pre * (2.0**-0.5))
    pdf = jnp.exp(pre * pre * -0.5) * ((2.0 * math.pi) ** -0.5)
    act = (pre * cdf).astype(bf)
    gpre = (gact * (cdf + pre * pdf)).astype(bf)
    act_ref[:, here] = act
    gpre_ref[:, here] = gpre

    @pl.when(j == 0)
    def _():
        loads[2].wait()
        loads[3].wait()

    half = keep_ref.shape[0]
    for at, left, right in ((0, n2t_ref, gpre), (FB, ogt_ref, act)):
        dw = jnp.dot(left[...], right, preferred_element_type=f32).astype(bf)
        keep_ref[:, at : at + FB] = dw[:half]
        send_ref[:, at : at + FB] = dw[half:]
    dhb_ref[0] = jnp.sum(gpre.astype(f32), axis=0, keepdims=True)

    @pl.when(j == pl.num_programs(0) - 1)
    def _():
        mix_ref[...] = dg(act_ref[...], down_ref[...], 1, 1).astype(bf)
        store = pltpu.make_async_copy(mix_ref, mix_far, sem.at[4])
        store.start()
        gn_ref[...] = dg(gpre_ref[...], up_ref[...], 1, 1).astype(bf)
        store.wait()


FB = 256


def ffn(n2, n2t, og, ogt, hb, w):
    slots, model = n2.shape
    hidden = w[0].shape[1] // 2
    blocks = hidden // FB
    far = pl.BlockSpec(memory_space=pl.ANY)
    up = pl.BlockSpec((model // 2, FB), lambda j: (0, j))
    down = pl.BlockSpec((model // 2, FB), lambda j: (0, blocks + j))
    bias = pl.BlockSpec((1, 1, FB), lambda j: (j, 0, 0))
    pair = pl.BlockSpec((model // 2, 2 * FB), lambda j: (0, j))
    return pl.pallas_call(
        feed_forward,
        grid=(hidden // FB,),
        out_shape=(
            shape((slots, model), bf),
            shape((slots, model), bf),
            shape((model // 2, 2 * hidden), bf),
            shape((model // 2, 2 * hidden), bf),
            shape((hidden // FB, 1, FB), f32),
        ),
        in_specs=[far] * 4 + [bias, up, up, down, down],
        out_specs=(far, VM, pair, pair, bias),
        scratch_shapes=[pltpu.VMEM((model, hidden), bf)] * 2
        + [pltpu.VMEM((slots, hidden), bf)] * 2
        + [pltpu.VMEM((slots, model), bf)] * 2
        + [pltpu.VMEM((model, slots), bf)] * 2
        + [pltpu.VMEM((slots, model), bf), pltpu.SemaphoreType.DMA((5,))],
        compiler_params=params(),
        cost_estimate=cost(10, 10),
        name="feed_forward",
    )(n2, n2t, og, ogt, hb, *w, *w)


def second_norm_backward(
    mine_ref, ma_ref, mb_ref, ga_ref, gb_ref, res_ref, og_ref, nv_ref, perm_ref, aan_ref, aaf_ref, abn_ref, abf_ref, oa_ref, ob_ref,
    whole_ref, out_ref, gres_ref, gt_ref, dota_ref, dotb_ref, dela_ref, delb_ref, vec_ref, wot_ref,
):
    res, og = res_ref[...], og_ref[...].astype(f32)
    out = (res + (ma_ref[...].astype(f32) + mb_ref[...].astype(f32)) + nv_ref[5:6]).astype(bf)
    out = dg(out, perm_ref[...], 1, 1).astype(bf)
    whole_ref[...], out_ref[...] = out, out
    xhat, scale = normalize(res)
    gn = ga_ref[...].astype(f32) + gb_ref[...].astype(f32)
    gres = og + norm_backward(gn, nv_ref[3:4], xhat, scale)
    gres_ref[...] = gres.astype(bf)
    width = oa_ref.shape[0]

    @pl.when(pl.program_id(0) == 0)
    def _():
        for at, near, far in ((0, aan_ref, aaf_ref), (1, abn_ref, abf_ref)):
            both = jnp.concatenate([near[:, width:], far[:, width:]], axis=0)
            wot_ref[at] = jnp.transpose(both)

    low = jnp.transpose(gres.astype(bf))
    gt_ref[...] = low
    for at, o_ref, dot_ref, del_ref in (
        (0, oa_ref, dota_ref, dela_ref),
        (1, ob_ref, dotb_ref, delb_ref),
    ):
        dot = jnp.dot(wot_ref[at], low, preferred_element_type=f32).astype(bf)
        dot_ref[...] = dot
        prod = dot.astype(f32) * o_ref[...].astype(f32)
        for h in range(prod.shape[0] // HD):
            del_ref[h : h + 1, :] = jnp.sum(prod[HD * h : HD * h + HD], axis=0, keepdims=True)
    column_sums(vec_ref, [gres, gn * xhat, gn, og], res.shape[1])


def middle_back(mine, ma, mb, ga, gb, res, og, nv, perm, aa, ab, oa, ob):
    slots, model = res.shape
    width = oa.shape[0]
    tok, lane = token_block(model), lane_block(width)
    return pl.pallas_call(
        second_norm_backward,
        out_shape=(
            shape((2 * slots, model), bf),
            shape((slots, model), bf),
            shape((slots, model), bf),
            shape((model, slots), bf),
            shape((width, slots), bf),
            shape((width, slots), bf),
            shape((16, slots), f32),
            shape((16, slots), f32),
            shape((8, model), f32),
        ),
        grid_spec=pltpu.PrefetchScalarGridSpec(
            num_scalar_prefetch=1,
            grid=(slots // TB,),
            in_specs=[tok] * 6 + [VM] * 2 + [late_columns(aa)] * 4 + [lane] * 2,
            out_specs=(own_rows(slots, model), tok, tok, lane_block(model), lane, lane)
            + (lane_block(16), lane_block(16), VM),
            scratch_shapes=[pltpu.VMEM((2, width, model), bf)],
        ),
        compiler_params=params(),
        cost_estimate=cost(2, 10),
        name="second_norm_backward",
    )(mine, ma, mb, ga, gb, res, og, nv, perm, *aa, *ab, oa, ob)


def first_norm_backward(mine_ref, aan_ref, aaf_ref, abn_ref, abf_ref, gres_ref, x_ref, nv_ref, perm_ref, *refs):
    *parts, whole_ref, out_ref, vec_ref = refs
    half = len(parts) // 2
    rows = [
        jnp.concatenate([part[c] for c in range(3) for part in mine], axis=0)
        for mine in (parts[:half], parts[half:])
    ]
    wide = rows[0].shape[0]
    planes = [
        jnp.dot(a_ref[:, :wide], rows[0], preferred_element_type=f32)
        + jnp.dot(b_ref[:, :wide], rows[1], preferred_element_type=f32)
        for a_ref, b_ref in ((aan_ref, abn_ref), (aaf_ref, abf_ref))
    ]
    gn = jnp.transpose(jnp.concatenate(planes, axis=0))
    xhat, scale = normalize(x_ref[...].astype(f32))
    gres = gres_ref[...].astype(f32)
    out = (gres + norm_backward(gn, nv_ref[0:1], xhat, scale)).astype(bf)
    out = dg(out, perm_ref[...], 1, 1).astype(bf)
    whole_ref[...], out_ref[...] = out, out
    column_sums(vec_ref, [gn * xhat, gn], gn.shape[1])


def tail(mine, aa, ab, gres, x, nv, perm, parts):
    slots, model = x.shape
    tok = token_block(model)
    blocks = [pl.BlockSpec((3, part.shape[1], TB), lambda j, *_: (0, 0, j)) for part in parts]
    return pl.pallas_call(
        first_norm_backward,
        out_shape=(
            shape((2 * slots, model), bf),
            shape((slots, model), bf),
            shape((8, model), f32),
        ),
        grid_spec=pltpu.PrefetchScalarGridSpec(
            num_scalar_prefetch=1,
            grid=(slots // TB,),
            in_specs=[VM] * 4 + [tok] * 2 + [VM] * 2 + blocks,
            out_specs=(own_rows(slots, model), tok, VM),
        ),
        compiler_params=params(),
        cost_estimate=cost(2, 10),
        name="first_norm_backward",
    )(mine, *aa, *ab, gres, x, nv, perm, *parts)


def tables(seg):
    slots = seg.shape[0]
    ids = jnp.arange(8, dtype=jnp.int32)
    starts = jnp.sum((seg[None, :] < ids[:, None]).astype(jnp.int32), axis=1)
    ends = jnp.sum((seg[None, :] <= ids[:, None]).astype(jnp.int32), axis=1)
    member = seg[None, :] == ids[:, None]
    before = jnp.sum(jnp.where(member, starts[:, None], 0), axis=0)
    after = jnp.sum(jnp.where(member, ends[:, None], 0), axis=0)
    position = (jnp.arange(slots, dtype=jnp.int32) - before).astype(f32)
    frequency = 10000.0 ** (-jnp.arange(0, HD, 2).astype(f32) / HD)
    angles = frequency[:, None] * position[None, :]
    fq = jnp.concatenate([jnp.where(member, 0.0, -BIG), jnp.zeros((56, slots))], axis=0).astype(bf)
    past = jnp.broadcast_to(ids[:, None] == 7, (8, SPARE))
    fk = jnp.concatenate([member, past], axis=1).astype(bf)
    fk = jnp.concatenate([fk, jnp.zeros((56, slots + SPARE), bf)], axis=0)
    lo = before[::QT] // STRIDE
    count = (after[QT - 1 :: QT] - lo * STRIDE + KC - 1) // KC
    return jnp.cos(angles), jnp.sin(angles), fq, fk, jnp.stack([lo, count])


def moments(weight, grad, first, second):
    first = BETA_ONE * first + (1.0 - BETA_ONE) * grad
    second = BETA_TWO * second + (1.0 - BETA_TWO) * grad * grad
    corrected = first / (1.0 - BETA_ONE**STEP)
    variance = second / (1.0 - BETA_TWO**STEP)
    return first, second, corrected / (jnp.sqrt(variance) + EPS_ADAM) + DECAY * weight


class Squares:
    def __init__(self):
        self.lane = lax.broadcasted_iota(jnp.int32, (8, 128), 1)
        self.row = lax.broadcasted_iota(jnp.int32, (8, 128), 0)
        self.total = jnp.zeros((8, 128), f32)

    def add(self, group, weight, update, share=1.0):
        for row, value in ((0, weight), (1, update)):
            square = jnp.sum(value * value, axis=(0, 1), keepdims=True) * share
            self.total = self.total + jnp.where(
                (self.lane == group) & (self.row == row), square, 0.0
            )


def all_parts(parts_ref, width):
    total = parts_ref[0, :, :width].astype(f32)
    for i in range(1, parts_ref.shape[0]):
        total = total + parts_ref[i, :, :width].astype(f32)
    return total


def lamb_ffn(parts_ref, peer_ref, w_ref, m_ref, v_ref, m_out, v_out, u_out, sq_out):
    grad = all_parts(parts_ref, peer_ref.shape[1]) + peer_ref[...].astype(f32)
    blocks = w_ref.shape[2] // FB
    squares = Squares()
    for c in range(2):
        pieces = [grad[:, (2 * j + c) * FB : (2 * j + c + 1) * FB] for j in range(blocks)]
        first, second, update = moments(
            w_ref[c], jnp.concatenate(pieces, axis=1), m_ref[c], v_ref[c]
        )
        m_out[c], v_out[c], u_out[c] = first, second, update
        squares.add(4 + c, w_ref[c], update)
    sq_out[...] = squares.total


def step_ffn(parts, peer, w, m, v):
    return pl.pallas_call(
        lamb_ffn,
        out_shape=(shape(w.shape, f32),) * 3 + (shape((8, 128), f32),),
        in_specs=[VM] * 5,
        out_specs=(VM,) * 4,
        compiler_params=params(),
        cost_estimate=cost(1, 5),
        name="lamb_ffn",
    )(parts, peer, w, m, v)


def lamb_rest(
    shares, mine_ref, parts_ref, small_ref, sq_ref,
    w_ref, m_ref, v_ref, hw_ref, hm_ref, hv_ref, bw_ref, bm_ref, bv_ref, nw_ref, nm_ref, nv_ref,
    m_out, v_out, vo_out, u_out, hm_out, hv_out, hu_out, bm_out, bv_out, bu_out,
    nm_out, nv_out, nvo_out, nu_out, sq_out,
):
    grad = all_parts(parts_ref, parts_ref.shape[2])
    width = w_ref.shape[2]
    squares = Squares()
    for c in range(4):
        first, second, update = moments(
            w_ref[c], grad[:, c * width : c * width + width], m_ref[c], v_ref[c]
        )
        m_out[c], u_out[c] = first, update
        if c < 3:
            v_out[c] = second
        else:
            vo_out[...] = second
        squares.add(c, w_ref[c], update)
    lower = mine_ref[0] == 0
    small = small_ref[...]
    grad = jnp.where(lower, small[0:3, :width], small[0:3, width:])
    hm_out[...], hv_out[...], hu_out[...] = moments(hw_ref[...], grad, hm_ref[...], hv_ref[...])
    grad = jnp.where(lower, small[9:11], small[11:13])
    bm_out[...], bv_out[...], bu_out[...] = moments(bw_ref[...], grad, bm_ref[...], bv_ref[...])
    first, second, update = moments(nw_ref[...], small[3:9], nm_ref[...], nv_ref[...])
    nm_out[...], nu_out[...] = first, update
    nvo_out[...], nv_out[...] = second[:2], second[2:]
    for c in range(3):
        squares.add(6 + c, hw_ref[c : c + 1], hu_out[c : c + 1], shares[0])
    squares.add(9, bw_ref[...], bu_out[...], shares[0])
    for c in range(6):
        squares.add(10 + c, nw_ref[c : c + 1], update[c : c + 1], shares[1])
    sq_out[...] = squares.total + sq_ref[...]


def step_rest(shares, mine, parts, small, sq, attn, head, hidden, vector):
    w, h, b, n = attn[0], head[0], hidden[0], vector[0]
    return pl.pallas_call(
        partial(lamb_rest, shares),
        out_shape=tuple(
            shape(dims, f32)
            for dims in (
                w.shape, (3,) + w.shape[1:], w.shape[1:], w.shape,
                h.shape, h.shape, h.shape, b.shape, b.shape, b.shape,
                n.shape, (4, n.shape[1]), (2, n.shape[1]), n.shape, (8, 128),
            )
        ),
        in_specs=[SM] + [VM] * 15,
        out_specs=(VM,) * 15,
        compiler_params=params(),
        cost_estimate=cost(1, 5),
        name="lamb_rest",
    )(mine, parts, small, sq, *attn, *head, *hidden, *vector)


def apply_updates(sums_ref, *refs):
    weights, updates, outs, norms_out = refs[:5], refs[5:10], refs[10:15], refs[15]
    total = sums_ref[0]
    for i in range(1, sums_ref.shape[0]):
        total = total + sums_ref[i]
    norms = jnp.sqrt(total)
    norms_out[...] = norms[:2, :16]
    ratio = norms[0:1] / norms[1:2]
    lane = lax.broadcasted_iota(jnp.int32, (1, 128), 1)

    def rate(group):
        picked = jnp.where(lane == group, ratio, 0.0)
        return RATE * jnp.sum(picked, axis=1, keepdims=True)

    at = 0
    for count, w, u, out in zip((4, 2, 3, 1, 6), weights, updates, outs):
        for c in range(count):
            where = c if len(w.shape) == 3 else slice(None) if count == 1 else slice(c, c + 1)
            out[where] = w[where] - rate(at + c) * u[where]
        at += count


def new_weights(sums, weights, updates):
    return pl.pallas_call(
        apply_updates,
        out_shape=tuple(shape(w.shape, f32) for w in weights) + (shape((2, 16), f32),),
        in_specs=[VM] * 11,
        out_specs=(VM,) * 6,
        compiler_params=params(),
        cost_estimate=cost(1, 5),
        name="new_weights",
    )(sums, *weights, *updates)


def swap(value, axis_name, offset):
    count = lax.axis_size(axis_name)
    return lax.ppermute(value, axis_name, [(i, i ^ offset) for i in range(count)])


def planes():
    count = lax.axis_size("dp")
    return [[2 * u + core for u in range(count // 2)] for core in range(2)]


def exchange(blocks):
    return lax.all_to_all(blocks, "dp", 0, 0, axis_index_groups=planes())


def row_order(model, count):
    block = model // count
    place = np.arange(model) // block
    other = jnp.asarray(place // (count // 2), jnp.int32)
    owner = jnp.asarray(2 * (place % (count // 2)), jnp.int32) + (lax.axis_index("dp") % 2 ^ other)
    feature = owner * block + jnp.asarray(np.arange(model) % block, jnp.int32)
    return jnp.arange(model, dtype=jnp.int32)[:, None] == feature[None, :]


class Gather:
    def __init__(self, value, steps=("plane", "core")):
        self.value, self.steps, self.flying = value, list(steps), []

    def peer(self):
        return Gather(self.value, ("tp", "core"))

    def launch(self):
        step = self.steps[0]
        if step == "plane":
            count = lax.axis_size("dp") // 2
            spread = jnp.broadcast_to(self.value[None], (count,) + self.value.shape)
            self.flying = [exchange(spread)]
        else:
            self.flying = [swap(self.value, "dp" if step == "core" else "tp", 1)]

    def finish(self):
        step = self.steps.pop(0)
        if step == "core":
            self.value = (self.value, self.flying[0])
        else:
            self.value = self.flying[0].reshape(-1, self.flying[0].shape[-1])
        self.flying = []


def far_exchange(blocks):
    count = lax.axis_size("dp") // 4
    groups = [[4 * z + low for z in range(count)] for low in range(4)]
    return lax.all_to_all(blocks, "dp", 0, 0, axis_index_groups=groups)


class Scatter:
    def __init__(self, keep, send):
        self.parts, self.send = [keep], send
        self.steps, self.flying = ["core", "pair", "tp", "far"], []

    def side(self, other):
        at = (lax.axis_index("dp") >> 1) % 2 ^ other
        count = lax.axis_size("dp") // 4
        total = 0.0
        for part in self.parts:
            blocks = part.reshape(count, 2, -1, part.shape[-1])
            total = total + lax.dynamic_index_in_dim(blocks, at, 1, False).astype(f32)
        return total

    def launch(self):
        step = self.steps[0]
        if step == "pair":
            self.send = self.side(1).astype(bf)
        if step == "far":
            self.flying = [far_exchange(self.value)]
        elif step == "tp":
            self.flying = [swap(self.value, "tp", 1)]
        else:
            self.flying = [swap(self.send, "dp", 1 if step == "core" else 2)]

    def finish(self):
        step = self.steps.pop(0)
        if step == "core":
            self.parts = self.parts + self.flying
        elif step == "pair":
            self.value = (self.side(0) + self.flying[0].astype(f32)).astype(bf)
        else:
            self.value = self.flying[0]
        self.flying = []

    def merge(self, peer):
        self.value = (self.value.astype(f32) + peer.value.astype(f32)).astype(bf)
        self.steps = ["far"]


class Pool:
    def __init__(self, own, peer):
        self.width = own.value.shape[-1]
        self.value = jnp.concatenate([own.value, peer.value], axis=-1)
        self.steps, self.flying = ["far", "tp"], []

    def launch(self):
        if self.steps[0] == "far":
            self.flying = [far_exchange(self.value)]
        else:
            peer = self.value[..., self.width :].astype(f32)
            self.flying = [swap(jnp.sum(peer, axis=0).astype(bf), "tp", 1)]

    def finish(self):
        if self.steps.pop(0) == "far":
            self.value = self.flying[0]
        else:
            self.peer = self.flying[0]
        self.flying = []


def tie(value, *others):
    return lax.optimization_barrier((value, *others))[0]


def meet(value, *movers):
    out = lax.optimization_barrier((value, *[a for mover in movers for a in mover.flying]))
    at = 1
    for mover in movers:
        count = len(mover.flying)
        mover.flying = list(out[at : at + count])
        at += count
        mover.finish()
    return out[0]


def sum_over_dp(value):
    step = 2
    while step < lax.axis_size("dp"):
        value = value + swap(value, "dp", step)
        step *= 2
    return value


def by_peer(own, peer, axis):
    first = lax.axis_index("tp") == 0
    return jnp.where(
        first, jnp.concatenate([own, peer], axis), jnp.concatenate([peer, own], axis)
    )


def on_device(
    inputs, out_grad, segment_ids, attn_weights, ffn_weights, head_bias, hidden_bias, norm_vectors,
    attn_first, ffn_first, head_first, hidden_first, vector_first,
    attn_second, ffn_second, head_second, hidden_second, vector_second,
):
    dp_count, tp_count = lax.axis_size("dp"), lax.axis_size("tp")
    mine = lax.axis_index("tp")
    rows, slots = segment_ids.shape
    assert rows == tp_count == 2
    shard, head_width = attn_weights.shape[1:]
    hidden = ffn_weights.shape[2]
    model = inputs.shape[1]

    a_own = Gather(jnp.concatenate(list(attn_weights.astype(bf)), axis=1))
    a_own.launch()
    x = lax.dynamic_slice_in_dim(inputs, mine * slots, slots, 0)
    order = row_order(model, dp_count)
    perm = order.astype(bf)
    exact = partial(jnp.dot, precision=lax.Precision.HIGHEST, preferred_element_type=f32)
    nv = exact(jnp.concatenate([norm_vectors, jnp.zeros((2, model), f32)], 0), order.astype(f32))
    xt = dg(perm, x, 0, 1)
    centered = xt - jnp.mean(xt, axis=0, keepdims=True)
    scale = lax.rsqrt(jnp.mean(centered * centered, axis=0, keepdims=True) + EPS_NORM)
    n1t = (centered * scale * nv[0][:, None] + nv[1][:, None]).astype(bf)
    bias_own = jnp.concatenate([head_bias.reshape(-1), hidden_bias])
    def hidden_blocks(bias):
        return bias[3 * head_width :].reshape(-1, 1, FB)

    both = jnp.concatenate(list(ffn_weights.astype(bf)), axis=1)
    og = lax.dynamic_slice_in_dim(out_grad, mine * slots, slots, 0)
    seg = lax.dynamic_index_in_dim(segment_ids, mine, 0, keepdims=False)
    cos, sin, fq, fk, rng = tables(seg)
    x = dg(x, perm, 1, 0).astype(bf)
    ogt = dg(perm, og, 0, 1).astype(bf)
    og = dg(og, perm, 1, 0).astype(bf)
    n1t, cos, sin, fq, fk, rng, x, ogt, og, both = lax.optimization_barrier(
        (n1t, cos, sin, fq, fk, rng, x, ogt, og, both)
    )
    n1t = meet(n1t, a_own)
    a_peer = a_own.peer()
    w_own = Gather(tie(both, a_own.value))
    a_own.launch()
    a_peer.launch()
    w_own.launch()
    bias_own, _ = lax.optimization_barrier((bias_own, a_own.value))
    bias_peer = swap(bias_own.reshape(-1, head_width), "tp", 1).reshape(-1)

    head_columns = jnp.concatenate(
        [bias[: 3 * head_width].reshape(3, head_width) for bias in (bias_own, bias_peer)]
        + [jnp.zeros((2, head_width), f32)],
        0,
    ).T


    n1t = meet(n1t, a_own)
    a_one = a_own.value
    saved_own, o_own, lse_own = attn_fwd(0, rng, n1t, a_one, head_columns, cos, sin, fq, fk)
    o_own = meet(o_own, a_peer)
    a_peer.launch()
    again = meet(tie(n1t, o_own), a_peer)
    a_two = a_peer.value
    saved_peer, o_peer, lse_peer = attn_fwd(
        3, rng, again, a_two, head_columns, cos, sin, fq, fk
    )
    o_peer = meet(o_peer, w_own)
    w_peer = w_own.peer()
    w_own.launch()
    w_peer.launch()
    res, n2, n2t = middle(o_own, o_peer, a_one, a_two, x, nv)

    n2 = meet(n2, w_own)
    mix_own, gn_own, keep, send, dhb_own = ffn(n2, n2t, og, ogt, hidden_blocks(bias_own), w_own.value)
    f_own = Scatter(keep, send)
    f_own.launch()
    again = meet(tie(n2, mix_own), w_peer)
    w_peer.launch()
    again = meet(again, w_peer)
    mix_peer, gn_peer, keep, send, dhb_peer = ffn(
        again, n2t, og, ogt, hidden_blocks(bias_peer), w_peer.value
    )
    f_peer = Scatter(keep, send)
    mix_peer = meet(mix_peer, f_own)
    f_own.launch()
    f_peer.launch()
    layer_output, out_low, gres, gt, dot_own, dot_peer, delta_own, delta_peer, sums_two = middle_back(
        mine.reshape(1), mix_own, mix_peer, gn_own, gn_peer, res, og, nv, perm, a_one, a_two, o_own, o_peer
    )

    out_far = swap(out_low, "tp", 1)

    def back(dot, saved, lse, delta, heads):
        return attn_bwd(rng, dot, saved[0], lse, delta, cos, sin, fq, n1t, gt, heads)

    dot_peer = meet(dot_peer, f_peer)
    f_peer.launch()
    keep, send, dbias_peer, dt_peer = back(dot_peer, saved_peer, lse_peer, delta_peer, o_peer)
    g_peer = Scatter(keep, send)
    g_peer.launch()
    dot_own, out_far, dt_peer = lax.optimization_barrier((dot_own, out_far, dt_peer))
    dot_own = meet(dot_own, f_own, f_peer)
    f_pool = Pool(f_own, f_peer)
    f_pool.launch()
    dot_own = meet(dot_own, g_peer)
    g_peer.launch()
    keep, send, dbias_own, dt_own = back(dot_own, saved_own, lse_own, delta_own, o_own)
    g_own = Scatter(keep, send)
    g_own.launch()
    dt_own, gres = lax.optimization_barrier((dt_own, gres))
    gres = meet(gres, g_peer)
    g_peer.launch()
    gres = meet(gres, g_own)
    g_own.launch()
    input_grad, in_low, sums_one = tail(mine.reshape(1), a_one, a_two, gres, x, nv, perm, [dt_own, dt_peer])
    in_low = meet(in_low, g_own, g_peer)
    g_own.merge(g_peer)
    g_own.value, f_pool.flying[0] = lax.optimization_barrier((g_own.value, f_pool.flying[0]))
    g_own.launch()
    f_pool.finish()
    f_pool.launch()
    sums = exact(jnp.concatenate([sums_one[:2], sums_two[:4]], 0), order.astype(f32).T)
    small = jnp.concatenate(
        [
            by_peer(dbias_own[:, :3].T, dbias_peer[:, :3].T, 1),
            sums,
            by_peer(dhb_own.reshape(-1), dhb_peer.reshape(-1), 0).reshape(-1, model),
        ],
        0,
    )
    small_far = swap(small, "tp", 1)
    in_low, small_far = lax.optimization_barrier((in_low, small_far))
    in_low = meet(in_low, f_pool)
    small = small + small_far
    in_far = swap(in_low, "tp", 1)
    g_own.finish()

    ffn_first_new, ffn_second_new, ffn_update, squares = step_ffn(
        f_pool.value, f_pool.peer, ffn_weights, ffn_first, ffn_second
    )
    near = swap(small, "dp", 1)
    near, squares = lax.optimization_barrier((near, squares))
    small = sum_over_dp(small + near)
    wide = lambda v: v.reshape(2, -1)
    shares = (1.0 / dp_count, 1.0 / (dp_count * tp_count))
    (
        attn_first_new, attn_second_new, out_second_new, attn_update,
        head_first_new, head_second_new, head_update,
        hidden_first_new, hidden_second_new, hidden_update,
        vector_first_new, vector_second_new, norm_second_new, vector_update, squares,
    ) = step_rest(
        shares, mine.reshape(1), g_own.value, small, squares,
        (attn_weights, attn_first, attn_second),
        (head_bias, head_first, head_second),
        (wide(hidden_bias), wide(hidden_first), wide(hidden_second)),
        (norm_vectors, vector_first, vector_second),
    )
    copies = dp_count * tp_count
    squares, out_far = lax.optimization_barrier((squares, out_far))
    other = (1 - mine) * slots
    layer_output = lax.dynamic_update_slice_in_dim(layer_output, out_far, other, 0)
    input_grad = lax.dynamic_update_slice_in_dim(input_grad, in_far, other, 0)
    sums = lax.all_to_all(
        jnp.broadcast_to(squares[None], (copies, 8, 128)), ("dp", "tp"), 0, 0
    )
    sums, input_grad, layer_output = lax.optimization_barrier((sums, input_grad, layer_output))
    new_attn, new_ffn, new_head, new_hidden, new_vectors, norms = new_weights(
        sums,
        (attn_weights, ffn_weights, head_bias, wide(hidden_bias), norm_vectors),
        (attn_update, ffn_update, head_update, hidden_update, vector_update),
    )
    return (
        layer_output,
        input_grad,
        new_attn,
        new_ffn,
        new_head,
        new_hidden.reshape(-1),
        new_vectors,
        attn_first_new,
        ffn_first_new,
        head_first_new,
        hidden_first_new.reshape(-1),
        vector_first_new,
        attn_second_new,
        out_second_new,
        ffn_second_new,
        head_second_new,
        hidden_second_new.reshape(-1),
        vector_second_new,
        norm_second_new,
        norms,
    )


def solution(mesh):
    in_specs = (
        P("dp", None),
        P("dp", None),
        P("dp", None),
        P(None, "dp", "tp"),
        P(None, "dp", "tp"),
        P(None, "tp"),
        P("tp"),
        P(),
        P(None, "dp", "tp"),
        P(None, "dp", "tp"),
        P(None, "tp"),
        P("tp"),
        P(),
        P(None, "dp", "tp"),
        P(None, "dp", "tp"),
        P(None, "tp"),
        P("tp"),
        P(),
    )
    out_specs = (
        P("dp", None),
        P("dp", None),
        P(None, "dp", "tp"),
        P(None, "dp", "tp"),
        P(None, "tp"),
        P("tp"),
        P(),
        P(None, "dp", "tp"),
        P(None, "dp", "tp"),
        P(None, "tp"),
        P("tp"),
        P(),
        P(None, "dp", "tp"),
        P("dp", "tp"),
        P(None, "dp", "tp"),
        P(None, "tp"),
        P("tp"),
        P(),
        P(),
        P(),
    )
    return jax.shard_map(
        on_device, mesh=mesh, in_specs=in_specs, out_specs=out_specs, check_vma=False
    )
```

```python
import math
from functools import partial

import jax
import jax.numpy as jnp
import numpy as np
from jax import lax
from jax.experimental import pallas as pl
from jax.experimental.pallas import tpu as pltpu
from jax.sharding import PartitionSpec as P

STEP = 10
EPS_NORM = 1e-05
EPS_ADAM = 1e-06
BETA_ONE = 0.9
BETA_TWO = 0.999
DECAY = 0.01
RATE = 0.5

HD = 32
QT = 128
KC = 256
BIG = 1e30
STRIDE = 64
SPARE = 256
LN2 = math.log(2.0)
QSCALE = math.log2(math.e) / math.sqrt(HD)
bf = jnp.bfloat16
f32 = jnp.float32
VM = pl.BlockSpec(memory_space=pltpu.VMEM)
SM = pl.BlockSpec(memory_space=pltpu.SMEM)


def dg(a, b, ca, cb):
    return lax.dot_general(a, b, (((ca,), (cb,)), ((), ())), preferred_element_type=f32)


def shape(dims, kind):
    return jax.ShapeDtypeStruct(dims, kind)


def cost(gflop, mbytes):
    return pl.CostEstimate(
        flops=int(gflop * 1e9), bytes_accessed=int(mbytes * 1e6), transcendentals=0
    )


def params(mbytes=56):
    return pltpu.CompilerParams(vmem_limit_bytes=mbytes * 1024 * 1024)


def rope_rows(y, cos, sin, sign):
    out = []
    for h in range(y.shape[0] // HD):
        top = y[HD * h : HD * h + HD // 2]
        bot = y[HD * h + HD // 2 : HD * h + HD]
        out.append(top * cos - sign * bot * sin)
        out.append(bot * cos + sign * top * sin)
    return jnp.concatenate(out, axis=0)


def two_heads(block, extra):
    zero = jnp.zeros((HD, QT), bf)
    left = jnp.concatenate([block[:HD], zero] + extra, axis=0)
    right = jnp.concatenate([zero, block[HD:]] + extra, axis=0)
    return jnp.concatenate([left, right], axis=1)


def attention_forward(col, rng_ref, n1t_ref, an_ref, af_ref, b_ref, cos_ref, sin_ref, fq_ref, fk_ref, *refs):
    count = len(PARTS)
    outs = refs[: 4 * count]
    ot_ref, lse_ref, vt_ref, qbd_ref, s_ref, *held, sem = refs[4 * count :]
    qts, kts, kps, vns = (held[count * i : count * i + count] for i in range(4))
    width = ot_ref.shape[0]
    heads = width // HD
    groups = heads // 2
    slots = n1t_ref.shape[1]
    pad = kts[0].shape[1] - slots
    cos, sin = cos_ref[...], sin_ref[...]
    a = jnp.concatenate([an_ref[:, : 3 * width], af_ref[:, : 3 * width]], axis=0)
    y = dg(a, n1t_ref[...], 0, 0)
    qb = (rope_rows(y[:width] + b_ref[:, col : col + 1], cos, sin, 1.0) * QSCALE).astype(bf)
    kb = rope_rows(y[width : 2 * width] + b_ref[:, col + 1 : col + 2], cos, sin, 1.0).astype(bf)
    vb = (y[2 * width :] + b_ref[:, col + 2 : col + 3]).astype(bf)
    ones = jnp.ones((16, slots + pad), bf)
    for odd, moved in enumerate((vb, vb[:, STRIDE:])):
        moved = jnp.concatenate(
            [moved, jnp.zeros((width, slots + pad - moved.shape[1]), bf)], axis=1
        )
        for h in range(heads):
            top = 48 * (h % 2)
            vt_ref[odd, h // 2, top : top + HD, :] = moved[HD * h : HD * h + HD]
            vt_ref[odd, h // 2, top + HD : top + 48, :] = ones
    past = jnp.transpose(jnp.concatenate([jnp.zeros((64, pad), bf), fk_ref[:, slots:]], axis=0))
    for (first, last), qt_ref, kt_ref, kp_ref, vn_ref in zip(PARTS, qts, kts, kps, vns):
        qt_ref[...] = qb[64 * first : 64 * last]
        kt_ref[:, :slots] = kb[64 * first : 64 * last]
        kt_ref[:, slots:] = jnp.zeros((64 * (last - first), pad), bf)
        for g in range(first, last):
            rows = slice(64 * g, 64 * g + 64)
            both = jnp.concatenate([kb[rows], fk_ref[:, :slots]], axis=0)
            kp_ref[g - first, :slots, :] = jnp.transpose(both)
            kp_ref[g - first, slots:, :] = past
            both = jnp.concatenate([vb[rows], jnp.zeros((64, slots), bf)], axis=0)
            vn_ref[g - first, :slots, :] = jnp.transpose(both)
            vn_ref[g - first, slots:, :] = jnp.zeros((pad, 128), bf)
    saving = [
        pltpu.make_async_copy(src, dst, sem.at[i]) for i, (src, dst) in enumerate(zip(held, outs))
    ]
    for copy in saving:
        copy.start()
    where = [(p, g - first) for p, (first, last) in enumerate(PARTS) for g in range(first, last)]

    def tile(i, _):
        q0 = pl.multiple_of(i * QT, QT)
        lo, count = rng_ref[0, i], rng_ref[1, i]
        fq = fq_ref[:, pl.ds(q0, QT)]
        for g in range(groups):
            p, r = where[g]
            qbd_ref[g] = two_heads(qts[p][64 * r : 64 * r + 64, pl.ds(q0, QT)], [fq])

        def scores(j, tops):
            k0 = pl.multiple_of(lo * STRIDE + j * KC, STRIDE)
            at = pl.multiple_of(j * KC, KC)
            out = []
            for g in range(groups):
                p, r = where[g]
                keys = kps[p][r, pl.ds(k0, KC), :]
                s = jnp.dot(keys, qbd_ref[g], preferred_element_type=f32)
                s_ref[g, pl.ds(at, KC), :] = s
                top = tops[g]
                for r in range(KC // 8):
                    top = jnp.maximum(top, s[8 * r : 8 * r + 8])
                out.append(top)
            return tuple(out)

        start = tuple(jnp.full((8, 2 * QT), -3e38, f32) for _ in range(groups))
        tops = lax.fori_loop(0, count, scores, start)
        tops = [jnp.max(top, axis=0, keepdims=True) for top in tops]

        def mix(j, sums):
            k0 = pl.multiple_of((lo >> 1) * 128 + j * KC, 128)
            at = pl.multiple_of(j * KC, KC)
            out = []
            for g in range(groups):
                p = jnp.exp2(s_ref[g, pl.ds(at, KC), :] - tops[g]).astype(bf)
                values = vt_ref[lo & 1, g, :, pl.ds(k0, KC)]
                part = jnp.dot(values, p, preferred_element_type=f32)
                out.append(sums[2 * g] + part[:48, :QT])
                out.append(sums[2 * g + 1] + part[48:, QT:])
            return tuple(out)

        start = tuple(jnp.zeros((48, QT), f32) for _ in range(heads))
        sums = lax.fori_loop(0, count, mix, start)
        for h in range(heads):
            total = sums[h][HD : HD + 1]
            ot_ref[HD * h : HD * h + HD, pl.ds(q0, QT)] = (sums[h][:HD] / total).astype(bf)
            col = QT * (h % 2)
            lse_ref[h : h + 1, pl.ds(q0, QT)] = tops[h // 2][:, col : col + QT] + jnp.log2(total)
        return 0

    lax.fori_loop(0, slots // QT, tile, 0)
    for copy in saving:
        copy.wait()


PARTS = ((0, 5),)


def attn_fwd(col, rng, n1t, a, b, cos, sin, fq, fk):
    slots, width = n1t.shape[1], b.shape[0]
    heads, groups, longer = width // HD, width // 64, slots + SPARE
    assert groups == PARTS[-1][1]
    sizes = [last - first for first, last in PARTS]
    held = (
        [(64 * n, slots) for n in sizes]
        + [(64 * n, longer) for n in sizes]
        + [(n, longer, 128) for n in sizes] * 2
    )
    out = pl.pallas_call(
        partial(attention_forward, col),
        out_shape=tuple(
            [shape(dims, bf) for dims in held] + [shape((width, slots), bf), shape((16, slots), f32)]
        ),
        in_specs=[SM] + [VM] * 8,
        out_specs=(pl.BlockSpec(memory_space=pl.ANY),) * len(held) + (VM, VM),
        scratch_shapes=[
            pltpu.VMEM((2, groups, 96, longer), bf),
            pltpu.VMEM((groups, 128, 2 * QT), bf),
            pltpu.VMEM((groups, longer, 2 * QT), f32),
        ]
        + [pltpu.VMEM(dims, bf) for dims in held]
        + [pltpu.SemaphoreType.DMA((len(held),))],
        compiler_params=params(),
        cost_estimate=cost(12, 10),
        name="attention_forward",
    )(rng, n1t, *a, b, cos, sin, fq, fk)
    count = len(sizes)
    saved = [tuple(out[count * i + p] for i in range(4)) for p in range(count)]
    return saved, out[4 * count], out[4 * count + 1]


def attention_backward(
    first, rng_ref, dot_ref, qt_ref, kt_ref, kp_ref, vn_ref, lse_ref, delta_ref, cos_ref, sin_ref, fq_ref,
    n1t_far, gt_far, ot_far, keep_ref, send_ref, db_ref, dt_far,
    dqt_ref, dkt_ref, dvt_ref, qbd_ref, dobd_ref, both_ref, n1t_ref, gt_ref, ot_ref, dt_ref, sem,
):
    loads = [
        pltpu.make_async_copy(src, dst, sem.at[i])
        for i, (src, dst) in enumerate(((n1t_far, n1t_ref), (gt_far, gt_ref), (ot_far, ot_ref)))
    ]
    for copy in loads:
        copy.start()
    width, slots = qt_ref.shape
    heads = width // HD
    groups = heads // 2
    base = 64 * first
    dkt_ref[...] = jnp.zeros_like(dkt_ref)
    dvt_ref[...] = jnp.zeros_like(dvt_ref)
    both_ref[0] = kt_ref[...]
    both_ref[1] = jnp.concatenate(
        [kt_ref[:, STRIDE:], jnp.zeros((width, STRIDE), bf)], axis=1
    )
    blank = jnp.zeros((64, QT), bf)

    def tile(i, _):
        q0 = pl.multiple_of(i * QT, QT)
        lo, count = rng_ref[0, i], rng_ref[1, i]
        fq = fq_ref[:, pl.ds(q0, QT)]
        for g in range(groups):
            rows = slice(64 * g, 64 * g + 64)
            qbd_ref[g] = two_heads(qt_ref[rows, pl.ds(q0, QT)], [fq])
            dobd_ref[g] = two_heads(
                dot_ref[base + 64 * g : base + 64 * g + 64, pl.ds(q0, QT)], [blank]
            )

        def pair(ref, g):
            return jnp.concatenate(
                [
                    ref[2 * (first + g) + a : 2 * (first + g) + a + 1, pl.ds(q0, QT)]
                    for a in range(2)
                ],
                axis=1,
            )

        def chunk(j, sums):
            k0 = pl.multiple_of(lo * STRIDE + j * KC, STRIDE)
            kl = pl.multiple_of((lo >> 1) * 128 + j * KC, 128)
            odd = lo & 1
            out = []
            for g in range(groups):
                s = jnp.dot(kp_ref[g, pl.ds(k0, KC), :], qbd_ref[g], preferred_element_type=f32)
                dp = jnp.dot(vn_ref[g, pl.ds(k0, KC), :], dobd_ref[g], preferred_element_type=f32)
                p = jnp.exp2(s - pair(lse_ref, g))
                ds = (p * (dp - pair(delta_ref, g))).astype(bf)
                p = p.astype(bf)
                rows = slice(64 * g, 64 * g + 64)
                dvt_ref[odd, rows, pl.ds(kl, KC)] += dg(dobd_ref[g, :64], p, 1, 1)
                dkt_ref[odd, rows, pl.ds(kl, KC)] += dg(qbd_ref[g, :64], ds, 1, 1)
                dq = jnp.dot(both_ref[odd, rows, pl.ds(kl, KC)], ds, preferred_element_type=f32)
                out.append(sums[2 * g] + dq[:HD, :QT])
                out.append(sums[2 * g + 1] + dq[HD:, QT:])
            return tuple(out)

        start = tuple(jnp.zeros((HD, QT), f32) for _ in range(heads))
        sums = lax.fori_loop(0, count, chunk, start)
        for h in range(heads):
            dqt_ref[HD * h : HD * h + HD, pl.ds(q0, QT)] = sums[h]
        return 0

    lax.fori_loop(0, slots // QT, tile, 0)
    cos, sin = cos_ref[...], sin_ref[...]
    dt_ref[0] = rope_rows(dqt_ref[...] * HD**-0.5, cos, sin, -1.0).astype(bf)

    def joined(ref):
        moved = jnp.concatenate(
            [jnp.zeros((width, STRIDE), f32), ref[1, :, : slots - STRIDE]], axis=1
        )
        return ref[0, :, :slots] + moved

    dt_ref[1] = rope_rows(joined(dkt_ref) * LN2, cos, sin, -1.0).astype(bf)
    dt_ref[2] = joined(dvt_ref).astype(bf)
    store = pltpu.make_async_copy(dt_ref, dt_far, sem.at[3])
    store.start()
    rows = jnp.concatenate([dt_ref[c] for c in range(3)], axis=0)
    for c in range(3):
        db_ref[:, c : c + 1] = jnp.sum(dt_ref[c].astype(f32), axis=1, keepdims=True)
    for copy in loads:
        copy.wait()
    half, wide = keep_ref.shape[0], rows.shape[0]
    for cols, left, right in (
        (slice(0, wide), n1t_ref[...], rows),
        (slice(wide, keep_ref.shape[1]), gt_ref[...], ot_ref[...]),
    ):
        dw = dg(left, right, 1, 1).astype(bf)
        keep_ref[:, cols] = dw[:half]
        send_ref[:, cols] = dw[half:]
    store.wait()


def attn_bwd(rng, dot, saved, lse, delta, cos, sin, fq, n1t, gt, ot):
    first, last = PARTS[0]
    width, slots = saved[0].shape
    model = n1t.shape[0]
    groups, longer = last - first, slots + SPARE
    far = pl.BlockSpec(memory_space=pl.ANY)
    return pl.pallas_call(
        partial(attention_backward, first),
        out_shape=(shape((model // 2, 4 * width), bf),) * 2
        + (shape((width, 8), f32), shape((3, width, slots), bf)),
        in_specs=[SM] + [VM] * 10 + [far] * 3,
        out_specs=(VM, VM, VM, far),
        scratch_shapes=[
            pltpu.VMEM((width, slots), f32),
            pltpu.VMEM((2, width, longer), f32),
            pltpu.VMEM((2, width, longer), f32),
            pltpu.VMEM((groups, 128, 2 * QT), bf),
            pltpu.VMEM((groups, 128, 2 * QT), bf),
            pltpu.VMEM((2, width, longer), bf),
            pltpu.VMEM((model, slots), bf),
            pltpu.VMEM((model, slots), bf),
            pltpu.VMEM((width, slots), bf),
            pltpu.VMEM((3, width, slots), bf),
            pltpu.SemaphoreType.DMA((4,)),
        ],
        compiler_params=params(),
        cost_estimate=cost(4 * groups, 10),
        name="attention_backward",
    )(rng, dot, *saved, lse, delta, cos, sin, fq, n1t, gt, ot)


def normalize(values):
    centered = values - jnp.mean(values, axis=1, keepdims=True)
    scale = lax.rsqrt(jnp.mean(centered * centered, axis=1, keepdims=True) + EPS_NORM)
    return centered * scale, scale


def norm_backward(grad, gain, xhat, scale):
    e = grad * gain
    return scale * (
        e - jnp.mean(e, axis=1, keepdims=True) - xhat * jnp.mean(e * xhat, axis=1, keepdims=True)
    )


def column_sums(ref, parts, width):
    rows = [jnp.sum(part, axis=0, keepdims=True) for part in parts]
    rows.append(jnp.zeros((8 - len(parts), width), f32))
    total = jnp.concatenate(rows, axis=0)

    @pl.when(pl.program_id(0) == 0)
    def _():
        ref[...] = total

    @pl.when(pl.program_id(0) > 0)
    def _():
        ref[...] += total


TB = 512


def own_rows(slots, width):
    return pl.BlockSpec((TB, width), lambda j, mine: (mine[0] * (slots // TB) + j, 0))


def token_block(width):
    return pl.BlockSpec((TB, width), lambda j, *_: (j, 0))


def lane_block(height):
    return pl.BlockSpec((height, TB), lambda j, *_: (0, j))


def late_columns(a):
    return pl.BlockSpec((a[0].shape[0], a[0].shape[1] // 2), lambda j, *_: (0, 1))


def attended_norm(oa_ref, ob_ref, aan_ref, aaf_ref, abn_ref, abf_ref, x_ref, nv_ref, res_ref, n2_ref, n2t_ref):
    width = oa_ref.shape[0]
    planes = [
        jnp.dot(a_ref[:, width:], oa_ref[...], preferred_element_type=f32)
        + jnp.dot(b_ref[:, width:], ob_ref[...], preferred_element_type=f32)
        for a_ref, b_ref in ((aan_ref, abn_ref), (aaf_ref, abf_ref))
    ]
    attended = jnp.transpose(jnp.concatenate(planes, axis=0))
    res = x_ref[...].astype(f32) + attended + nv_ref[2:3]
    res_ref[...] = res.astype(bf)
    n2 = (normalize(res)[0] * nv_ref[3:4] + nv_ref[4:5]).astype(bf)
    n2_ref[...] = n2
    n2t_ref[...] = jnp.transpose(n2)


def middle(oa, ob, aa, ab, x, nv):
    slots, model = x.shape
    width = oa.shape[0]
    return pl.pallas_call(
        attended_norm,
        grid=(slots // TB,),
        out_shape=(
            shape((slots, model), bf),
            shape((slots, model), bf),
            shape((model, slots), bf),
        ),
        in_specs=[lane_block(width)] * 2 + [late_columns(aa)] * 4 + [token_block(model), VM],
        out_specs=(token_block(model),) * 2 + (lane_block(model),),
        compiler_params=params(),
        cost_estimate=cost(2, 10),
        name="attended_norm",
    )(oa, ob, *aa, *ab, x, nv)


def gelu_parts(pre):
    z = jnp.abs(pre) * (2.0**-0.5)
    bell = jnp.exp(-z * z)
    t = 1.0 / (1.0 + 0.3275911 * z)
    tail = t * (0.254829592 + t * (-0.284496736 + t * (1.421413741 + t * (-1.453152027 + t * 1.061405429))))
    half = 0.5 * tail * bell
    return jnp.where(pre >= 0.0, 1.0 - half, half), bell * ((2.0 * math.pi) ** -0.5)


def feed_forward(
    n2_far, n2t_far, og_far, ogt_far, hb_ref, w1n_ref, w1f_ref, w2n_ref, w2f_ref,
    mix_far, gn_ref, keep_ref, send_ref, dhb_ref,
    up_ref, down_ref, act_ref, gpre_ref, n2_ref, og_ref, n2t_ref, ogt_ref, mix_ref, sem,
):
    j = pl.program_id(0)
    pairs = ((n2_far, n2_ref), (og_far, og_ref), (n2t_far, n2t_ref), (ogt_far, ogt_ref))
    loads = [pltpu.make_async_copy(src, dst, sem.at[i]) for i, (src, dst) in enumerate(pairs)]

    @pl.when(j == 0)
    def _():
        for copy in loads:
            copy.start()
        loads[0].wait()
        loads[1].wait()

    w1 = jnp.concatenate([w1n_ref[...], w1f_ref[...]], axis=0)
    w2 = jnp.concatenate([w2n_ref[...], w2f_ref[...]], axis=0)
    here = pl.ds(pl.multiple_of(j * FB, FB), FB)
    up_ref[:, here] = w1
    down_ref[:, here] = w2
    pre = jnp.dot(n2_ref[...], w1, preferred_element_type=f32) + hb_ref[0]
    gact = jnp.dot(og_ref[...], w2, preferred_element_type=f32)
    cdf = 0.5 + 0.5 * lax.erf(pre * (2.0**-0.5))
    pdf = jnp.exp(pre * pre * -0.5) * ((2.0 * math.pi) ** -0.5)
    act = (pre * cdf).astype(bf)
    gpre = (gact * (cdf + pre * pdf)).astype(bf)
    act_ref[:, here] = act
    gpre_ref[:, here] = gpre

    @pl.when(j == 0)
    def _():
        loads[2].wait()
        loads[3].wait()

    half = keep_ref.shape[0]
    for at, left, right in ((0, n2t_ref, gpre), (FB, ogt_ref, act)):
        dw = jnp.dot(left[...], right, preferred_element_type=f32).astype(bf)
        keep_ref[:, at : at + FB] = dw[:half]
        send_ref[:, at : at + FB] = dw[half:]
    dhb_ref[0] = jnp.sum(gpre.astype(f32), axis=0, keepdims=True)

    @pl.when(j == pl.num_programs(0) - 1)
    def _():
        mix_ref[...] = dg(act_ref[...], down_ref[...], 1, 1).astype(bf)
        store = pltpu.make_async_copy(mix_ref, mix_far, sem.at[4])
        store.start()
        gn_ref[...] = dg(gpre_ref[...], up_ref[...], 1, 1).astype(bf)
        store.wait()


FB = 256


def ffn(n2, n2t, og, ogt, hb, w):
    slots, model = n2.shape
    hidden = w[0].shape[1] // 2
    blocks = hidden // FB
    far = pl.BlockSpec(memory_space=pl.ANY)
    up = pl.BlockSpec((model // 2, FB), lambda j: (0, j))
    down = pl.BlockSpec((model // 2, FB), lambda j: (0, blocks + j))
    bias = pl.BlockSpec((1, 1, FB), lambda j: (j, 0, 0))
    pair = pl.BlockSpec((model // 2, 2 * FB), lambda j: (0, j))
    return pl.pallas_call(
        feed_forward,
        grid=(hidden // FB,),
        out_shape=(
            shape((slots, model), bf),
            shape((slots, model), bf),
            shape((model // 2, 2 * hidden), bf),
            shape((model // 2, 2 * hidden), bf),
            shape((hidden // FB, 1, FB), f32),
        ),
        in_specs=[far] * 4 + [bias, up, up, down, down],
        out_specs=(far, VM, pair, pair, bias),
        scratch_shapes=[pltpu.VMEM((model, hidden), bf)] * 2
        + [pltpu.VMEM((slots, hidden), bf)] * 2
        + [pltpu.VMEM((slots, model), bf)] * 2
        + [pltpu.VMEM((model, slots), bf)] * 2
        + [pltpu.VMEM((slots, model), bf), pltpu.SemaphoreType.DMA((5,))],
        compiler_params=params(),
        cost_estimate=cost(10, 10),
        name="feed_forward",
    )(n2, n2t, og, ogt, hb, *w, *w)


def second_norm_backward(
    mine_ref, ma_ref, mb_ref, ga_ref, gb_ref, res_ref, og_ref, nv_ref, perm_ref, aan_ref, aaf_ref, abn_ref, abf_ref, oa_ref, ob_ref,
    whole_ref, out_ref, gres_ref, gt_ref, dota_ref, dotb_ref, dela_ref, delb_ref, vec_ref, wot_ref,
):
    res, og = res_ref[...].astype(f32), og_ref[...].astype(f32)
    out = (res + (ma_ref[...].astype(f32) + mb_ref[...].astype(f32)) + nv_ref[5:6]).astype(bf)
    out = dg(out, perm_ref[...], 1, 1).astype(bf)
    whole_ref[...], out_ref[...] = out, out
    xhat, scale = normalize(res)
    gn = ga_ref[...].astype(f32) + gb_ref[...].astype(f32)
    gres = og + norm_backward(gn, nv_ref[3:4], xhat, scale)
    gres_ref[...] = gres.astype(bf)
    width = oa_ref.shape[0]

    @pl.when(pl.program_id(0) == 0)
    def _():
        for at, near, far in ((0, aan_ref, aaf_ref), (1, abn_ref, abf_ref)):
            both = jnp.concatenate([near[:, width:], far[:, width:]], axis=0)
            wot_ref[at] = jnp.transpose(both)

    low = jnp.transpose(gres.astype(bf))
    gt_ref[...] = low
    for at, o_ref, dot_ref, del_ref in (
        (0, oa_ref, dota_ref, dela_ref),
        (1, ob_ref, dotb_ref, delb_ref),
    ):
        dot = jnp.dot(wot_ref[at], low, preferred_element_type=f32).astype(bf)
        dot_ref[...] = dot
        prod = dot.astype(f32) * o_ref[...].astype(f32)
        for h in range(prod.shape[0] // HD):
            del_ref[h : h + 1, :] = jnp.sum(prod[HD * h : HD * h + HD], axis=0, keepdims=True)
    column_sums(vec_ref, [gres, gn * xhat, gn, og], res.shape[1])


def middle_back(mine, ma, mb, ga, gb, res, og, nv, perm, aa, ab, oa, ob):
    slots, model = res.shape
    width = oa.shape[0]
    tok, lane = token_block(model), lane_block(width)
    return pl.pallas_call(
        second_norm_backward,
        out_shape=(
            shape((2 * slots, model), bf),
            shape((slots, model), bf),
            shape((slots, model), bf),
            shape((model, slots), bf),
            shape((width, slots), bf),
            shape((width, slots), bf),
            shape((16, slots), f32),
            shape((16, slots), f32),
            shape((8, model), f32),
        ),
        grid_spec=pltpu.PrefetchScalarGridSpec(
            num_scalar_prefetch=1,
            grid=(slots // TB,),
            in_specs=[tok] * 6 + [VM] * 2 + [late_columns(aa)] * 4 + [lane] * 2,
            out_specs=(own_rows(slots, model), tok, tok, lane_block(model), lane, lane)
            + (lane_block(16), lane_block(16), VM),
            scratch_shapes=[pltpu.VMEM((2, width, model), bf)],
        ),
        compiler_params=params(),
        cost_estimate=cost(2, 10),
        name="second_norm_backward",
    )(mine, ma, mb, ga, gb, res, og, nv, perm, *aa, *ab, oa, ob)


def first_norm_backward(mine_ref, aan_ref, aaf_ref, abn_ref, abf_ref, gres_ref, x_ref, nv_ref, perm_ref, *refs):
    *parts, whole_ref, out_ref, vec_ref = refs
    half = len(parts) // 2
    rows = [
        jnp.concatenate([part[c] for c in range(3) for part in mine], axis=0)
        for mine in (parts[:half], parts[half:])
    ]
    wide = rows[0].shape[0]
    planes = [
        jnp.dot(a_ref[:, :wide], rows[0], preferred_element_type=f32)
        + jnp.dot(b_ref[:, :wide], rows[1], preferred_element_type=f32)
        for a_ref, b_ref in ((aan_ref, abn_ref), (aaf_ref, abf_ref))
    ]
    gn = jnp.transpose(jnp.concatenate(planes, axis=0))
    xhat, scale = normalize(x_ref[...].astype(f32))
    gres = gres_ref[...].astype(f32)
    out = (gres + norm_backward(gn, nv_ref[0:1], xhat, scale)).astype(bf)
    out = dg(out, perm_ref[...], 1, 1).astype(bf)
    whole_ref[...], out_ref[...] = out, out
    column_sums(vec_ref, [gn * xhat, gn], gn.shape[1])


def tail(mine, aa, ab, gres, x, nv, perm, parts):
    slots, model = x.shape
    tok = token_block(model)
    blocks = [pl.BlockSpec((3, part.shape[1], TB), lambda j, *_: (0, 0, j)) for part in parts]
    return pl.pallas_call(
        first_norm_backward,
        out_shape=(
            shape((2 * slots, model), bf),
            shape((slots, model), bf),
            shape((8, model), f32),
        ),
        grid_spec=pltpu.PrefetchScalarGridSpec(
            num_scalar_prefetch=1,
            grid=(slots // TB,),
            in_specs=[VM] * 4 + [tok] * 2 + [VM] * 2 + blocks,
            out_specs=(own_rows(slots, model), tok, VM),
        ),
        compiler_params=params(),
        cost_estimate=cost(2, 10),
        name="first_norm_backward",
    )(mine, *aa, *ab, gres, x, nv, perm, *parts)


def tables(seg):
    slots = seg.shape[0]
    ids = jnp.arange(8, dtype=jnp.int32)
    starts = jnp.sum((seg[None, :] < ids[:, None]).astype(jnp.int32), axis=1)
    ends = jnp.sum((seg[None, :] <= ids[:, None]).astype(jnp.int32), axis=1)
    member = seg[None, :] == ids[:, None]
    before = jnp.sum(jnp.where(member, starts[:, None], 0), axis=0)
    after = jnp.sum(jnp.where(member, ends[:, None], 0), axis=0)
    position = (jnp.arange(slots, dtype=jnp.int32) - before).astype(f32)
    frequency = 10000.0 ** (-jnp.arange(0, HD, 2).astype(f32) / HD)
    angles = frequency[:, None] * position[None, :]
    fq = jnp.concatenate([jnp.where(member, 0.0, -BIG), jnp.zeros((56, slots))], axis=0).astype(bf)
    past = jnp.broadcast_to(ids[:, None] == 7, (8, SPARE))
    fk = jnp.concatenate([member, past], axis=1).astype(bf)
    fk = jnp.concatenate([fk, jnp.zeros((56, slots + SPARE), bf)], axis=0)
    lo = before[::QT] // STRIDE
    count = (after[QT - 1 :: QT] - lo * STRIDE + KC - 1) // KC
    return jnp.cos(angles), jnp.sin(angles), fq, fk, jnp.stack([lo, count])


def moments(weight, grad, first, second):
    first = BETA_ONE * first + (1.0 - BETA_ONE) * grad
    second = BETA_TWO * second + (1.0 - BETA_TWO) * grad * grad
    corrected = first / (1.0 - BETA_ONE**STEP)
    variance = second / (1.0 - BETA_TWO**STEP)
    return first, second, corrected / (jnp.sqrt(variance) + EPS_ADAM) + DECAY * weight


class Squares:
    def __init__(self):
        self.lane = lax.broadcasted_iota(jnp.int32, (8, 128), 1)
        self.row = lax.broadcasted_iota(jnp.int32, (8, 128), 0)
        self.total = jnp.zeros((8, 128), f32)

    def add(self, group, weight, update, share=1.0):
        for row, value in ((0, weight), (1, update)):
            square = jnp.sum(value * value, axis=(0, 1), keepdims=True) * share
            self.total = self.total + jnp.where(
                (self.lane == group) & (self.row == row), square, 0.0
            )


def all_parts(parts_ref, rows):
    total = parts_ref[0, :rows].astype(f32)
    for i in range(1, parts_ref.shape[0]):
        total = total + parts_ref[i, :rows].astype(f32)
    return total


def lamb_ffn(parts_ref, peer_ref, w_ref, m_ref, v_ref, m_out, v_out, u_out, sq_out):
    grad = all_parts(parts_ref, peer_ref.shape[0]) + peer_ref[...].astype(f32)
    blocks = w_ref.shape[2] // FB
    squares = Squares()
    for c in range(2):
        pieces = [grad[:, (2 * j + c) * FB : (2 * j + c + 1) * FB] for j in range(blocks)]
        first, second, update = moments(
            w_ref[c], jnp.concatenate(pieces, axis=1), m_ref[c], v_ref[c]
        )
        m_out[c], v_out[c], u_out[c] = first, second, update
        squares.add(4 + c, w_ref[c], update)
    sq_out[...] = squares.total


def step_ffn(parts, peer, w, m, v):
    return pl.pallas_call(
        lamb_ffn,
        out_shape=(shape(w.shape, f32),) * 3 + (shape((8, 128), f32),),
        in_specs=[VM] * 5,
        out_specs=(VM,) * 4,
        compiler_params=params(),
        cost_estimate=cost(1, 5),
        name="lamb_ffn",
    )(parts, peer, w, m, v)


def lamb_rest(
    shares, mine_ref, parts_ref, small_ref, sq_ref,
    w_ref, m_ref, v_ref, hw_ref, hm_ref, hv_ref, bw_ref, bm_ref, bv_ref, nw_ref, nm_ref, nv_ref,
    m_out, v_out, vo_out, u_out, hm_out, hv_out, hu_out, bm_out, bv_out, bu_out,
    nm_out, nv_out, nvo_out, nu_out, sq_out,
):
    grad = all_parts(parts_ref, parts_ref.shape[1])
    width = w_ref.shape[2]
    squares = Squares()
    for c in range(4):
        first, second, update = moments(
            w_ref[c], grad[:, c * width : c * width + width], m_ref[c], v_ref[c]
        )
        m_out[c], u_out[c] = first, update
        if c < 3:
            v_out[c] = second
        else:
            vo_out[...] = second
        squares.add(c, w_ref[c], update)
    lower = mine_ref[0] == 0
    small = small_ref[...]
    grad = jnp.where(lower, small[0:3, :width], small[0:3, width:])
    hm_out[...], hv_out[...], hu_out[...] = moments(hw_ref[...], grad, hm_ref[...], hv_ref[...])
    grad = jnp.where(lower, small[9:11], small[11:13])
    bm_out[...], bv_out[...], bu_out[...] = moments(bw_ref[...], grad, bm_ref[...], bv_ref[...])
    first, second, update = moments(nw_ref[...], small[3:9], nm_ref[...], nv_ref[...])
    nm_out[...], nu_out[...] = first, update
    nvo_out[...], nv_out[...] = second[:2], second[2:]
    for c in range(3):
        squares.add(6 + c, hw_ref[c : c + 1], hu_out[c : c + 1], shares[0])
    squares.add(9, bw_ref[...], bu_out[...], shares[0])
    for c in range(6):
        squares.add(10 + c, nw_ref[c : c + 1], update[c : c + 1], shares[1])
    sq_out[...] = squares.total + sq_ref[...]


def step_rest(shares, mine, parts, small, sq, attn, head, hidden, vector):
    w, h, b, n = attn[0], head[0], hidden[0], vector[0]
    return pl.pallas_call(
        partial(lamb_rest, shares),
        out_shape=tuple(
            shape(dims, f32)
            for dims in (
                w.shape, (3,) + w.shape[1:], w.shape[1:], w.shape,
                h.shape, h.shape, h.shape, b.shape, b.shape, b.shape,
                n.shape, (4, n.shape[1]), (2, n.shape[1]), n.shape, (8, 128),
            )
        ),
        in_specs=[SM] + [VM] * 15,
        out_specs=(VM,) * 15,
        compiler_params=params(),
        cost_estimate=cost(1, 5),
        name="lamb_rest",
    )(mine, parts, small, sq, *attn, *head, *hidden, *vector)


def apply_updates(sums_ref, *refs):
    weights, updates, outs, norms_out = refs[:5], refs[5:10], refs[10:15], refs[15]
    total = sums_ref[0]
    for i in range(1, sums_ref.shape[0]):
        total = total + sums_ref[i]
    norms = jnp.sqrt(total)
    norms_out[...] = norms[:2, :16]
    ratio = norms[0:1] / norms[1:2]
    lane = lax.broadcasted_iota(jnp.int32, (1, 128), 1)

    def rate(group):
        picked = jnp.where(lane == group, ratio, 0.0)
        return RATE * jnp.sum(picked, axis=1, keepdims=True)

    at = 0
    for count, w, u, out in zip((4, 2, 3, 1, 6), weights, updates, outs):
        for c in range(count):
            where = c if len(w.shape) == 3 else slice(None) if count == 1 else slice(c, c + 1)
            out[where] = w[where] - rate(at + c) * u[where]
        at += count


def new_weights(sums, weights, updates):
    return pl.pallas_call(
        apply_updates,
        out_shape=tuple(shape(w.shape, f32) for w in weights) + (shape((2, 16), f32),),
        in_specs=[VM] * 11,
        out_specs=(VM,) * 6,
        compiler_params=params(),
        cost_estimate=cost(1, 5),
        name="new_weights",
    )(sums, *weights, *updates)


def swap(value, axis_name, offset):
    count = lax.axis_size(axis_name)
    return lax.ppermute(value, axis_name, [(i, i ^ offset) for i in range(count)])


def planes():
    count = lax.axis_size("dp")
    return [[2 * u + core for u in range(count // 2)] for core in range(2)]


def exchange(blocks):
    return lax.all_to_all(blocks, "dp", 0, 0, axis_index_groups=planes())


def row_order(model, count):
    block = model // count
    place = np.arange(model) // block
    other = jnp.asarray(place // (count // 2), jnp.int32)
    owner = jnp.asarray(2 * (place % (count // 2)), jnp.int32) + (lax.axis_index("dp") % 2 ^ other)
    feature = owner * block + jnp.asarray(np.arange(model) % block, jnp.int32)
    return jnp.arange(model, dtype=jnp.int32)[:, None] == feature[None, :]


class Gather:
    def __init__(self, value, steps=("plane", "core")):
        self.value, self.steps, self.flying = value, list(steps), []

    def peer(self):
        return Gather(self.value, ("tp", "core"))

    def launch(self):
        step = self.steps[0]
        if step == "plane":
            count = lax.axis_size("dp") // 2
            spread = jnp.broadcast_to(self.value[None], (count,) + self.value.shape)
            self.flying = [exchange(spread)]
        else:
            self.flying = [swap(self.value, "dp" if step == "core" else "tp", 1)]

    def finish(self):
        step = self.steps.pop(0)
        if step == "core":
            self.value = (self.value, self.flying[0])
        else:
            self.value = self.flying[0].reshape(-1, self.flying[0].shape[-1])
        self.flying = []


def far_exchange(blocks):
    count = lax.axis_size("dp") // 4
    groups = [[4 * z + low for z in range(count)] for low in range(4)]
    return lax.all_to_all(blocks, "dp", 0, 0, axis_index_groups=groups)


class Scatter:
    def __init__(self, keep, send):
        self.parts, self.send = [keep], send
        self.steps, self.flying = ["core", "pair", "tp", "far"], []

    def side(self, other):
        at = (lax.axis_index("dp") >> 1) % 2 ^ other
        count = lax.axis_size("dp") // 4
        total = 0.0
        for part in self.parts:
            blocks = part.reshape(count, 2, -1, part.shape[-1])
            total = total + lax.dynamic_index_in_dim(blocks, at, 1, False).astype(f32)
        return total

    def launch(self):
        step = self.steps[0]
        if step == "pair":
            self.send = self.side(1).astype(bf)
        if step == "far":
            self.flying = [far_exchange(self.value)]
        elif step == "tp":
            self.flying = [swap(self.value, "tp", 1)]
        else:
            self.flying = [swap(self.send, "dp", 1 if step == "core" else 2)]

    def finish(self):
        step = self.steps.pop(0)
        if step == "core":
            self.parts = self.parts + self.flying
        elif step == "pair":
            self.value = (self.side(0) + self.flying[0].astype(f32)).astype(bf)
        else:
            self.value = self.flying[0]
        self.flying = []

    def merge(self, peer):
        self.value = (self.value.astype(f32) + peer.value.astype(f32)).astype(bf)
        self.steps = ["far"]


class Pool:
    def __init__(self, own, peer):
        self.rows = own.value.shape[1]
        self.value = jnp.concatenate([own.value, peer.value], axis=1)
        self.steps, self.flying = ["far", "tp"], []

    def launch(self):
        if self.steps[0] == "far":
            self.flying = [far_exchange(self.value)]
        else:
            peer = self.value[:, self.rows :].astype(f32)
            self.flying = [swap(jnp.sum(peer, axis=0).astype(bf), "tp", 1)]

    def finish(self):
        if self.steps.pop(0) == "far":
            self.value = self.flying[0]
        else:
            self.peer = self.flying[0]
        self.flying = []


def tie(value, *others):
    return lax.optimization_barrier((value, *others))[0]


def meet(value, *movers):
    out = lax.optimization_barrier((value, *[a for mover in movers for a in mover.flying]))
    at = 1
    for mover in movers:
        count = len(mover.flying)
        mover.flying = list(out[at : at + count])
        at += count
        mover.finish()
    return out[0]


def sum_over_dp(value):
    step = 2
    while step < lax.axis_size("dp"):
        value = value + swap(value, "dp", step)
        step *= 2
    return value


def by_peer(own, peer, axis):
    first = lax.axis_index("tp") == 0
    return jnp.where(
        first, jnp.concatenate([own, peer], axis), jnp.concatenate([peer, own], axis)
    )


def on_device(
    inputs, out_grad, segment_ids, attn_weights, ffn_weights, head_bias, hidden_bias, norm_vectors,
    attn_first, ffn_first, head_first, hidden_first, vector_first,
    attn_second, ffn_second, head_second, hidden_second, vector_second,
):
    dp_count, tp_count = lax.axis_size("dp"), lax.axis_size("tp")
    mine = lax.axis_index("tp")
    rows, slots = segment_ids.shape
    assert rows == tp_count == 2
    shard, head_width = attn_weights.shape[1:]
    hidden = ffn_weights.shape[2]
    model = inputs.shape[1]

    a_own = Gather(jnp.concatenate(list(attn_weights.astype(bf)), axis=1))
    a_own.launch()
    x = lax.dynamic_slice_in_dim(inputs, mine * slots, slots, 0)
    order = row_order(model, dp_count)
    perm = order.astype(bf)
    exact = partial(jnp.dot, precision=lax.Precision.HIGHEST, preferred_element_type=f32)
    nv = exact(jnp.concatenate([norm_vectors, jnp.zeros((2, model), f32)], 0), order.astype(f32))
    xt = dg(perm, x, 0, 1)
    centered = xt - jnp.mean(xt, axis=0, keepdims=True)
    scale = lax.rsqrt(jnp.mean(centered * centered, axis=0, keepdims=True) + EPS_NORM)
    n1t = (centered * scale * nv[0][:, None] + nv[1][:, None]).astype(bf)
    bias_own = jnp.concatenate([head_bias.reshape(-1), hidden_bias])
    def hidden_blocks(bias):
        return bias[3 * head_width :].reshape(-1, 1, FB)

    both = jnp.concatenate(list(ffn_weights.astype(bf)), axis=1)
    og = lax.dynamic_slice_in_dim(out_grad, mine * slots, slots, 0)
    seg = lax.dynamic_index_in_dim(segment_ids, mine, 0, keepdims=False)
    cos, sin, fq, fk, rng = tables(seg)
    x = dg(x, perm, 1, 0).astype(bf)
    ogt = dg(perm, og, 0, 1).astype(bf)
    og = dg(og, perm, 1, 0).astype(bf)
    n1t, cos, sin, fq, fk, rng, x, ogt, og, both = lax.optimization_barrier(
        (n1t, cos, sin, fq, fk, rng, x, ogt, og, both)
    )
    n1t = meet(n1t, a_own)
    a_peer = a_own.peer()
    w_own = Gather(tie(both, a_own.value))
    a_own.launch()
    a_peer.launch()
    w_own.launch()
    bias_own, _ = lax.optimization_barrier((bias_own, a_own.value))
    bias_peer = swap(bias_own.reshape(-1, head_width), "tp", 1).reshape(-1)

    head_columns = jnp.concatenate(
        [bias[: 3 * head_width].reshape(3, head_width) for bias in (bias_own, bias_peer)]
        + [jnp.zeros((2, head_width), f32)],
        0,
    ).T


    n1t = meet(n1t, a_own)
    a_one = a_own.value
    saved_own, o_own, lse_own = attn_fwd(0, rng, n1t, a_one, head_columns, cos, sin, fq, fk)
    o_own = meet(o_own, a_peer)
    a_peer.launch()
    again = meet(tie(n1t, o_own), a_peer)
    a_two = a_peer.value
    saved_peer, o_peer, lse_peer = attn_fwd(
        3, rng, again, a_two, head_columns, cos, sin, fq, fk
    )
    o_peer = meet(o_peer, w_own)
    w_peer = w_own.peer()
    w_own.launch()
    w_peer.launch()
    res, n2, n2t = middle(o_own, o_peer, a_one, a_two, x, nv)

    n2 = meet(n2, w_own)
    mix_own, gn_own, keep, send, dhb_own = ffn(n2, n2t, og, ogt, hidden_blocks(bias_own), w_own.value)
    f_own = Scatter(keep, send)
    f_own.launch()
    again = meet(tie(n2, mix_own), w_peer)
    w_peer.launch()
    again = meet(again, w_peer)
    mix_peer, gn_peer, keep, send, dhb_peer = ffn(
        again, n2t, og, ogt, hidden_blocks(bias_peer), w_peer.value
    )
    f_peer = Scatter(keep, send)
    mix_peer = meet(mix_peer, f_own)
    f_own.launch()
    f_peer.launch()
    layer_output, out_low, gres, gt, dot_own, dot_peer, delta_own, delta_peer, sums_two = middle_back(
        mine.reshape(1), mix_own, mix_peer, gn_own, gn_peer, res, og, nv, perm, a_one, a_two, o_own, o_peer
    )

    out_far = swap(out_low, "tp", 1)

    def back(dot, saved, lse, delta, heads):
        return attn_bwd(rng, dot, saved[0], lse, delta, cos, sin, fq, n1t, gt, heads)

    dot_peer = meet(dot_peer, f_peer)
    f_peer.launch()
    keep, send, dbias_peer, dt_peer = back(dot_peer, saved_peer, lse_peer, delta_peer, o_peer)
    g_peer = Scatter(keep, send)
    g_peer.launch()
    dot_own, out_far, dt_peer = lax.optimization_barrier((dot_own, out_far, dt_peer))
    dot_own = meet(dot_own, f_own, f_peer)
    f_pool = Pool(f_own, f_peer)
    f_pool.launch()
    dot_own = meet(dot_own, g_peer)
    g_peer.launch()
    keep, send, dbias_own, dt_own = back(dot_own, saved_own, lse_own, delta_own, o_own)
    g_own = Scatter(keep, send)
    g_own.launch()
    dt_own, gres = lax.optimization_barrier((dt_own, gres))
    gres = meet(gres, g_peer)
    g_peer.launch()
    gres = meet(gres, g_own)
    g_own.launch()
    input_grad, in_low, sums_one = tail(mine.reshape(1), a_one, a_two, gres, x, nv, perm, [dt_own, dt_peer])
    in_low = meet(in_low, g_own, g_peer)
    g_own.merge(g_peer)
    g_own.value, f_pool.flying[0] = lax.optimization_barrier((g_own.value, f_pool.flying[0]))
    g_own.launch()
    f_pool.finish()
    f_pool.launch()
    sums = exact(jnp.concatenate([sums_one[:2], sums_two[:4]], 0), order.astype(f32).T)
    small = jnp.concatenate(
        [
            by_peer(dbias_own[:, :3].T, dbias_peer[:, :3].T, 1),
            sums,
            by_peer(dhb_own.reshape(-1), dhb_peer.reshape(-1), 0).reshape(-1, model),
        ],
        0,
    )
    small_far = swap(small, "tp", 1)
    in_low, small_far = lax.optimization_barrier((in_low, small_far))
    in_low = meet(in_low, f_pool)
    small = small + small_far
    in_far = swap(in_low, "tp", 1)
    g_own.finish()

    ffn_first_new, ffn_second_new, ffn_update, squares = step_ffn(
        f_pool.value, f_pool.peer, ffn_weights, ffn_first, ffn_second
    )
    near = swap(small, "dp", 1)
    near, squares = lax.optimization_barrier((near, squares))
    small = sum_over_dp(small + near)
    wide = lambda v: v.reshape(2, -1)
    shares = (1.0 / dp_count, 1.0 / (dp_count * tp_count))
    (
        attn_first_new, attn_second_new, out_second_new, attn_update,
        head_first_new, head_second_new, head_update,
        hidden_first_new, hidden_second_new, hidden_update,
        vector_first_new, vector_second_new, norm_second_new, vector_update, squares,
    ) = step_rest(
        shares, mine.reshape(1), g_own.value, small, squares,
        (attn_weights, attn_first, attn_second),
        (head_bias, head_first, head_second),
        (wide(hidden_bias), wide(hidden_first), wide(hidden_second)),
        (norm_vectors, vector_first, vector_second),
    )
    copies = dp_count * tp_count
    squares, out_far = lax.optimization_barrier((squares, out_far))
    other = (1 - mine) * slots
    layer_output = lax.dynamic_update_slice_in_dim(layer_output, out_far, other, 0)
    input_grad = lax.dynamic_update_slice_in_dim(input_grad, in_far, other, 0)
    sums = lax.all_to_all(
        jnp.broadcast_to(squares[None], (copies, 8, 128)), ("dp", "tp"), 0, 0
    )
    sums, input_grad, layer_output = lax.optimization_barrier((sums, input_grad, layer_output))
    new_attn, new_ffn, new_head, new_hidden, new_vectors, norms = new_weights(
        sums,
        (attn_weights, ffn_weights, head_bias, wide(hidden_bias), norm_vectors),
        (attn_update, ffn_update, head_update, hidden_update, vector_update),
    )
    return (
        layer_output,
        input_grad,
        new_attn,
        new_ffn,
        new_head,
        new_hidden.reshape(-1),
        new_vectors,
        attn_first_new,
        ffn_first_new,
        head_first_new,
        hidden_first_new.reshape(-1),
        vector_first_new,
        attn_second_new,
        out_second_new,
        ffn_second_new,
        head_second_new,
        hidden_second_new.reshape(-1),
        vector_second_new,
        norm_second_new,
        norms,
    )


def solution(mesh):
    in_specs = (
        P("dp", None),
        P("dp", None),
        P("dp", None),
        P(None, "dp", "tp"),
        P(None, "dp", "tp"),
        P(None, "tp"),
        P("tp"),
        P(),
        P(None, "dp", "tp"),
        P(None, "dp", "tp"),
        P(None, "tp"),
        P("tp"),
        P(),
        P(None, "dp", "tp"),
        P(None, "dp", "tp"),
        P(None, "tp"),
        P("tp"),
        P(),
    )
    out_specs = (
        P("dp", None),
        P("dp", None),
        P(None, "dp", "tp"),
        P(None, "dp", "tp"),
        P(None, "tp"),
        P("tp"),
        P(),
        P(None, "dp", "tp"),
        P(None, "dp", "tp"),
        P(None, "tp"),
        P("tp"),
        P(),
        P(None, "dp", "tp"),
        P("dp", "tp"),
        P(None, "dp", "tp"),
        P(None, "tp"),
        P("tp"),
        P(),
        P(),
        P(),
    )
    return jax.shard_map(
        on_device, mesh=mesh, in_specs=in_specs, out_specs=out_specs, check_vma=False
    )
```
